128 devices in a mesh: heads: 2 (over y_lo), seq: 64 (over y_hi, z, x, core).
Axes of the slice: x: 4, y: 4 (y_hi: 2, y_lo: 2; y = y_hi * 2 + y_lo), z: 4, core: 2. Of those that a mesh axis runs over, the one named last changes fastest.
Arguments:
- queries: bfloat16 [2, 24576, 4096], P(None, 'seq', 'heads'), may hold values from -72 to 72, as said below
- key_rows: bfloat16 [2, 24576, 4096], P(None, 'seq', 'heads'), may hold values from -6.06 to 6.06, as said below
- value_rows: bfloat16 [2, 24576, 4096], P(None, 'seq', 'heads'), may hold values from -6 to 6
- step_rates: float32 [8, 2, 24576], P('heads', None, 'seq'), may hold values from 0.0001 to 0.001
- w_gate: float32 [8, 512, 512], P('heads', 'seq'), may hold values from -0.25 to 0.25
- w_up: float32 [8, 512, 512], P('heads', 'seq'), may hold values from -0.25 to 0.25
- w_down: float32 [8, 512, 512], P('heads', 'seq'), may hold values from -0.25 to 0.25
- out_gain: float32 [4096], P('heads'), may hold values from 0.5 to 1.5
Outputs:
- layer_out: bfloat16 [2, 24576, 4096], P(None, 'seq', 'heads')
- new_gate: float32 [8, 512, 512], P('heads', 'seq')
- new_up: float32 [8, 512, 512], P('heads', 'seq')
- new_down: float32 [8, 512, 512], P('heads', 'seq')
The draws below stay inside these ranges and needn't reach their ends.
Inputs may be any that keep to these rules, and one draw needn't show every extreme that they name: `queries`: entries of order one with a few larger ones. `key_rows`: entries of order one.
All inputs are finite; a program needn't handle non-finite values.
Results may differ from the reference program's by a relative error of at most 0.0069.
The reference program's roundings to bfloat16 on the way count: a program that leaves them out, or rounds other values in their place, can miss the bound.
Values may be sent and summed in bfloat16 or wider, within the bound.
No kernel may reach another device: no remote copies, remote signals or barrier semaphores. Data moves between devices by JAX's collectives and lax.ppermute only.
A program may use at most 192 MiB of HBM per device.

```python
import math
import jax
import jax.numpy as jnp
from jax import lax

HEADS = 8
DH = 512
HID = 512
WINDOW = 768
STRETCHES = 2
TOK_DEV = 384
CTOK = 24576


def paired_draw(key):
    query_key = jax.random.fold_in(key, 11)
    keys_key = jax.random.fold_in(key, 23)
    full_shape = (STRETCHES, CTOK, HEADS * DH)
    keys_base = jnp.clip(jax.random.normal(keys_key, full_shape, jnp.float32), -6.0, 6.0)
    queries_base = jnp.clip(jax.random.normal(query_key, full_shape, jnp.float32), -6.0, 6.0)
    return (queries_base, keys_base)


def draw_queries(key, part):
    return paired_draw(key)[0].astype(jnp.bfloat16)


def draw_key_rows(key, part):
    return paired_draw(key)[1].astype(jnp.bfloat16)


def block_levels(own_key, dims, cuts, least, largest):
    loudness = 1.0
    for dim, shards_of in cuts:
        steps = jax.random.uniform(jax.random.fold_in(jax.random.fold_in(own_key, 6), dim), (shards_of,), jnp.float32, least / len(cuts), largest / len(cuts))
        loudness = loudness * jnp.repeat(jnp.exp(steps), dims[dim] // shards_of).reshape((-1,) + (1,) * (len(dims) - 1 - dim))
    return loudness


def gaussian(own_key, dims, spread, reach, cuts=(), held_as=jnp.bfloat16):
    drawn = jax.random.normal(own_key, dims, jnp.float32) * spread
    if len(cuts) > 0:
        drawn = block_levels(own_key, dims, cuts, -0.22, 0.18) * drawn
    return jnp.clip(drawn, min=-reach, max=reach).astype(held_as)


def setup_inputs(seed: int = 0) -> dict:
    streams_of = jax.random.split(jax.random.key(seed), 9)
    return {
        "queries": draw_queries(jax.random.fold_in(streams_of[8], 71), 0),
        "key_rows": draw_key_rows(jax.random.fold_in(streams_of[8], 71), 0),
        "value_rows": gaussian(streams_of[2], (STRETCHES, CTOK, HEADS * DH), 1.0, 6.0, ((1, 64), (2, 2))),
        "step_rates": jnp.clip(jnp.exp(math.log(0.001) - 2.3025852 * jax.random.uniform(streams_of[3], (HEADS, STRETCHES, CTOK), jnp.float32) ** block_levels(streams_of[3], (HEADS, STRETCHES, CTOK), ((0, 2), (2, 64)), -0.2, 0.2)), 0.0001, 0.001),
        "w_gate": gaussian(streams_of[4], (HEADS, DH, HID), DH ** -0.5, 0.25, ((0, 2), (1, 64)), jnp.float32),
        "w_up": gaussian(streams_of[5], (HEADS, DH, HID), DH ** -0.5, 0.25, ((0, 2), (1, 64)), jnp.float32),
        "w_down": gaussian(streams_of[6], (HEADS, HID, DH), HID ** -0.5, 0.25, ((0, 2), (1, 64)), jnp.float32),
        "out_gain": jnp.clip(1.0 + 0.1 * jax.random.normal(streams_of[7], (HEADS * DH,), jnp.float32), 0.5, 1.5),
    }


NORM_EPS = 1e-05
MASKED = -1e+30

def apply_head(inputs, copies):
    gate_copy, up_copy, down_copy = copies
    gate_pre = jnp.dot(inputs, gate_copy, preferred_element_type=jnp.float32)
    up_pre = jnp.dot(inputs, up_copy, preferred_element_type=jnp.float32)
    active = (jax.nn.silu(gate_pre) * up_pre).astype(jnp.bfloat16)
    return jnp.dot(active, down_copy, preferred_element_type=jnp.float32)

def grads_head(key_in, value_in, rate_in, copies):
    gate_copy, up_copy, down_copy = copies
    gate_pre = jnp.dot(key_in, gate_copy, preferred_element_type=jnp.float32)
    up_pre = jnp.dot(key_in, up_copy, preferred_element_type=jnp.float32)
    sigmoid_g = jax.nn.sigmoid(gate_pre)
    silu_g = gate_pre * sigmoid_g
    active = (silu_g * up_pre).astype(jnp.bfloat16)
    target = (-(rate_in[:, None] * value_in.astype(jnp.float32))).astype(jnp.bfloat16)
    grad_down = jnp.dot(active.T, target, preferred_element_type=jnp.float32)
    back = jnp.dot(target, down_copy.T, preferred_element_type=jnp.float32)
    d_gate = (back * up_pre * sigmoid_g * (1.0 + gate_pre * (1.0 - sigmoid_g))).astype(jnp.bfloat16)
    d_up = (back * silu_g).astype(jnp.bfloat16)
    grad_gate = jnp.dot(key_in.T, d_gate, preferred_element_type=jnp.float32)
    grad_up = jnp.dot(key_in.T, d_up, preferred_element_type=jnp.float32)
    return (grad_gate, grad_up, grad_down)

def head_pass(packed):
    query_head, key_head, value_head, rate_head, gate_master, up_master, down_master = packed
    masters = (gate_master, up_master, down_master)
    copies = tuple((member.astype(jnp.bfloat16) for member in masters))
    first_out = apply_head(query_head[0], copies)
    gradients = grads_head(key_head[0], value_head[0], rate_head[0], copies)
    updated = tuple((master - gradient for master, gradient in zip(masters, gradients)))
    second_out = apply_head(query_head[1], tuple((member.astype(jnp.bfloat16) for member in updated)))
    return (jnp.stack([first_out, second_out]), updated[0], updated[1], updated[2])

def window_reference(queries, key_rows, value_rows):
    total_rows = STRETCHES * CTOK
    query_flat = queries.reshape(total_rows, HEADS, DH)
    zero_rows = jnp.zeros((WINDOW, HEADS, DH), jnp.bfloat16)
    key_padded = jnp.concatenate([zero_rows, key_rows.reshape(total_rows, HEADS, DH)], axis=0)
    value_padded = jnp.concatenate([zero_rows, value_rows.reshape(total_rows, HEADS, DH)], axis=0)

    def query_block(block_index):
        row_start = (block_index * TOK_DEV).astype(jnp.int32)
        query_part = lax.dynamic_slice_in_dim(query_flat, row_start, TOK_DEV, 0)
        key_part = lax.dynamic_slice_in_dim(key_padded, row_start, TOK_DEV + WINDOW, 0)
        value_part = lax.dynamic_slice_in_dim(value_padded, row_start, TOK_DEV + WINDOW, 0)
        scores = jnp.einsum('qhd,khd->hqk', query_part.astype(jnp.float32), key_part.astype(jnp.float32)) * DH ** (-0.5)
        query_pos = jnp.arange(TOK_DEV, dtype=jnp.int32)[:, None]
        key_pos = jnp.arange(TOK_DEV + WINDOW, dtype=jnp.int32)[None, :]
        allowed = (key_pos > query_pos) & (key_pos <= query_pos + WINDOW) & (row_start + key_pos - WINDOW >= 0)
        scores = jnp.where(allowed[None], scores, MASKED)
        row_peak = lax.optimization_barrier(jnp.max(scores, axis=-1, keepdims=True))
        weights = jnp.exp(scores - row_peak)
        soft_weights = (weights / lax.optimization_barrier(jnp.sum(weights, axis=-1, keepdims=True))).astype(jnp.bfloat16)
        return jnp.einsum('hqk,khd->qhd', soft_weights.astype(jnp.float32), value_part.astype(jnp.float32))
    blocks_out = lax.map(query_block, jnp.arange(total_rows // TOK_DEV, dtype=jnp.int32))
    return blocks_out.reshape(STRETCHES, CTOK, HEADS * DH)

def reference(queries, key_rows, value_rows, step_rates, w_gate, w_up, w_down, out_gain):

    def by_head(array):
        return array.reshape(STRETCHES, CTOK, HEADS, DH).transpose(2, 0, 1, 3)
    fast_out, new_gate, new_up, new_down = lax.map(head_pass, (by_head(queries), by_head(key_rows), by_head(value_rows), step_rates, w_gate, w_up, w_down))
    fast_out = fast_out.transpose(1, 2, 0, 3).reshape(STRETCHES, CTOK, HEADS * DH)
    row_power = lax.optimization_barrier(jnp.sum(fast_out * fast_out, axis=-1, keepdims=True))
    normed = fast_out * out_gain * lax.rsqrt(row_power / (HEADS * DH) + NORM_EPS)
    attended = window_reference(queries, key_rows, value_rows)
    layer_out = (normed + attended).astype(jnp.bfloat16)
    return (layer_out, new_gate, new_up, new_down)
```

```python
import functools

import jax
import jax.numpy as jnp
from jax import lax
from jax.experimental import pallas as pl
from jax.experimental.pallas import tpu as pltpu
from jax.sharding import Mesh, PartitionSpec as P

NORM_EPS = 1e-05
MASKED = -1e30
SIZES = {"heads": 2, "yh": 2, "z": 4, "x": 4, "core": 2}
SEQ = ("yh", "z", "x", "core")
TOK = 384
DH = 512
SCALE = DH ** -0.5

f32 = jnp.float32
bf16 = jnp.bfloat16


def shift(value, axis, steps):
    count = SIZES[axis]
    return lax.ppermute(value, axis, [(i, (i + steps) % count) for i in range(count)])


def dot(a, b, dims):
    return lax.dot_general(a, b, (dims, ((), ())), preferred_element_type=f32)


NN = ((1,), (0,))
NT = ((1,), (1,))
TN = ((0,), (0,))


def cparams(**kw):
    return pltpu.CompilerParams(vmem_limit_bytes=56 * 1024 * 1024, **kw)


def piece_rows(kind, part, idx, item):
    yh, z, x = idx
    a, k = item % 2, item // 2
    y = lax.rem(yh + a, 2)
    if kind == 0:
        zz, xx = lax.rem(z + 4 - k, 4), lax.rem(x + 4 - part, 4)
    else:
        zz, xx = lax.rem(z + 4 - part, 4), lax.rem(x + 4 - k, 4)
    return pl.multiple_of(y * 256 + zz * 64 + xx * 16, 16)


def weight_copies(head, pieces, w_vmem, sem, idx):
    for part in range(4):
        for item in range(8):
            row = piece_rows(head, part, idx, item)
            yield pltpu.make_async_copy(
                pieces[head * 4 + part].at[item],
                w_vmem.at[head, :, pl.ds(row, 16), :],
                sem.at[head],
            )


def load_weights(pieces, w_vmem, sem, idx, head_now):
    @pl.when(head_now == 0)
    def _():
        for head in range(2):
            for copy in weight_copies(head, pieces, w_vmem, sem, idx):
                copy.start()

    for head in range(2):

        @pl.when(head_now == head)
        def _(head=head):
            pltpu.make_async_copy(w_vmem.at[head], w_vmem.at[head], sem.at[head]).wait()


def grads_kernel(s_ref, *refs):
    pieces = refs[:8]
    k_own, v_own, k_rec, v_rec, r_ref = refs[8:13]
    outs = refs[13:21]
    w_vmem, sums, sem = refs[21:]
    head = pl.program_id(0)
    idx = (s_ref[1], s_ref[2], s_ref[3])
    load_weights(pieces, w_vmem, sem, idx, head)
    gate, up, down = w_vmem[head, 0], w_vmem[head, 1], w_vmem[head, 2]
    for j, (k_ref, v_ref) in enumerate(((k_own, v_own), (k_rec, v_rec))):
        k = k_ref[0]
        rate = r_ref[0, j]
        target = (-(rate * v_ref[0].astype(f32))).astype(bf16)
        g = dot(k, gate, NN)
        u = dot(k, up, NN)
        back = dot(target, down, NT)
        s = jax.nn.sigmoid(g)
        silu = g * s
        active = (silu * u).astype(bf16)
        d_gate = (back * u * s * (1.0 + g * (1.0 - s))).astype(bf16)
        d_up = (back * silu).astype(bf16)
        parts = (dot(k, d_gate, TN), dot(k, d_up, TN), dot(active, target, TN))
        for m in range(3):
            if j == 0:
                sums[m] = parts[m]
            else:
                sums[m] += parts[m]
    yh, z, x = idx
    for kind in range(2):

        @pl.when(head == kind)
        def _(kind=kind):
            for part in range(4):
                for item in range(8):
                    a, k = item % 2, item // 2
                    y = lax.rem(yh + a, 2)
                    zz = lax.rem(z + (k if kind == 0 else part), 4)
                    xx = lax.rem(x + (part if kind == 0 else k), 4)
                    row = pl.multiple_of(y * 256 + zz * 64 + xx * 16, 16)
                    for m in range(3):
                        outs[kind * 4 + part][item, m] = sums[m, pl.ds(row, 16), :].astype(bf16)


def own_spec(c):
    return pl.BlockSpec((1, TOK, DH), lambda h, s: (c, 0, s[0] * 2 + h))


def rec_spec(c):
    return pl.BlockSpec((1, TOK, DH), lambda h, s: (c, 0, h))


ANY = pl.BlockSpec(memory_space=pl.ANY)


def compute_grads(scal, pieces, k, v, k_rec, v_rec, rates):
    whole = pl.BlockSpec((8, 3, 16, DH), lambda h, s: (0, 0, 0, 0))
    return pl.pallas_call(
        grads_kernel,
        name="fast_grads",
        out_shape=[jax.ShapeDtypeStruct((8, 3, 16, DH), bf16)] * 8,
        grid_spec=pltpu.PrefetchScalarGridSpec(
            num_scalar_prefetch=1,
            grid=(2,),
            in_specs=[ANY] * 8
            + [own_spec(0), own_spec(0), rec_spec(0), rec_spec(0)]
            + [pl.BlockSpec((1, 2, TOK, 1), lambda h, s: (h, 0, 0, 0))],
            out_specs=[whole] * 8,
            scratch_shapes=[
                pltpu.VMEM((2, 3, DH, DH), bf16),
                pltpu.VMEM((3, DH, DH), f32),
                pltpu.SemaphoreType.DMA((2,)),
            ],
        ),
        compiler_params=cparams(),
    )(scal, *pieces, k, v, k_rec, v_rec, rates)


def apply_kernel(s_ref, *refs):
    pieces = refs[:8]
    q_own, q_rec = refs[8:10]
    out_ref, pow_ref = refs[10:12]
    w_vmem, sem = refs[12:]
    head = pl.program_id(0)
    idx = (s_ref[1], s_ref[2], s_ref[3])
    load_weights(pieces, w_vmem, sem, idx, head)
    gate, up, down = w_vmem[head, 0], w_vmem[head, 1], w_vmem[head, 2]
    ones = jnp.ones((8, DH), f32)
    for j, q_ref in enumerate((q_own, q_rec)):
        q = q_ref[0]
        g = dot(q, gate, NN)
        u = dot(q, up, NN)
        active = (g * jax.nn.sigmoid(g) * u).astype(bf16)
        out = dot(active, down, NN)
        out_ref[j] = out
        power = lax.dot_general(
            ones, out * out, (NT, ((), ())),
            precision=lax.Precision.HIGHEST, preferred_element_type=f32,
        )

        @pl.when(head == 0)
        def _(j=j, power=power):
            pow_ref[j] = power

        @pl.when(head == 1)
        def _(j=j, power=power):
            pow_ref[j] += power


def fast_apply(c, scal, pieces, q, q_rec):
    return pl.pallas_call(
        apply_kernel,
        name="fast_apply",
        out_shape=[
            jax.ShapeDtypeStruct((2, TOK, 2 * DH), f32),
            jax.ShapeDtypeStruct((2, 8, TOK), f32),
        ],
        grid_spec=pltpu.PrefetchScalarGridSpec(
            num_scalar_prefetch=1,
            grid=(2,),
            in_specs=[ANY] * 8 + [own_spec(c), rec_spec(c)],
            out_specs=[
                pl.BlockSpec((2, TOK, DH), lambda h, s: (0, 0, h)),
                pl.BlockSpec((2, 8, TOK), lambda h, s: (0, 0, 0)),
            ],
            scratch_shapes=[
                pltpu.VMEM((2, 3, DH, DH), bf16),
                pltpu.SemaphoreType.DMA((2,)),
            ],
        ),
        compiler_params=cparams(),
    )(scal, *pieces, q, q_rec)


def attend_block(q, keys, values, masks):
    scores = []
    for k_ref, mask in zip(keys, masks):
        s = dot(q, k_ref[0], NT) * SCALE
        if mask is not None:
            s = jnp.where(mask, s, MASKED)
        scores.append(s)
    peak = functools.reduce(jnp.maximum, [jnp.max(s, axis=-1, keepdims=True) for s in scores])
    weights = [jnp.exp(s - peak) for s in scores]
    total = sum(jnp.sum(w, axis=-1, keepdims=True) for w in weights)
    inv = 1.0 / total
    return sum(
        dot((w * inv).astype(bf16), v_ref[0], NN) for w, v_ref in zip(weights, values)
    )


def attention_kernel(c, s_ref, qo, qr, ko, kr, vo, vr, pko, pkr, pvo, pvr, out_ref):
    row = lax.broadcasted_iota(jnp.int32, (TOK, TOK), 0)
    col = lax.broadcasted_iota(jnp.int32, (TOK, TOK), 1)
    causal = col <= row
    after = col > row
    if c == 0:
        started = jnp.broadcast_to(s_ref[4], (TOK, TOK)) == 0
        after = after & started
        full = started
    else:
        full = None

    def both(first, second):
        (q0, k0, v0, pk0, pv0, o0), (q1, k1, v1, pk1, pv1, o1) = first, second
        out_ref[o0] = attend_block(q0[0], (pk0, pk1, k0), (pv0, pv1, v0), (after, full, causal))
        out_ref[o1] = attend_block(q1[0], (pk1, k0, k1), (pv1, v0, v1), (after, None, causal))

    own = (qo, ko, vo, pko, pvo, 0)
    rec = (qr, kr, vr, pkr, pvr, 1)

    @pl.when(s_ref[0] == 0)
    def _():
        both(own, rec)

    @pl.when(s_ref[0] == 1)
    def _():
        both(rec, own)


def attention(c, scal, q, q_rec, k, k_rec, v, v_rec, pk_own, pk_rec, pv_own, pv_rec):
    if c == 0:
        prev = pl.BlockSpec((1, TOK, DH), lambda h, s: (0, 0, h))
    else:
        prev = pl.BlockSpec((1, TOK, DH), lambda h, s: (1 - s[4], 0, h))
    return pl.pallas_call(
        functools.partial(attention_kernel, c),
        name="window_attention",
        out_shape=jax.ShapeDtypeStruct((2, TOK, 2 * DH), f32),
        grid_spec=pltpu.PrefetchScalarGridSpec(
            num_scalar_prefetch=1,
            grid=(2,),
            in_specs=[own_spec(c), rec_spec(c)] * 3 + [prev] * 4,
            out_specs=pl.BlockSpec((2, TOK, DH), lambda h, s: (0, 0, h)),
        ),
        compiler_params=cparams(),
    )(scal, q, q_rec, k, k_rec, v, v_rec, pk_own, pk_rec, pv_own, pv_rec)


def finish_kernel(fast_ref, p0, p1, p2, p3, gain_ref, att_ref, own_ref, rec_ref):
    for j, out in enumerate((own_ref, rec_ref)):
        total = p0[j] + p1[j] + p2[j] + p3[j]
        rs = lax.rsqrt(total * (1.0 / 4096.0) + NORM_EPS)
        col = jnp.transpose(rs)[:, :1]
        out[...] = (fast_ref[j] * gain_ref[...] * col + att_ref[j]).astype(bf16)


def finish(fast, powers, gain, att):
    return pl.pallas_call(
        finish_kernel,
        name="finish",
        out_shape=[jax.ShapeDtypeStruct((TOK, 2 * DH), bf16)] * 2,
        compiler_params=cparams(),
    )(fast, *powers, gain, att)


def gather_pieces(m16):
    other = shift(m16, "yh", 1)
    out = []
    for head, (first, last) in enumerate((("z", "x"), ("x", "z"))):
        v = jnp.stack([m16[head], other[head]])
        v = jnp.concatenate([v] + [shift(v, first, k) for k in range(1, 4)], axis=0)
        out.append([v] + [shift(v, last, k) for k in range(1, 4)])
    return out[0] + out[1]


def scatter_sums(slabs):
    done = []
    for head, (first, last) in enumerate((("x", "z"), ("z", "x"))):
        mine = slabs[head * 4 : head * 4 + 4]
        total = mine[0].astype(f32)
        for k in range(1, 4):
            total = total + shift(mine[k], first, k).astype(f32)
        low = total.astype(bf16)
        part = total[0:2]
        for k in range(1, 4):
            part = part + shift(low[2 * k : 2 * k + 2], last, k).astype(f32)
        done.append(part)
    both = jnp.stack(done)
    return both[:, 0] + shift(both[:, 1].astype(bf16), "yh", 1).astype(f32)


def on_device(queries, key_rows, value_rows, step_rates, w_gate, w_up, w_down, out_gain):
    core = lax.axis_index("core")
    yh, z, x = lax.axis_index("yh"), lax.axis_index("z"), lax.axis_index("x")
    chip = (yh * 4 + z) * 4 + x
    first = (chip == 0).astype(jnp.int32)
    scal = jnp.stack([core, yh, z, x, first]).astype(jnp.int32)

    masters = jnp.stack([w_gate, w_up, w_down], axis=1)
    mine = lax.dynamic_slice_in_dim(masters, core * 2, 2, 0)
    theirs = lax.dynamic_slice_in_dim(masters, (1 - core) * 2, 2, 0)
    got = shift(theirs, "core", 1)
    m16 = jnp.where(
        core == 0,
        jnp.concatenate([mine, got], axis=2),
        jnp.concatenate([got, mine], axis=2),
    )
    pieces = gather_pieces(m16.astype(bf16))

    def split(a):
        keep = lax.dynamic_slice_in_dim(a, core * 1024, 1024, 2)
        give = lax.dynamic_slice_in_dim(a, (1 - core) * 1024, 1024, 2)
        return keep, shift(give, "core", 1)

    k_own, k_rec = split(key_rows)
    v_own, v_rec = split(value_rows)
    q_rec = split(queries)[1]
    rates = step_rates[:, 0, :]
    r_own = lax.dynamic_slice_in_dim(rates, core * 2, 2, 0)
    r_rec = shift(lax.dynamic_slice_in_dim(rates, (1 - core) * 2, 2, 0), "core", 1)
    rates = jnp.stack([r_own, r_rec], axis=1)[..., None]

    chips = ("yh", "z", "x")
    pairs = [(i, (i + 1) % 32) for i in range(32)]
    halo = [lax.ppermute(a, chips, pairs) for a in (k_own, k_rec, v_own, v_rec)]

    slabs = compute_grads(scal, pieces, key_rows, value_rows, k_rec, v_rec, rates)
    fast0, pow0 = fast_apply(0, scal, pieces, queries, q_rec)
    grad16 = scatter_sums(slabs)
    new16 = m16 - grad16
    pieces2 = gather_pieces(new16.astype(bf16))

    own_rows = lax.dynamic_slice_in_dim(new16, core * 8, 8, 2)
    their_rows = shift(lax.dynamic_slice_in_dim(new16, (1 - core) * 8, 8, 2), "core", 1)
    new_all = jnp.where(
        core == 0,
        jnp.concatenate([own_rows, their_rows], axis=0),
        jnp.concatenate([their_rows, own_rows], axis=0),
    )

    gain = lax.dynamic_slice_in_dim(out_gain, core * 1024, 1024, 0)[None]
    att = [
        attention(c, scal, queries, q_rec, key_rows, k_rec, value_rows, v_rec,
                  halo[0], halo[1], halo[2], halo[3])
        for c in range(2)
    ]
    fast1, pow1 = fast_apply(1, scal, pieces2, queries, q_rec)

    flat = ("heads", "core")

    def complete(fast, power, attended):
        swapped = power[::-1]
        others = [
            lax.ppermute(swapped, flat, [(0, 1), (1, 0), (2, 3), (3, 2)]),
            lax.ppermute(power, flat, [(0, 2), (2, 0), (1, 3), (3, 1)]),
            lax.ppermute(swapped, flat, [(0, 3), (3, 0), (1, 2), (2, 1)]),
        ]
        out_own, out_rec = finish(fast, [power] + others, gain, attended)
        arrived = shift(out_rec, "core", 1)
        return jnp.where(
            core == 0,
            jnp.concatenate([out_own, arrived], axis=1),
            jnp.concatenate([arrived, out_own], axis=1),
        )

    layer_out = jnp.stack(
        [complete(fast0, pow0, att[0]), complete(fast1, pow1, att[1])]
    )
    return layer_out, new_all[:, 0], new_all[:, 1], new_all[:, 2]


def solution(mesh):
    fine = Mesh(mesh.devices.reshape(2, 2, 4, 4, 2), ("heads",) + SEQ)
    rows = P(None, SEQ, "heads")
    weight = P("heads", SEQ, None)
    return jax.shard_map(
        on_device,
        mesh=fine,
        in_specs=(rows, rows, rows, P("heads", None, SEQ), weight, weight, weight, P("heads")),
        out_specs=(rows, weight, weight, weight),
        check_vma=False,
    )
```

```python
import functools

import jax
import jax.numpy as jnp
from jax import lax
from jax.experimental import pallas as pl
from jax.experimental.pallas import tpu as pltpu
from jax.sharding import Mesh, PartitionSpec as P

NORM_EPS = 1e-05
MASKED = -1e30
SIZES = {"heads": 2, "yh": 2, "z": 4, "x": 4, "core": 2}
SEQ = ("yh", "z", "x", "core")
TOK = 384
DH = 512
SCALE = DH ** -0.5

f32 = jnp.float32
bf16 = jnp.bfloat16


def shift(value, axis, steps):
    count = SIZES[axis]
    return lax.ppermute(value, axis, [(i, (i + steps) % count) for i in range(count)])


def dot(a, b, dims):
    return lax.dot_general(a, b, (dims, ((), ())), preferred_element_type=f32)


NN = ((1,), (0,))
NT = ((1,), (1,))
TN = ((0,), (0,))


def cparams(**kw):
    return pltpu.CompilerParams(vmem_limit_bytes=56 * 1024 * 1024, **kw)


def piece_rows(kind, part, idx, item):
    yh, z, x = idx
    a, k = item % 2, item // 2
    y = lax.rem(yh + a, 2)
    if kind == 0:
        zz, xx = lax.rem(z + k, 4), lax.rem(x + part, 4)
    else:
        zz, xx = lax.rem(z + part, 4), lax.rem(x + k, 4)
    return pl.multiple_of(y * 256 + zz * 64 + xx * 16, 16)


def weight_copies(head, pieces, w_vmem, sem, idx):
    for part in range(4):
        for item in range(8):
            row = piece_rows(head, part, idx, item)
            yield pltpu.make_async_copy(
                pieces[head * 4 + part].at[item],
                w_vmem.at[head, :, pl.ds(row, 16), :],
                sem.at[head],
            )


def load_weights(pieces, w_vmem, sem, idx, head_now):
    @pl.when(head_now == 0)
    def _():
        for head in range(2):
            for copy in weight_copies(head, pieces, w_vmem, sem, idx):
                copy.start()

    for head in range(2):

        @pl.when(head_now == head)
        def _(head=head):
            pltpu.make_async_copy(w_vmem.at[head], w_vmem.at[head], sem.at[head]).wait()


def grads_kernel(s_ref, *refs):
    pieces = refs[:8]
    k_own, v_own, k_rec, v_rec, r_ref = refs[8:13]
    outs = refs[13:21]
    w_vmem, sums, sem = refs[21:]
    head = pl.program_id(0)
    idx = (s_ref[1], s_ref[2], s_ref[3])
    load_weights(pieces, w_vmem, sem, idx, head)
    gate, up, down = w_vmem[head, 0], w_vmem[head, 1], w_vmem[head, 2]
    for j, (k_ref, v_ref) in enumerate(((k_own, v_own), (k_rec, v_rec))):
        k = k_ref[0]
        rate = r_ref[0, j]
        target = (-(rate * v_ref[0].astype(f32))).astype(bf16)
        g = dot(k, gate, NN)
        u = dot(k, up, NN)
        back = dot(target, down, NT)
        s = jax.nn.sigmoid(g)
        silu = g * s
        active = (silu * u).astype(bf16)
        d_gate = (back * u * s * (1.0 + g * (1.0 - s))).astype(bf16)
        d_up = (back * silu).astype(bf16)
        parts = (dot(k, d_gate, TN), dot(k, d_up, TN), dot(active, target, TN))
        for m in range(3):
            if j == 0:
                sums[m] = parts[m]
            else:
                sums[m] += parts[m]
    yh, z, x = idx
    for kind in range(2):

        @pl.when(head == kind)
        def _(kind=kind):
            for part in range(4):
                for item in range(8):
                    a, k = item % 2, item // 2
                    y = lax.rem(yh + a, 2)
                    zz = lax.rem(z + 4 - (k if kind == 0 else part), 4)
                    xx = lax.rem(x + 4 - (part if kind == 0 else k), 4)
                    row = pl.multiple_of(y * 256 + zz * 64 + xx * 16, 16)
                    for m in range(3):
                        outs[kind * 4 + part][item, m] = sums[m, pl.ds(row, 16), :].astype(bf16)


def own_spec(c):
    return pl.BlockSpec((1, TOK, DH), lambda h, s: (c, 0, s[0] * 2 + h))


def rec_spec(c):
    return pl.BlockSpec((1, TOK, DH), lambda h, s: (c, 0, h))


ANY = pl.BlockSpec(memory_space=pl.ANY)


def compute_grads(scal, pieces, k, v, k_rec, v_rec, rates):
    whole = pl.BlockSpec((8, 3, 16, DH), lambda h, s: (0, 0, 0, 0))
    return pl.pallas_call(
        grads_kernel,
        name="fast_grads",
        out_shape=[jax.ShapeDtypeStruct((8, 3, 16, DH), bf16)] * 8,
        grid_spec=pltpu.PrefetchScalarGridSpec(
            num_scalar_prefetch=1,
            grid=(2,),
            in_specs=[ANY] * 8
            + [own_spec(0), own_spec(0), rec_spec(0), rec_spec(0)]
            + [pl.BlockSpec((1, 2, TOK, 1), lambda h, s: (h, 0, 0, 0))],
            out_specs=[whole] * 8,
            scratch_shapes=[
                pltpu.VMEM((2, 3, DH, DH), bf16),
                pltpu.VMEM((3, DH, DH), f32),
                pltpu.SemaphoreType.DMA((2,)),
            ],
        ),
        compiler_params=cparams(),
    )(scal, *pieces, k, v, k_rec, v_rec, rates)


def apply_kernel(s_ref, *refs):
    pieces = refs[:8]
    q_own, q_rec = refs[8:10]
    out_ref, pow_ref = refs[10:12]
    w_vmem, sem = refs[12:]
    head = pl.program_id(0)
    idx = (s_ref[1], s_ref[2], s_ref[3])
    load_weights(pieces, w_vmem, sem, idx, head)
    gate, up, down = w_vmem[head, 0], w_vmem[head, 1], w_vmem[head, 2]
    ones = jnp.ones((8, DH), f32)
    for j, q_ref in enumerate((q_own, q_rec)):
        q = q_ref[0]
        g = dot(q, gate, NN)
        u = dot(q, up, NN)
        active = (g * jax.nn.sigmoid(g) * u).astype(bf16)
        out = dot(active, down, NN)
        out_ref[j] = out
        power = lax.dot_general(
            ones, out * out, (NT, ((), ())),
            precision=lax.Precision.HIGHEST, preferred_element_type=f32,
        )

        @pl.when(head == 0)
        def _(j=j, power=power):
            pow_ref[j] = power

        @pl.when(head == 1)
        def _(j=j, power=power):
            pow_ref[j] += power


def fast_apply(c, scal, pieces, q, q_rec):
    return pl.pallas_call(
        apply_kernel,
        name="fast_apply",
        out_shape=[
            jax.ShapeDtypeStruct((2, TOK, 2 * DH), f32),
            jax.ShapeDtypeStruct((2, 8, TOK), f32),
        ],
        grid_spec=pltpu.PrefetchScalarGridSpec(
            num_scalar_prefetch=1,
            grid=(2,),
            in_specs=[ANY] * 8 + [own_spec(c), rec_spec(c)],
            out_specs=[
                pl.BlockSpec((2, TOK, DH), lambda h, s: (0, 0, h)),
                pl.BlockSpec((2, 8, TOK), lambda h, s: (0, 0, 0)),
            ],
            scratch_shapes=[
                pltpu.VMEM((2, 3, DH, DH), bf16),
                pltpu.SemaphoreType.DMA((2,)),
            ],
        ),
        compiler_params=cparams(),
    )(scal, *pieces, q, q_rec)


def attend_block(q, keys, values, masks):
    scores = []
    for k_ref, mask in zip(keys, masks):
        s = dot(q, k_ref[0], NT) * SCALE
        if mask is not None:
            s = jnp.where(mask, s, MASKED)
        scores.append(s)
    peak = functools.reduce(jnp.maximum, [jnp.max(s, axis=-1, keepdims=True) for s in scores])
    weights = [jnp.exp(s - peak) for s in scores]
    total = sum(jnp.sum(w, axis=-1, keepdims=True) for w in weights)
    inv = 1.0 / total
    return sum(
        dot((w * inv).astype(bf16), v_ref[0], NN) for w, v_ref in zip(weights, values)
    )


def attention_kernel(c, s_ref, qo, qr, ko, kr, vo, vr, pko, pkr, pvo, pvr, out_ref):
    row = lax.broadcasted_iota(jnp.int32, (TOK, TOK), 0)
    col = lax.broadcasted_iota(jnp.int32, (TOK, TOK), 1)
    causal = col <= row
    after = col > row
    if c == 0:
        started = jnp.broadcast_to(s_ref[4], (TOK, TOK)) == 0
        after = after & started
        full = started
    else:
        full = None

    def both(first, second):
        (q0, k0, v0, pk0, pv0, o0), (q1, k1, v1, pk1, pv1, o1) = first, second
        out_ref[o0] = attend_block(q0[0], (pk0, pk1, k0), (pv0, pv1, v0), (after, full, causal))
        out_ref[o1] = attend_block(q1[0], (pk1, k0, k1), (pv1, v0, v1), (after, None, causal))

    own = (qo, ko, vo, pko, pvo, 0)
    rec = (qr, kr, vr, pkr, pvr, 1)

    @pl.when(s_ref[0] == 0)
    def _():
        both(own, rec)

    @pl.when(s_ref[0] == 1)
    def _():
        both(rec, own)


def attention(c, scal, q, q_rec, k, k_rec, v, v_rec, prev):
    return pl.pallas_call(
        functools.partial(attention_kernel, c),
        name="window_attention",
        out_shape=jax.ShapeDtypeStruct((2, TOK, 2 * DH), f32),
        grid_spec=pltpu.PrefetchScalarGridSpec(
            num_scalar_prefetch=1,
            grid=(2,),
            in_specs=[own_spec(c), rec_spec(c)] * 3
            + [pl.BlockSpec((1, TOK, DH), lambda h, s, j=j: (j, 0, h)) for j in range(4)],
            out_specs=pl.BlockSpec((2, TOK, DH), lambda h, s: (0, 0, h)),
        ),
        compiler_params=cparams(),
    )(scal, q, q_rec, k, k_rec, v, v_rec, prev, prev, prev, prev)


def finish_kernel(fast_ref, p0, p1, p2, p3, gain_ref, att_ref, own_ref, rec_ref):
    for j, out in enumerate((own_ref, rec_ref)):
        total = p0[j] + p1[j] + p2[j] + p3[j]
        rs = lax.rsqrt(total * (1.0 / 4096.0) + NORM_EPS)
        col = jnp.transpose(rs)[:, :1]
        out[...] = (fast_ref[j] * gain_ref[...] * col + att_ref[j]).astype(bf16)


def finish(fast, powers, gain, att):
    return pl.pallas_call(
        finish_kernel,
        name="finish",
        out_shape=[jax.ShapeDtypeStruct((TOK, 2 * DH), bf16)] * 2,
        compiler_params=cparams(),
    )(fast, *powers, gain, att)


def gather_direct(m16):
    other = shift(m16, "yh", 1)
    out = []
    for head, (first, last) in enumerate((("z", "x"), ("x", "z"))):
        v = jnp.stack([m16[head], other[head]])
        v = jnp.concatenate([v] + [shift(v, first, -k) for k in range(1, 4)], axis=0)
        out.append([v] + [shift(v, last, -k) for k in range(1, 4)])
    return out[0] + out[1]


def gather_rings(m16):
    other = shift(m16, "yh", 1)
    axes = (("z", "x"), ("x", "z"))
    now = [jnp.stack([m16[h], other[h]]) for h in range(2)]
    held = [[n] for n in now]
    for _ in range(3):
        for h in range(2):
            now[h] = shift(now[h], axes[h][0], -1)
            held[h].append(now[h])
    now = [jnp.concatenate(held[h], axis=0) for h in range(2)]
    out = [[n] for n in now]
    for _ in range(3):
        for h in range(2):
            now[h] = shift(now[h], axes[h][1], -1)
            out[h].append(now[h])
    return out[0] + out[1]


def scatter_rings(slabs):
    axes = (("x", "z"), ("z", "x"))
    now = [slabs[3], slabs[7]]
    for k in (2, 1, 0):
        for h in range(2):
            got = shift(now[h], axes[h][0], -1)
            total = got.astype(f32) + slabs[h * 4 + k].astype(f32)
            now[h] = total.astype(bf16) if k else total
    parts = now
    now = [p[6:8] for p in parts]
    for k in (2, 1, 0):
        for h in range(2):
            got = shift(now[h], axes[h][1], -1)
            now[h] = got + parts[h][2 * k : 2 * k + 2]
    both = jnp.stack(now)
    return both[:, 0] + shift(both[:, 1], "yh", 1)


def on_device(queries, key_rows, value_rows, step_rates, w_gate, w_up, w_down, out_gain):
    core = lax.axis_index("core")
    yh, z, x = lax.axis_index("yh"), lax.axis_index("z"), lax.axis_index("x")
    chip = (yh * 4 + z) * 4 + x
    first = (chip == 0).astype(jnp.int32)
    scal = jnp.stack([core, yh, z, x, first]).astype(jnp.int32)

    masters = jnp.stack([w_gate, w_up, w_down], axis=1)
    mine = lax.dynamic_slice_in_dim(masters, core * 2, 2, 0)
    theirs = lax.dynamic_slice_in_dim(masters, (1 - core) * 2, 2, 0)
    got = shift(theirs, "core", 1)
    m16 = jnp.where(
        core == 0,
        jnp.concatenate([mine, got], axis=2),
        jnp.concatenate([got, mine], axis=2),
    )
    pieces = gather_direct(m16.astype(bf16))

    def split(a):
        keep = lax.dynamic_slice_in_dim(a, core * 1024, 1024, 2)
        give = lax.dynamic_slice_in_dim(a, (1 - core) * 1024, 1024, 2)
        return keep, shift(give, "core", 1)

    k_own, k_rec = split(key_rows)
    v_own, v_rec = split(value_rows)
    q_rec = split(queries)[1]
    rates = step_rates[:, 0, :]
    r_own = lax.dynamic_slice_in_dim(rates, core * 2, 2, 0)
    r_rec = shift(lax.dynamic_slice_in_dim(rates, (1 - core) * 2, 2, 0), "core", 1)
    rates = jnp.stack([r_own, r_rec], axis=1)[..., None]

    chips = ("yh", "z", "x")
    row = [(i, (i + 1) % 32) for i in range(32) if i % 16 != 15]
    turn = [(15, 16), (31, 0)]
    pair = [jnp.stack([k_own[c], k_rec[c], v_own[c], v_rec[c]]) for c in range(2)]
    pair[0], pair[1], *pieces = lax.optimization_barrier((pair[0], pair[1], *pieces))
    halo = []
    for c in range(2):
        halo.append(lax.ppermute(pair[c], chips, row))
    turned0 = lax.ppermute(pair[0], chips, turn)

    slabs = compute_grads(scal, pieces, key_rows, value_rows, k_rec, v_rec, rates)
    fast0, pow0 = fast_apply(0, scal, pieces, queries, q_rec)
    grad16 = scatter_rings(slabs)
    new16 = m16 - grad16
    pieces2 = gather_rings(new16.astype(bf16))
    pair1, _ = lax.optimization_barrier((pair[1], grad16[0, 0, 0, 0]))
    turned1 = lax.ppermute(pair1, chips, turn)
    at_turn = (z == 0) & (x == 0)
    prev = [jnp.where(at_turn, t, h) for t, h in zip((turned0, turned1), halo)]

    own_rows = lax.dynamic_slice_in_dim(new16, core * 8, 8, 2)
    their_rows = shift(lax.dynamic_slice_in_dim(new16, (1 - core) * 8, 8, 2), "core", 1)
    new_all = jnp.where(
        core == 0,
        jnp.concatenate([own_rows, their_rows], axis=0),
        jnp.concatenate([their_rows, own_rows], axis=0),
    )

    gain = lax.dynamic_slice_in_dim(out_gain, core * 1024, 1024, 0)[None]
    before = [prev[0], jnp.where(chip == 0, prev[0], prev[1])]
    att = []
    for c in range(2):
        att.append(attention(c, scal, queries, q_rec, key_rows, k_rec,
                             value_rows, v_rec, before[c]))
    fast1, pow1 = fast_apply(1, scal, pieces2, queries, q_rec)

    flat = ("heads", "core")

    def complete(fast, power, attended):
        swapped = power[::-1]
        others = [
            lax.ppermute(swapped, flat, [(0, 1), (1, 0), (2, 3), (3, 2)]),
            lax.ppermute(power, flat, [(0, 2), (2, 0), (1, 3), (3, 1)]),
            lax.ppermute(swapped, flat, [(0, 3), (3, 0), (1, 2), (2, 1)]),
        ]
        out_own, out_rec = finish(fast, [power] + others, gain, attended)
        arrived = shift(out_rec, "core", 1)
        return jnp.where(
            core == 0,
            jnp.concatenate([out_own, arrived], axis=1),
            jnp.concatenate([arrived, out_own], axis=1),
        )

    layer_out = jnp.stack([complete(fast0, pow0, att[0]), complete(fast1, pow1, att[1])])
    return layer_out, new_all[:, 0], new_all[:, 1], new_all[:, 2]


def solution(mesh):
    fine = Mesh(mesh.devices.reshape(2, 2, 4, 4, 2), ("heads",) + SEQ)
    rows = P(None, SEQ, "heads")
    weight = P("heads", SEQ, None)
    return jax.shard_map(
        on_device,
        mesh=fine,
        in_specs=(rows, rows, rows, P("heads", None, SEQ), weight, weight, weight, P("heads")),
        out_specs=(rows, weight, weight, weight),
        check_vma=False,
    )
```

```python
import functools

import jax
import jax.numpy as jnp
from jax import lax
from jax.experimental import pallas as pl
from jax.experimental.pallas import tpu as pltpu
from jax.sharding import Mesh, PartitionSpec as P

NORM_EPS = 1e-05
MASKED = -1e30
SIZES = {"heads": 2, "yh": 2, "z": 4, "x": 4, "core": 2}
SEQ = ("yh", "z", "x", "core")
TOK = 384
DH = 512
SCALE = DH ** -0.5

f32 = jnp.float32
bf16 = jnp.bfloat16


def shift(value, axis, steps):
    count = SIZES[axis]
    return lax.ppermute(value, axis, [(i, (i + steps) % count) for i in range(count)])


def dot(a, b, dims):
    return lax.dot_general(a, b, (dims, ((), ())), preferred_element_type=f32)


NN = ((1,), (0,))
NT = ((1,), (1,))
TN = ((0,), (0,))


def cparams(**kw):
    return pltpu.CompilerParams(vmem_limit_bytes=56 * 1024 * 1024, **kw)


def piece_rows(kind, part, idx, item):
    yh, z, x = idx
    a, k = item % 2, item // 2
    y = lax.rem(yh + a, 2)
    if kind == 0:
        zz, xx = lax.rem(z + k, 4), lax.rem(x + part, 4)
    else:
        zz, xx = lax.rem(z + part, 4), lax.rem(x + k, 4)
    return pl.multiple_of(y * 256 + zz * 64 + xx * 16, 16)


def weight_copies(head, pieces, w_vmem, sem, idx):
    for part in range(4):
        for item in range(8):
            row = piece_rows(head, part, idx, item)
            yield pltpu.make_async_copy(
                pieces[head * 4 + part].at[item],
                w_vmem.at[head, :, pl.ds(row, 16), :],
                sem.at[head],
            )


def load_weights(pieces, w_vmem, sem, idx, head_now):
    @pl.when(head_now == 0)
    def _():
        for head in range(2):
            for copy in weight_copies(head, pieces, w_vmem, sem, idx):
                copy.start()

    for head in range(2):

        @pl.when(head_now == head)
        def _(head=head):
            pltpu.make_async_copy(w_vmem.at[head], w_vmem.at[head], sem.at[head]).wait()


def grads_kernel(s_ref, *refs):
    pieces = refs[:8]
    k_own, v_own, k_rec, v_rec, r_ref = refs[8:13]
    outs = refs[13:21]
    w_vmem, sums, sem = refs[21:]
    head = pl.program_id(0)
    idx = (s_ref[1], s_ref[2], s_ref[3])
    load_weights(pieces, w_vmem, sem, idx, head)
    gate, up, down = w_vmem[head, 0], w_vmem[head, 1], w_vmem[head, 2]
    for j, (k_ref, v_ref) in enumerate(((k_own, v_own), (k_rec, v_rec))):
        k = k_ref[0]
        rate = r_ref[0, j]
        target = (-(rate * v_ref[0].astype(f32))).astype(bf16)
        g = dot(k, gate, NN)
        u = dot(k, up, NN)
        back = dot(target, down, NT)
        s = jax.nn.sigmoid(g)
        silu = g * s
        active = (silu * u).astype(bf16)
        d_gate = (back * u * s * (1.0 + g * (1.0 - s))).astype(bf16)
        d_up = (back * silu).astype(bf16)
        parts = (dot(k, d_gate, TN), dot(k, d_up, TN), dot(active, target, TN))
        for m in range(3):
            if j == 0:
                sums[m] = parts[m]
            else:
                sums[m] += parts[m]
    yh, z, x = idx
    for kind in range(2):

        @pl.when(head == kind)
        def _(kind=kind):
            for part in range(4):
                for item in range(8):
                    a, k = item % 2, item // 2
                    y = lax.rem(yh + a, 2)
                    zz = lax.rem(z + 4 - (k if kind == 0 else part), 4)
                    xx = lax.rem(x + 4 - (part if kind == 0 else k), 4)
                    row = pl.multiple_of(y * 256 + zz * 64 + xx * 16, 16)
                    for m in range(3):
                        outs[kind * 4 + part][item, m] = sums[m, pl.ds(row, 16), :].astype(bf16)


def own_spec(c):
    return pl.BlockSpec((1, TOK, DH), lambda h, s: (c, 0, s[0] * 2 + h))


def rec_spec(c):
    return pl.BlockSpec((1, TOK, DH), lambda h, s: (c, 0, h))


ANY = pl.BlockSpec(memory_space=pl.ANY)


def compute_grads(scal, pieces, k, v, k_rec, v_rec, rates):
    whole = pl.BlockSpec((8, 3, 16, DH), lambda h, s: (0, 0, 0, 0))
    return pl.pallas_call(
        grads_kernel,
        name="fast_grads",
        out_shape=[jax.ShapeDtypeStruct((8, 3, 16, DH), bf16)] * 8,
        grid_spec=pltpu.PrefetchScalarGridSpec(
            num_scalar_prefetch=1,
            grid=(2,),
            in_specs=[ANY] * 8
            + [own_spec(0), own_spec(0), rec_spec(0), rec_spec(0)]
            + [pl.BlockSpec((1, 2, TOK, 1), lambda h, s: (h, 0, 0, 0))],
            out_specs=[whole] * 8,
            scratch_shapes=[
                pltpu.VMEM((2, 3, DH, DH), bf16),
                pltpu.VMEM((3, DH, DH), f32),
                pltpu.SemaphoreType.DMA((2,)),
            ],
        ),
        compiler_params=cparams(),
    )(scal, *pieces, k, v, k_rec, v_rec, rates)


def apply_kernel(s_ref, *refs):
    pieces = refs[:8]
    q_own, q_rec = refs[8:10]
    out_ref, pow_ref = refs[10:12]
    w_vmem, sem = refs[12:]
    head = pl.program_id(0)
    idx = (s_ref[1], s_ref[2], s_ref[3])
    load_weights(pieces, w_vmem, sem, idx, head)
    gate, up, down = w_vmem[head, 0], w_vmem[head, 1], w_vmem[head, 2]
    ones = jnp.ones((8, DH), f32)
    for j, q_ref in enumerate((q_own, q_rec)):
        q = q_ref[0]
        g = dot(q, gate, NN)
        u = dot(q, up, NN)
        active = (g * jax.nn.sigmoid(g) * u).astype(bf16)
        out = dot(active, down, NN)
        out_ref[j] = out
        power = lax.dot_general(
            ones, out * out, (NT, ((), ())),
            precision=lax.Precision.HIGHEST, preferred_element_type=f32,
        )

        @pl.when(head == 0)
        def _(j=j, power=power):
            pow_ref[j] = power

        @pl.when(head == 1)
        def _(j=j, power=power):
            pow_ref[j] += power


def fast_apply(c, scal, pieces, q, q_rec):
    return pl.pallas_call(
        apply_kernel,
        name="fast_apply",
        out_shape=[
            jax.ShapeDtypeStruct((2, TOK, 2 * DH), f32),
            jax.ShapeDtypeStruct((2, 8, TOK), f32),
        ],
        grid_spec=pltpu.PrefetchScalarGridSpec(
            num_scalar_prefetch=1,
            grid=(2,),
            in_specs=[ANY] * 8 + [own_spec(c), rec_spec(c)],
            out_specs=[
                pl.BlockSpec((2, TOK, DH), lambda h, s: (0, 0, h)),
                pl.BlockSpec((2, 8, TOK), lambda h, s: (0, 0, 0)),
            ],
            scratch_shapes=[
                pltpu.VMEM((2, 3, DH, DH), bf16),
                pltpu.SemaphoreType.DMA((2,)),
            ],
        ),
        compiler_params=cparams(),
    )(scal, *pieces, q, q_rec)


def attend_block(q, keys, values, masks):
    scores = []
    for k_ref, mask in zip(keys, masks):
        s = dot(q, k_ref[0], NT) * SCALE
        if mask is not None:
            s = jnp.where(mask, s, MASKED)
        scores.append(s)
    peak = functools.reduce(jnp.maximum, [jnp.max(s, axis=-1, keepdims=True) for s in scores])
    weights = [jnp.exp(s - peak) for s in scores]
    total = sum(jnp.sum(w, axis=-1, keepdims=True) for w in weights)
    inv = 1.0 / total
    return sum(
        dot((w * inv).astype(bf16), v_ref[0], NN) for w, v_ref in zip(weights, values)
    )


def attention_kernel(c, s_ref, qo, qr, ko, kr, vo, vr, pko, pkr, pvo, pvr, out_ref):
    row = lax.broadcasted_iota(jnp.int32, (TOK, TOK), 0)
    col = lax.broadcasted_iota(jnp.int32, (TOK, TOK), 1)
    causal = col <= row
    after = col > row
    if c == 0:
        started = jnp.broadcast_to(s_ref[4], (TOK, TOK)) == 0
        after = after & started
        full = started
    else:
        full = None

    def both(first, second):
        (q0, k0, v0, pk0, pv0, o0), (q1, k1, v1, pk1, pv1, o1) = first, second
        out_ref[o0] = attend_block(q0[0], (pk0, pk1, k0), (pv0, pv1, v0), (after, full, causal))
        out_ref[o1] = attend_block(q1[0], (pk1, k0, k1), (pv1, v0, v1), (after, None, causal))

    own = (qo, ko, vo, pko, pvo, 0)
    rec = (qr, kr, vr, pkr, pvr, 1)

    @pl.when(s_ref[0] == 0)
    def _():
        both(own, rec)

    @pl.when(s_ref[0] == 1)
    def _():
        both(rec, own)


def attention(c, scal, q, q_rec, k, k_rec, v, v_rec, prev):
    return pl.pallas_call(
        functools.partial(attention_kernel, c),
        name="window_attention",
        out_shape=jax.ShapeDtypeStruct((2, TOK, 2 * DH), f32),
        grid_spec=pltpu.PrefetchScalarGridSpec(
            num_scalar_prefetch=1,
            grid=(2,),
            in_specs=[own_spec(c), rec_spec(c)] * 3
            + [pl.BlockSpec((1, TOK, DH), lambda h, s, j=j: (j, 0, h)) for j in range(4)],
            out_specs=pl.BlockSpec((2, TOK, DH), lambda h, s: (0, 0, h)),
        ),
        compiler_params=cparams(),
    )(scal, q, q_rec, k, k_rec, v, v_rec, prev, prev, prev, prev)


def finish_kernel(s_ref, fast_ref, p0, p1, p2, p3, gain_ref, att_ref, *refs):
    own_ref, rec_ref = refs[-2:]
    total = p0[...] + p1[...] + p2[...] + p3[...]
    rs = lax.rsqrt(total * (1.0 / 4096.0) + NORM_EPS)
    for j in range(2):
        col = jnp.transpose(rs[j])[:, :1]
        out = (fast_ref[j] * gain_ref[...] * col + att_ref[j]).astype(bf16)
        if j == 0:
            own_ref[0] = out
        else:
            rec_ref[...] = out


def finish(c, scal, fast, powers, gain, att, layer):
    both = pl.BlockSpec((2, TOK, DH), lambda h, s: (0, 0, h))
    power = pl.BlockSpec((2, 8, TOK), lambda h, s: (0, 0, 0))
    more = [] if layer is None else [layer]
    return pl.pallas_call(
        finish_kernel,
        name="finish",
        out_shape=[
            jax.ShapeDtypeStruct((2, TOK, 4 * DH), bf16),
            jax.ShapeDtypeStruct((TOK, 2 * DH), bf16),
        ],
        grid_spec=pltpu.PrefetchScalarGridSpec(
            num_scalar_prefetch=1,
            grid=(2,),
            in_specs=[both] + [power] * 4 + [pl.BlockSpec((1, DH), lambda h, s: (0, h)), both]
            + [ANY] * len(more),
            out_specs=[
                pl.BlockSpec((1, TOK, DH), lambda h, s: (c, 0, s[0] * 2 + h)),
                pl.BlockSpec((TOK, DH), lambda h, s: (0, h)),
            ],
        ),
        input_output_aliases={8: 0} if more else {},
        compiler_params=cparams(),
    )(scal, fast, *powers, gain, att, *more)


def place_kernel(s_ref, arrived_ref, layer_ref, out_ref):
    out_ref[0] = arrived_ref[...]


def place(c, scal, arrived, layer):
    return pl.pallas_call(
        place_kernel,
        name="place",
        out_shape=jax.ShapeDtypeStruct((2, TOK, 4 * DH), bf16),
        grid_spec=pltpu.PrefetchScalarGridSpec(
            num_scalar_prefetch=1,
            grid=(2,),
            in_specs=[pl.BlockSpec((TOK // 2, 2 * DH), lambda i, s: (i, 0)), ANY],
            out_specs=pl.BlockSpec((1, TOK // 2, 2 * DH), lambda i, s: (c, i, 1 - s[0])),
        ),
        input_output_aliases={2: 0},
        compiler_params=cparams(),
    )(scal, arrived, layer)


def gather_direct(both):
    out = []
    for head, (first, last) in enumerate((("z", "x"), ("x", "z"))):
        v = both[head]
        v = jnp.concatenate([v] + [shift(v, first, -k) for k in range(1, 4)], axis=0)
        out.append([v] + [shift(v, last, -k) for k in range(1, 4)])
    return out[0] + out[1]


def gather_rings(both):
    axes = (("z", "x"), ("x", "z"))
    now = [both[h] for h in range(2)]
    held = [[n] for n in now]
    for _ in range(3):
        for h in range(2):
            now[h] = shift(now[h], axes[h][0], -1)
            held[h].append(now[h])
    now = [jnp.concatenate(held[h], axis=0) for h in range(2)]
    out = [[n] for n in now]
    for _ in range(3):
        for h in range(2):
            now[h] = shift(now[h], axes[h][1], -1)
            out[h].append(now[h])
    return out[0] + out[1]


def scatter_rings(slabs):
    axes = (("x", "z"), ("z", "x"))
    now = [slabs[3], slabs[7]]
    for k in (2, 1, 0):
        for h in range(2):
            got = shift(now[h], axes[h][0], -1)
            total = got.astype(f32) + slabs[h * 4 + k].astype(f32)
            now[h] = total.astype(bf16) if k else total
    parts = now
    now = [p[6:8] for p in parts]
    for k in (2, 1, 0):
        for h in range(2):
            got = shift(now[h], axes[h][1], -1)
            now[h] = got + parts[h][2 * k : 2 * k + 2]
    return jnp.stack(now).astype(bf16)


def power_parts(power):
    flat = ("heads", "core")
    swapped = power[::-1]
    return [
        lax.ppermute(swapped, flat, [(0, 1), (1, 0), (2, 3), (3, 2)]),
        lax.ppermute(power, flat, [(0, 2), (2, 0), (1, 3), (3, 1)]),
        lax.ppermute(swapped, flat, [(0, 3), (3, 0), (1, 2), (2, 1)]),
    ]


def on_device(queries, key_rows, value_rows, step_rates, w_gate, w_up, w_down, out_gain):
    core = lax.axis_index("core")
    yh, z, x = lax.axis_index("yh"), lax.axis_index("z"), lax.axis_index("x")
    chip = (yh * 4 + z) * 4 + x
    first = (chip == 0).astype(jnp.int32)
    scal = jnp.stack([core, yh, z, x, first]).astype(jnp.int32)

    masters = jnp.stack([w_gate, w_up, w_down], axis=1)
    mine = lax.dynamic_slice_in_dim(masters, core * 2, 2, 0)
    theirs = lax.dynamic_slice_in_dim(masters, (1 - core) * 2, 2, 0)
    got = shift(theirs, "core", 1)
    m16 = jnp.where(
        core == 0,
        jnp.concatenate([mine, got], axis=2),
        jnp.concatenate([got, mine], axis=2),
    )
    m16_other = shift(m16, "yh", 1)
    m16_other, key_rows, value_rows, queries, step_rates = lax.optimization_barrier(
        (m16_other, key_rows, value_rows, queries, step_rates)
    )
    both = jnp.stack([m16, m16_other], axis=1)
    pieces = gather_direct(both.astype(bf16))

    def split(a):
        keep = lax.dynamic_slice_in_dim(a, core * 1024, 1024, 2)
        give = lax.dynamic_slice_in_dim(a, (1 - core) * 1024, 1024, 2)
        return keep, shift(give, "core", 1)

    k_own, k_rec = split(key_rows)
    v_own, v_rec = split(value_rows)
    q_rec = split(queries)[1]
    rates = step_rates[:, 0, :]
    r_own = lax.dynamic_slice_in_dim(rates, core * 2, 2, 0)
    r_rec = shift(lax.dynamic_slice_in_dim(rates, (1 - core) * 2, 2, 0), "core", 1)
    rates = jnp.stack([r_own, r_rec], axis=1)[..., None]

    chips = ("yh", "z", "x")
    row = [(i, (i + 1) % 32) for i in range(32) if i % 16 != 15]
    turn = [(15, 16), (31, 0)]
    pair = [jnp.stack([k_own[c], k_rec[c], v_own[c], v_rec[c]]) for c in range(2)]
    pair[0], pair[1], *pieces = lax.optimization_barrier((pair[0], pair[1], *pieces))
    halo = []
    for c in range(2):
        halo.append(lax.ppermute(pair[c], chips, row))
    turned0 = lax.ppermute(pair[0], chips, turn)

    slabs = compute_grads(scal, pieces, key_rows, value_rows, k_rec, v_rec, rates)
    fast0, pow0 = fast_apply(0, scal, pieces, queries, q_rec)
    half_sums = scatter_rings(slabs)
    half_sums, pow0 = lax.optimization_barrier((half_sums, pow0))
    other_sums = shift(half_sums, "yh", 1)
    powers0 = [pow0] + power_parts(pow0)
    grad_both = half_sums.astype(f32) + other_sums[:, ::-1].astype(f32)
    grad_both, pair1, *powers0 = lax.optimization_barrier((grad_both, pair[1], *powers0))
    new_both = both - grad_both
    new16 = new_both[:, 0]
    pieces2 = gather_rings(new_both.astype(bf16))
    turned1 = lax.ppermute(pair1, chips, turn[:1])
    own_rows = lax.dynamic_slice_in_dim(new16, core * 8, 8, 2)
    their_rows = shift(lax.dynamic_slice_in_dim(new16, (1 - core) * 8, 8, 2), "core", 1)
    new_all = jnp.where(
        core == 0,
        jnp.concatenate([own_rows, their_rows], axis=0),
        jnp.concatenate([their_rows, own_rows], axis=0),
    )

    gain = lax.dynamic_slice_in_dim(out_gain, core * 1024, 1024, 0)[None]
    at_turn = (z == 0) & (x == 0)

    def attend(c, before):
        return attention(c, scal, queries, q_rec, key_rows, k_rec, value_rows, v_rec, before)

    before0 = jnp.where(at_turn, turned0, halo[0])
    att0 = attend(0, before0)
    fast1, pow1 = fast_apply(1, scal, pieces2, queries, q_rec)
    powers1 = [pow1] + power_parts(pow1)
    fast1, turned1, halo1, before0 = lax.optimization_barrier(
        (fast1, turned1, halo[1], before0)
    )
    before1 = jnp.where(chip == 0, before0, jnp.where(at_turn, turned1, halo1))
    att1 = attend(1, before1)

    def complete(c, fast, powers, attended, layer):
        layer, out_rec = finish(c, scal, fast, powers, gain, attended, layer)
        arrived = shift(out_rec, "core", 1)
        return place(c, scal, arrived, layer)

    layer_out = complete(0, fast0, powers0, att0, None)
    layer_out = complete(1, fast1, powers1, att1, layer_out)
    return layer_out, new_all[:, 0], new_all[:, 1], new_all[:, 2]


def solution(mesh):
    fine = Mesh(mesh.devices.reshape(2, 2, 4, 4, 2), ("heads",) + SEQ)
    rows = P(None, SEQ, "heads")
    weight = P("heads", SEQ, None)
    return jax.shard_map(
        on_device,
        mesh=fine,
        in_specs=(rows, rows, rows, P("heads", None, SEQ), weight, weight, weight, P("heads")),
        out_specs=(rows, weight, weight, weight),
        check_vma=False,
    )
```

```python
import functools

import jax
import jax.numpy as jnp
from jax import lax
from jax.experimental import pallas as pl
from jax.experimental.pallas import tpu as pltpu
from jax.sharding import Mesh, PartitionSpec as P

NORM_EPS = 1e-05
MASKED = -1e30
SIZES = {"heads": 2, "yh": 2, "z": 4, "x": 4, "core": 2}
SEQ = ("yh", "z", "x", "core")
TOK = 384
DH = 512
SCALE = DH ** -0.5

f32 = jnp.float32
bf16 = jnp.bfloat16


def shift(value, axis, steps):
    count = SIZES[axis]
    return lax.ppermute(value, axis, [(i, (i + steps) % count) for i in range(count)])


def dot(a, b, dims):
    return lax.dot_general(a, b, (dims, ((), ())), preferred_element_type=f32)


NN = ((1,), (0,))
NT = ((1,), (1,))
TN = ((0,), (0,))


def cparams(**kw):
    return pltpu.CompilerParams(vmem_limit_bytes=56 * 1024 * 1024, **kw)


def piece_rows(kind, part, idx, item):
    yh, z, x = idx
    a, k = item % 2, item // 2
    y = lax.rem(yh + a, 2)
    if kind == 0:
        zz, xx = lax.rem(z + k, 4), lax.rem(x + part, 4)
    else:
        zz, xx = lax.rem(z + part, 4), lax.rem(x + k, 4)
    return pl.multiple_of(y * 256 + zz * 64 + xx * 16, 16)


def weight_copies(head, pieces, w_vmem, sem, idx):
    for part in range(4):
        for item in range(8):
            row = piece_rows(head, part, idx, item)
            yield pltpu.make_async_copy(
                pieces[head * 4 + part].at[item],
                w_vmem.at[head, :, pl.ds(row, 16), :],
                sem.at[head],
            )


def load_weights(pieces, w_vmem, sem, idx, head_now):
    @pl.when(head_now == 0)
    def _():
        for head in range(2):
            for copy in weight_copies(head, pieces, w_vmem, sem, idx):
                copy.start()

    for head in range(2):

        @pl.when(head_now == head)
        def _(head=head):
            pltpu.make_async_copy(w_vmem.at[head], w_vmem.at[head], sem.at[head]).wait()


def grads_kernel(s_ref, *refs):
    pieces = refs[:8]
    k_own, v_own, k_rec, v_rec, r_ref = refs[8:13]
    outs = refs[13:21]
    w_vmem, sums, sem = refs[21:]
    head = pl.program_id(0)
    idx = (s_ref[1], s_ref[2], s_ref[3])
    load_weights(pieces, w_vmem, sem, idx, head)
    gate, up, down = w_vmem[head, 0], w_vmem[head, 1], w_vmem[head, 2]
    for j, (k_ref, v_ref) in enumerate(((k_own, v_own), (k_rec, v_rec))):
        k = k_ref[0]
        rate = r_ref[0, j]
        target = (-(rate * v_ref[0].astype(f32))).astype(bf16)
        g = dot(k, gate, NN)
        u = dot(k, up, NN)
        back = dot(target, down, NT)
        s = jax.nn.sigmoid(g)
        silu = g * s
        active = (silu * u).astype(bf16)
        d_gate = (back * u * s * (1.0 + g * (1.0 - s))).astype(bf16)
        d_up = (back * silu).astype(bf16)
        parts = (dot(k, d_gate, TN), dot(k, d_up, TN), dot(active, target, TN))
        for m in range(3):
            if j == 0:
                sums[m] = parts[m]
            else:
                sums[m] += parts[m]
    yh, z, x = idx
    for kind in range(2):

        @pl.when(head == kind)
        def _(kind=kind):
            for part in range(4):
                for item in range(8):
                    a, k = item % 2, item // 2
                    y = lax.rem(yh + a, 2)
                    zz = lax.rem(z + 4 - (k if kind == 0 else part), 4)
                    xx = lax.rem(x + 4 - (part if kind == 0 else k), 4)
                    row = pl.multiple_of(y * 256 + zz * 64 + xx * 16, 16)
                    for m in range(3):
                        outs[kind * 4 + part][item, m] = sums[m, pl.ds(row, 16), :].astype(bf16)


def own_spec(c):
    return pl.BlockSpec((1, TOK, DH), lambda h, s: (c, 0, s[0] * 2 + h))


def rec_spec(c):
    return pl.BlockSpec((1, TOK, DH), lambda h, s: (c, 0, h))


ANY = pl.BlockSpec(memory_space=pl.ANY)


def compute_grads(scal, pieces, k, v, k_rec, v_rec, rates):
    whole = pl.BlockSpec((8, 3, 16, DH), lambda h, s: (0, 0, 0, 0))
    return pl.pallas_call(
        grads_kernel,
        name="fast_grads",
        out_shape=[jax.ShapeDtypeStruct((8, 3, 16, DH), bf16)] * 8,
        grid_spec=pltpu.PrefetchScalarGridSpec(
            num_scalar_prefetch=1,
            grid=(2,),
            in_specs=[ANY] * 8
            + [own_spec(0), own_spec(0), rec_spec(0), rec_spec(0)]
            + [pl.BlockSpec((1, 2, TOK, 1), lambda h, s: (h, 0, 0, 0))],
            out_specs=[whole] * 8,
            scratch_shapes=[
                pltpu.VMEM((2, 3, DH, DH), bf16),
                pltpu.VMEM((3, DH, DH), f32),
                pltpu.SemaphoreType.DMA((2,)),
            ],
        ),
        compiler_params=cparams(),
    )(scal, *pieces, k, v, k_rec, v_rec, rates)


def apply_kernel(s_ref, *refs):
    pieces = refs[:8]
    q_own, q_rec = refs[8:10]
    out_ref, pow_ref = refs[10:12]
    w_vmem, sem = refs[12:]
    head = pl.program_id(0)
    idx = (s_ref[1], s_ref[2], s_ref[3])
    load_weights(pieces, w_vmem, sem, idx, head)
    gate, up, down = w_vmem[head, 0], w_vmem[head, 1], w_vmem[head, 2]
    for j, q_ref in enumerate((q_own, q_rec)):
        q = q_ref[0]
        g = dot(q, gate, NN)
        u = dot(q, up, NN)
        active = (g * jax.nn.sigmoid(g) * u).astype(bf16)
        out = dot(active, down, NN)
        out_ref[j] = out
        power = jnp.sum(out * out, axis=-1, keepdims=True)
        power = jnp.transpose(jnp.broadcast_to(power, (TOK, 128)))[:8]

        @pl.when(head == 0)
        def _(j=j, power=power):
            pow_ref[j] = power

        @pl.when(head == 1)
        def _(j=j, power=power):
            pow_ref[j] += power


def fast_apply(c, scal, pieces, q, q_rec):
    return pl.pallas_call(
        apply_kernel,
        name="fast_apply",
        out_shape=[
            jax.ShapeDtypeStruct((2, TOK, 2 * DH), f32),
            jax.ShapeDtypeStruct((2, 8, TOK), f32),
        ],
        grid_spec=pltpu.PrefetchScalarGridSpec(
            num_scalar_prefetch=1,
            grid=(2,),
            in_specs=[ANY] * 8 + [own_spec(c), rec_spec(c)],
            out_specs=[
                pl.BlockSpec((2, TOK, DH), lambda h, s: (0, 0, h)),
                pl.BlockSpec((2, 8, TOK), lambda h, s: (0, 0, 0)),
            ],
            scratch_shapes=[
                pltpu.VMEM((2, 3, DH, DH), bf16),
                pltpu.SemaphoreType.DMA((2,)),
            ],
        ),
        compiler_params=cparams(),
    )(scal, *pieces, q, q_rec)


def attention_kernel(c, s_ref, qo, qr, k0, ka, kb, k2, v0, va, vb, v2, out_ref):
    block = pl.program_id(1)
    row = lax.broadcasted_iota(jnp.int32, (TOK, TOK), 0)
    col = lax.broadcasted_iota(jnp.int32, (TOK, TOK), 1)
    q = jnp.where(s_ref[0] == block, qo[0], qr[0])
    keys = (k0[0], jnp.where(block == 0, ka[0], kb[0]), k2[0])
    values = (v0[0], jnp.where(block == 0, va[0], vb[0]), v2[0])
    scores = [dot(q, k, NT) * SCALE for k in keys]
    if c == 0:
        low = jnp.where(s_ref[4] == 1, TOK, row)
        scores[1] = jnp.where(col >= jnp.where((s_ref[4] == 1) & (block == 0), TOK, 0), scores[1], MASKED)
    else:
        low = row
    scores[0] = jnp.where(col > low, scores[0], MASKED)
    scores[2] = jnp.where(col <= row, scores[2], MASKED)
    peak = jnp.max(jnp.maximum(jnp.maximum(scores[0], scores[1]), scores[2]), axis=-1, keepdims=True)
    weights = [jnp.exp(s - peak) for s in scores]
    total = jnp.sum(weights[0] + weights[1] + weights[2], axis=-1, keepdims=True)
    inv = 1.0 / total
    out_ref[0] = sum(
        dot((w * inv).astype(bf16), v, NN) for w, v in zip(weights, values)
    )


def attention(c, scal, q, q_rec, before, mine):
    def block(at):
        return pl.BlockSpec((1, TOK, DH), lambda h, b, s: (at(b), 0, h))

    return pl.pallas_call(
        functools.partial(attention_kernel, c),
        name="window_attention",
        out_shape=jax.ShapeDtypeStruct((2, TOK, 2 * DH), f32),
        grid_spec=pltpu.PrefetchScalarGridSpec(
            num_scalar_prefetch=1,
            grid=(2, 2),
            in_specs=[
                pl.BlockSpec((1, TOK, DH), lambda h, b, s: (c, 0, s[0] * 2 + h)),
                pl.BlockSpec((1, TOK, DH), lambda h, b, s: (c, 0, h)),
            ]
            + [
                block(at)
                for o in (0, 2)
                for at in (lambda b, o=o: o + b, lambda b, o=o: o + 1, lambda b, o=o: o, lambda b, o=o: o + b)
            ],
            out_specs=pl.BlockSpec(
                (1, TOK, DH), lambda h, b, s: (jnp.where(s[0] == b, 0, 1), 0, h)
            ),
        ),
        compiler_params=cparams(),
    )(scal, q, q_rec, *(before, before, mine, mine) * 2)


def finish_kernel(s_ref, fast_ref, p0, p1, p2, p3, gain_ref, att_ref, *refs):
    own_ref, rec_ref = refs[-2:]
    total = p0[...] + p1[...] + p2[...] + p3[...]
    rs = lax.rsqrt(total * (1.0 / 4096.0) + NORM_EPS)
    for j in range(2):
        col = jnp.transpose(rs[j])[:, :1]
        out = (fast_ref[j] * gain_ref[...] * col + att_ref[j]).astype(bf16)
        if j == 0:
            own_ref[0] = out
        else:
            rec_ref[...] = out


ROWS = 128


def finish(c, scal, fast, powers, gain, att, layer):
    both = pl.BlockSpec((2, ROWS, 2 * DH), lambda i, s: (0, i, 0))
    power = pl.BlockSpec((2, 8, ROWS), lambda i, s: (0, 0, i))
    more = [] if layer is None else [layer]
    return pl.pallas_call(
        finish_kernel,
        name="finish",
        out_shape=[
            jax.ShapeDtypeStruct((2, TOK, 4 * DH), bf16),
            jax.ShapeDtypeStruct((TOK, 2 * DH), bf16),
        ],
        grid_spec=pltpu.PrefetchScalarGridSpec(
            num_scalar_prefetch=1,
            grid=(TOK // ROWS,),
            in_specs=[both] + [power] * 4 + [pl.BlockSpec((1, 2 * DH), lambda i, s: (0, 0)), both]
            + [ANY] * len(more),
            out_specs=[
                pl.BlockSpec((1, ROWS, 2 * DH), lambda i, s: (c, i, s[0])),
                pl.BlockSpec((ROWS, 2 * DH), lambda i, s: (i, 0)),
            ],
        ),
        input_output_aliases={8: 0} if more else {},
        compiler_params=cparams(),
    )(scal, fast, *powers, gain, att, *more)


def place_kernel(c, s_ref, arrived_ref, layer_ref, out_ref, sem):
    column = pl.multiple_of((1 - s_ref[0]) * 2 * DH, 2 * DH)
    copy = pltpu.make_async_copy(arrived_ref, out_ref.at[c, :, pl.ds(column, 2 * DH)], sem)
    copy.start()
    copy.wait()


def place(c, scal, arrived, layer):
    return pl.pallas_call(
        functools.partial(place_kernel, c),
        name="place",
        out_shape=jax.ShapeDtypeStruct((2, TOK, 4 * DH), bf16),
        grid_spec=pltpu.PrefetchScalarGridSpec(
            num_scalar_prefetch=1,
            grid=(1,),
            in_specs=[ANY, ANY],
            out_specs=ANY,
            scratch_shapes=[pltpu.SemaphoreType.DMA(())],
        ),
        input_output_aliases={2: 0},
        compiler_params=cparams(),
    )(scal, arrived, layer)


def gather_direct(both):
    out = []
    for head, (first, last) in enumerate((("z", "x"), ("x", "z"))):
        v = both[head]
        v = jnp.concatenate([v] + [shift(v, first, -k) for k in range(1, 4)], axis=0)
        out.append([v] + [shift(v, last, -k) for k in range(1, 4)])
    return out[0] + out[1]


def gather_rings(both):
    axes = (("z", "x"), ("x", "z"))
    now = [both[h] for h in range(2)]
    held = [[n] for n in now]
    for _ in range(3):
        for h in range(2):
            now[h] = shift(now[h], axes[h][0], -1)
            held[h].append(now[h])
    now = [jnp.concatenate(held[h], axis=0) for h in range(2)]
    out = [[n] for n in now]
    for _ in range(3):
        for h in range(2):
            now[h] = shift(now[h], axes[h][1], -1)
            out[h].append(now[h])
    return out[0] + out[1]


def scatter_rings(slabs):
    axes = (("x", "z"), ("z", "x"))
    now = [slabs[3], slabs[7]]
    for k in (2, 1, 0):
        for h in range(2):
            got = shift(now[h], axes[h][0], -1)
            total = got.astype(f32) + slabs[h * 4 + k].astype(f32)
            now[h] = total.astype(bf16) if k else total
    parts = now
    now = [p[6:8].astype(bf16) for p in parts]
    for k in (2, 1, 0):
        for h in range(2):
            got = shift(now[h], axes[h][1], -1)
            now[h] = (got.astype(f32) + parts[h][2 * k : 2 * k + 2]).astype(bf16)
    return jnp.stack(now)


def power_parts(power):
    flat = ("heads", "core")
    swapped = power[::-1]
    return [
        lax.ppermute(swapped, flat, [(0, 1), (1, 0), (2, 3), (3, 2)]),
        lax.ppermute(power, flat, [(0, 2), (2, 0), (1, 3), (3, 1)]),
        lax.ppermute(swapped, flat, [(0, 3), (3, 0), (1, 2), (2, 1)]),
    ]


def on_device(queries, key_rows, value_rows, step_rates, w_gate, w_up, w_down, out_gain):
    core = lax.axis_index("core")
    yh, z, x = lax.axis_index("yh"), lax.axis_index("z"), lax.axis_index("x")
    chip = (yh * 4 + z) * 4 + x
    first = (chip == 0).astype(jnp.int32)
    scal = jnp.stack([core, yh, z, x, first]).astype(jnp.int32)

    masters = jnp.stack([w_gate, w_up, w_down], axis=1)
    mine = lax.dynamic_slice_in_dim(masters, core * 2, 2, 0)
    theirs = lax.dynamic_slice_in_dim(masters, (1 - core) * 2, 2, 0)
    got = shift(theirs, "core", 1)
    m16 = jnp.where(
        core == 0,
        jnp.concatenate([mine, got], axis=2),
        jnp.concatenate([got, mine], axis=2),
    )
    m16_other = shift(m16, "yh", 1)
    m16_other, key_rows, value_rows, queries, step_rates = lax.optimization_barrier(
        (m16_other, key_rows, value_rows, queries, step_rates)
    )
    both = jnp.stack([m16, m16_other], axis=1)
    pieces = gather_direct(both.astype(bf16))

    def split_in(a):
        keep = lax.dynamic_slice_in_dim(a, core * 1024, 1024, 2)
        give = lax.dynamic_slice_in_dim(a, (1 - core) * 1024, 1024, 2)
        return keep, shift(give, "core", 1)

    k_own, k_rec = split_in(key_rows)
    v_own, v_rec = split_in(value_rows)
    q_rec = split_in(queries)[1]
    rates = step_rates[:, 0, :]
    r_own = lax.dynamic_slice_in_dim(rates, core * 2, 2, 0)
    r_rec = shift(lax.dynamic_slice_in_dim(rates, (1 - core) * 2, 2, 0), "core", 1)
    rates = jnp.stack([r_own, r_rec], axis=1)[..., None]

    chips = ("yh", "z", "x")
    row = [(i, (i + 1) % 32) for i in range(32) if i % 16 != 15]
    turn = [(15, 16), (31, 0)]
    pair = [
        jnp.where(
            core == 0,
            jnp.stack([k_own[c], k_rec[c], v_own[c], v_rec[c]]),
            jnp.stack([k_rec[c], k_own[c], v_rec[c], v_own[c]]),
        )
        for c in range(2)
    ]
    pair[0], pair[1], *pieces = lax.optimization_barrier((pair[0], pair[1], *pieces))
    halo = []
    for c in range(2):
        halo.append(lax.ppermute(pair[c], chips, row))
    turned0 = lax.ppermute(pair[0], chips, turn)

    slabs = compute_grads(scal, pieces, key_rows, value_rows, k_rec, v_rec, rates)
    fast0, pow0 = fast_apply(0, scal, pieces, queries, q_rec)
    half_sums = scatter_rings(slabs)
    half_sums, pow0 = lax.optimization_barrier((half_sums, pow0))
    other_sums = shift(half_sums, "yh", 1)
    powers0 = [pow0] + power_parts(pow0)
    grad_both = half_sums.astype(f32) + other_sums[:, ::-1].astype(f32)
    grad_both, pair1, *powers0 = lax.optimization_barrier((grad_both, pair[1], *powers0))
    new_both = both - grad_both
    new16 = new_both[:, 0]
    pieces2 = gather_rings(new_both.astype(bf16))
    turned1 = lax.ppermute(pair1, chips, turn[:1])
    own_rows = lax.dynamic_slice_in_dim(new16, core * 8, 8, 2)
    their_rows = shift(lax.dynamic_slice_in_dim(new16, (1 - core) * 8, 8, 2), "core", 1)
    new_all = jnp.where(
        core == 0,
        jnp.concatenate([own_rows, their_rows], axis=0),
        jnp.concatenate([their_rows, own_rows], axis=0),
    )

    gain = lax.dynamic_slice_in_dim(out_gain, core * 1024, 1024, 0)[None]
    at_turn = (z == 0) & (x == 0)

    def attend(c, before, mine):
        return attention(c, scal, queries, q_rec, before, mine)

    before0 = jnp.where(at_turn, turned0, halo[0])
    att0 = attend(0, before0, pair[0])
    fast1, pow1 = fast_apply(1, scal, pieces2, queries, q_rec)
    powers1 = [pow1] + power_parts(pow1)
    fast1, turned1, halo1, earlier0 = lax.optimization_barrier(
        (fast1, turned1, halo[1], before0)
    )
    before1 = jnp.where(chip == 0, earlier0, jnp.where(at_turn, turned1, halo1))
    att1 = attend(1, before1, pair[1])

    def complete(c, fast, powers, attended, layer):
        layer, out_rec = finish(c, scal, fast, powers, gain, attended, layer)
        arrived = shift(out_rec, "core", 1)
        return place(c, scal, arrived, layer)

    layer_out = complete(0, fast0, powers0, att0, None)
    layer_out = complete(1, fast1, powers1, att1, layer_out)
    return layer_out, new_all[:, 0], new_all[:, 1], new_all[:, 2]


def solution(mesh):
    fine = Mesh(mesh.devices.reshape(2, 2, 4, 4, 2), ("heads",) + SEQ)
    rows = P(None, SEQ, "heads")
    weight = P("heads", SEQ, None)
    return jax.shard_map(
        on_device,
        mesh=fine,
        in_specs=(rows, rows, rows, P("heads", None, SEQ), weight, weight, weight, P("heads")),
        out_specs=(rows, weight, weight, weight),
        check_vma=False,
    )
```

```python
import functools

import jax
import jax.numpy as jnp
from jax import lax
from jax.experimental import pallas as pl
from jax.experimental.pallas import tpu as pltpu
from jax.sharding import Mesh, PartitionSpec as P

NORM_EPS = 1e-05
MASKED = -1e30
SIZES = {"heads": 2, "yh": 2, "z": 4, "x": 4, "core": 2}
SEQ = ("yh", "z", "x", "core")
TOK = 384
DH = 512
SCALE = DH ** -0.5

f32 = jnp.float32
bf16 = jnp.bfloat16


def shift(value, axis, steps):
    count = SIZES[axis]
    return lax.ppermute(value, axis, [(i, (i + steps) % count) for i in range(count)])


def dot(a, b, dims):
    return lax.dot_general(a, b, (dims, ((), ())), preferred_element_type=f32)


NN = ((1,), (0,))
NT = ((1,), (1,))
TN = ((0,), (0,))


def cparams(**kw):
    return pltpu.CompilerParams(vmem_limit_bytes=56 * 1024 * 1024, **kw)


def piece_rows(kind, part, idx, item):
    yh, z, x = idx
    a, k = item % 2, item // 2
    y = lax.rem(yh + a, 2)
    if kind == 0:
        zz, xx = lax.rem(z + k, 4), lax.rem(x + part, 4)
    else:
        zz, xx = lax.rem(z + part, 4), lax.rem(x + k, 4)
    return pl.multiple_of(y * 256 + zz * 64 + xx * 16, 16)


def weight_copies(head, pieces, w_vmem, sem, idx):
    for part in range(4):
        for item in range(8):
            row = piece_rows(head, part, idx, item)
            yield pltpu.make_async_copy(
                pieces[head * 4 + part].at[item],
                w_vmem.at[head, :, pl.ds(row, 16), :],
                sem.at[head],
            )


def load_weights(pieces, w_vmem, sem, idx, head_now):
    @pl.when(head_now == 0)
    def _():
        for head in range(2):
            for copy in weight_copies(head, pieces, w_vmem, sem, idx):
                copy.start()

    for head in range(2):

        @pl.when(head_now == head)
        def _(head=head):
            pltpu.make_async_copy(w_vmem.at[head], w_vmem.at[head], sem.at[head]).wait()


def grads_kernel(s_ref, *refs):
    pieces = refs[:8]
    k_own, v_own, k_rec, v_rec, r_ref = refs[8:13]
    outs = refs[13:21]
    w_vmem, sums, sem = refs[21:]
    head = pl.program_id(0)
    idx = (s_ref[1], s_ref[2], s_ref[3])
    load_weights(pieces, w_vmem, sem, idx, head)
    gate, up, down = w_vmem[head, 0], w_vmem[head, 1], w_vmem[head, 2]
    for j, (k_ref, v_ref) in enumerate(((k_own, v_own), (k_rec, v_rec))):
        k = k_ref[0]
        rate = r_ref[0, j]
        target = (-(rate * v_ref[0].astype(f32))).astype(bf16)
        g = dot(k, gate, NN)
        u = dot(k, up, NN)
        back = dot(target, down, NT)
        s = jax.nn.sigmoid(g)
        silu = g * s
        active = (silu * u).astype(bf16)
        d_gate = (back * u * s * (1.0 + g * (1.0 - s))).astype(bf16)
        d_up = (back * silu).astype(bf16)
        parts = (dot(k, d_gate, TN), dot(k, d_up, TN), dot(active, target, TN))
        for m in range(3):
            if j == 0:
                sums[m] = parts[m]
            else:
                sums[m] += parts[m]
    yh, z, x = idx
    for kind in range(2):

        @pl.when(head == kind)
        def _(kind=kind):
            for part in range(4):
                for item in range(8):
                    a, k = item % 2, item // 2
                    y = lax.rem(yh + a, 2)
                    zz = lax.rem(z + 4 - (k if kind == 0 else part), 4)
                    xx = lax.rem(x + 4 - (part if kind == 0 else k), 4)
                    row = pl.multiple_of(y * 256 + zz * 64 + xx * 16, 16)
                    for m in range(3):
                        outs[kind * 4 + part][item, m] = sums[m, pl.ds(row, 16), :].astype(bf16)


def own_spec(c):
    return pl.BlockSpec((1, TOK, DH), lambda h, s: (c, 0, s[0] * 2 + h))


def rec_spec(c):
    return pl.BlockSpec((1, TOK, DH), lambda h, s: (c, 0, h))


ANY = pl.BlockSpec(memory_space=pl.ANY)


def compute_grads(scal, pieces, k, v, k_rec, v_rec, rates):
    whole = pl.BlockSpec((8, 3, 16, DH), lambda h, s: (0, 0, 0, 0))
    return pl.pallas_call(
        grads_kernel,
        name="fast_grads",
        out_shape=[jax.ShapeDtypeStruct((8, 3, 16, DH), bf16)] * 8,
        grid_spec=pltpu.PrefetchScalarGridSpec(
            num_scalar_prefetch=1,
            grid=(2,),
            in_specs=[ANY] * 8
            + [own_spec(0), own_spec(0), rec_spec(0), rec_spec(0)]
            + [pl.BlockSpec((1, 2, TOK, 1), lambda h, s: (h, 0, 0, 0))],
            out_specs=[whole] * 8,
            scratch_shapes=[
                pltpu.VMEM((2, 3, DH, DH), bf16),
                pltpu.VMEM((3, DH, DH), f32),
                pltpu.SemaphoreType.DMA((2,)),
            ],
        ),
        compiler_params=cparams(),
    )(scal, *pieces, k, v, k_rec, v_rec, rates)


def apply_kernel(s_ref, *refs):
    pieces = refs[:8]
    q_own, q_rec = refs[8:10]
    out_ref, pow_ref = refs[10:12]
    w_vmem, sem = refs[12:]
    head = pl.program_id(0)
    idx = (s_ref[1], s_ref[2], s_ref[3])
    load_weights(pieces, w_vmem, sem, idx, head)
    gate, up, down = w_vmem[head, 0], w_vmem[head, 1], w_vmem[head, 2]
    core = s_ref[0]
    for j, q_ref in enumerate((q_own, q_rec)):
        block = core if j == 0 else 1 - core
        q = q_ref[0]
        g = dot(q, gate, NN)
        u = dot(q, up, NN)
        active = (g * jax.nn.sigmoid(g) * u).astype(bf16)
        out = dot(active, down, NN)
        out_ref[j] = out
        power = jnp.sum(out * out, axis=-1, keepdims=True)
        power = jnp.transpose(jnp.broadcast_to(power, (TOK, 128)))[:8]

        @pl.when(head == 0)
        def _(block=block, power=power):
            pow_ref[block] = power

        @pl.when(head == 1)
        def _(block=block, power=power):
            pow_ref[block] += power


def fast_apply(c, scal, pieces, q, q_rec):
    return pl.pallas_call(
        apply_kernel,
        name="fast_apply",
        out_shape=[
            jax.ShapeDtypeStruct((2, TOK, 2 * DH), f32),
            jax.ShapeDtypeStruct((2, 8, TOK), f32),
        ],
        grid_spec=pltpu.PrefetchScalarGridSpec(
            num_scalar_prefetch=1,
            grid=(2,),
            in_specs=[ANY] * 8 + [own_spec(c), rec_spec(c)],
            out_specs=[
                pl.BlockSpec((2, TOK, DH), lambda h, s: (0, 0, h)),
                pl.BlockSpec((2, 8, TOK), lambda h, s: (0, 0, 0)),
            ],
            scratch_shapes=[
                pltpu.VMEM((2, 3, DH, DH), bf16),
                pltpu.SemaphoreType.DMA((2,)),
            ],
        ),
        compiler_params=cparams(),
    )(scal, *pieces, q, q_rec)


def attention_kernel(c, s_ref, qo, qr, k0, ka, kb, k2, v0, va, vb, v2, out_ref):
    block = pl.program_id(1)
    row = lax.broadcasted_iota(jnp.int32, (TOK, TOK), 0)
    col = lax.broadcasted_iota(jnp.int32, (TOK, TOK), 1)
    q = jnp.where(s_ref[0] == block, qo[0], qr[0])
    keys = (k0[0], jnp.where(block == 0, ka[0], kb[0]), k2[0])
    values = (v0[0], jnp.where(block == 0, va[0], vb[0]), v2[0])
    scores = [dot(q, k, NT) * SCALE for k in keys]
    if c == 0:
        low = jnp.where(s_ref[4] == 1, TOK, row)
        scores[1] = jnp.where(col >= jnp.where((s_ref[4] == 1) & (block == 0), TOK, 0), scores[1], MASKED)
    else:
        low = row
    scores[0] = jnp.where(col > low, scores[0], MASKED)
    scores[2] = jnp.where(col <= row, scores[2], MASKED)
    peak = jnp.max(jnp.maximum(jnp.maximum(scores[0], scores[1]), scores[2]), axis=-1, keepdims=True)
    weights = [jnp.exp(s - peak) for s in scores]
    total = jnp.sum(weights[0] + weights[1] + weights[2], axis=-1, keepdims=True)
    inv = 1.0 / total
    out_ref[0] = sum(
        dot((w * inv).astype(bf16), v, NN) for w, v in zip(weights, values)
    )


def attention(c, scal, q, q_rec, before, mine):
    def block(at):
        return pl.BlockSpec((1, TOK, DH), lambda h, b, s: (at(b), 0, h))

    return pl.pallas_call(
        functools.partial(attention_kernel, c),
        name="window_attention",
        out_shape=jax.ShapeDtypeStruct((2, TOK, 2 * DH), f32),
        grid_spec=pltpu.PrefetchScalarGridSpec(
            num_scalar_prefetch=1,
            grid=(2, 2),
            in_specs=[
                pl.BlockSpec((1, TOK, DH), lambda h, b, s: (c, 0, s[0] * 2 + h)),
                pl.BlockSpec((1, TOK, DH), lambda h, b, s: (c, 0, h)),
            ]
            + [
                block(at)
                for o in (0, 2)
                for at in (lambda b, o=o: o + b, lambda b, o=o: o + 1, lambda b, o=o: o, lambda b, o=o: o + b)
            ],
            out_specs=pl.BlockSpec(
                (1, TOK, DH), lambda h, b, s: (jnp.where(s[0] == b, 0, 1), 0, h)
            ),
        ),
        compiler_params=cparams(),
    )(scal, q, q_rec, *(before, before, mine, mine) * 2)


def finish_kernel(count, s_ref, fast_ref, *refs):
    powers, (gain_ref, att_ref), out_ref = refs[:count], refs[count : count + 2], refs[-1]
    total = sum(p[0] for p in powers[1:]) + powers[0][0]
    rs = lax.rsqrt(total * (1.0 / 4096.0) + NORM_EPS)
    col = jnp.transpose(rs)[:, :1]
    out = (fast_ref[0] * gain_ref[...] * col + att_ref[0]).astype(bf16)
    out_ref[...] = out.reshape(out_ref.shape)


ROWS = 128


def finish(c, j, scal, fast, powers, gain, att, layer=None):
    one = pl.BlockSpec((1, ROWS, 2 * DH), lambda i, s: (j, i, 0))
    block = (lambda s: s[0]) if j == 0 else (lambda s: 1 - s[0])
    power = pl.BlockSpec((1, 8, ROWS), lambda i, s: (block(s), 0, i))
    more = [] if layer is None else [layer]
    if j == 0:
        shape = (2, TOK, 4 * DH)
        spec = pl.BlockSpec((1, ROWS, 2 * DH), lambda i, s: (c, i, s[0]))
    else:
        shape = (TOK, 2 * DH)
        spec = pl.BlockSpec((ROWS, 2 * DH), lambda i, s: (i, 0))
    count = len(powers)
    return pl.pallas_call(
        functools.partial(finish_kernel, count),
        name="finish",
        out_shape=jax.ShapeDtypeStruct(shape, bf16),
        grid_spec=pltpu.PrefetchScalarGridSpec(
            num_scalar_prefetch=1,
            grid=(TOK // ROWS,),
            in_specs=[one] + [power] * count
            + [pl.BlockSpec((1, 2 * DH), lambda i, s: (0, 0)), one]
            + [ANY] * len(more),
            out_specs=spec,
        ),
        input_output_aliases={count + 4: 0} if more else {},
        compiler_params=cparams(),
    )(scal, fast, *powers, gain, att, *more)


def place_kernel(s_ref, arrived_ref, layer_ref, out_ref):
    out_ref[0] = arrived_ref[...]


def place(c, scal, arrived, layer):
    return pl.pallas_call(
        place_kernel,
        name="place",
        out_shape=jax.ShapeDtypeStruct((2, TOK, 4 * DH), bf16),
        grid_spec=pltpu.PrefetchScalarGridSpec(
            num_scalar_prefetch=1,
            grid=(3,),
            in_specs=[pl.BlockSpec((TOK // 3, 2 * DH), lambda i, s: (i, 0)), ANY],
            out_specs=pl.BlockSpec((1, TOK // 3, 2 * DH), lambda i, s: (c, i, 1 - s[0])),
        ),
        input_output_aliases={2: 0},
        compiler_params=cparams(),
    )(scal, arrived, layer)


def gather_direct(both):
    out = []
    for head, (first, last) in enumerate((("z", "x"), ("x", "z"))):
        v = both[head]
        v = jnp.concatenate([v] + [shift(v, first, -k) for k in range(1, 4)], axis=0)
        out.append([v] + [shift(v, last, -k) for k in range(1, 4)])
    return out[0] + out[1]


def gather_rings(both):
    axes = (("z", "x"), ("x", "z"))
    now = [both[h] for h in range(2)]
    held = [[n] for n in now]
    for _ in range(3):
        for h in range(2):
            now[h] = shift(now[h], axes[h][0], -1)
            held[h].append(now[h])
    now = [jnp.concatenate(held[h], axis=0) for h in range(2)]
    out = [[n] for n in now]
    for _ in range(3):
        for h in range(2):
            now[h] = shift(now[h], axes[h][1], -1)
            out[h].append(now[h])
    return out[0] + out[1]


def scatter_rings(slabs):
    axes = (("x", "z"), ("z", "x"))
    now = [slabs[3], slabs[7]]
    for k in (2, 1, 0):
        for h in range(2):
            got = shift(now[h], axes[h][0], -1)
            total = got.astype(f32) + slabs[h * 4 + k].astype(f32)
            now[h] = total.astype(bf16) if k else total
    parts = now
    now = [p[6:8].astype(bf16) for p in parts]
    for k in (2, 1, 0):
        for h in range(2):
            got = shift(now[h], axes[h][1], -1)
            now[h] = (got.astype(f32) + parts[h][2 * k : 2 * k + 2]).astype(bf16)
    return jnp.stack(now)


CORES = [(0, 1), (1, 0), (2, 3), (3, 2)]
HALVES = [(0, 2), (2, 0), (1, 3), (3, 1)]
ACROSS = [(0, 3), (3, 0), (1, 2), (2, 1)]


def with_parts(power, pairs):
    return [power] + [lax.ppermute(power, ("heads", "core"), p) for p in pairs]


def on_device(queries, key_rows, value_rows, step_rates, w_gate, w_up, w_down, out_gain):
    core = lax.axis_index("core")
    yh, z, x = lax.axis_index("yh"), lax.axis_index("z"), lax.axis_index("x")
    chip = (yh * 4 + z) * 4 + x
    first = (chip == 0).astype(jnp.int32)
    scal = jnp.stack([core, yh, z, x, first]).astype(jnp.int32)

    masters = jnp.stack([w_gate, w_up, w_down], axis=1)
    mine = lax.dynamic_slice_in_dim(masters, core * 2, 2, 0)
    theirs = lax.dynamic_slice_in_dim(masters, (1 - core) * 2, 2, 0)
    got = shift(theirs, "core", 1)
    m16 = jnp.where(
        core == 0,
        jnp.concatenate([mine, got], axis=2),
        jnp.concatenate([got, mine], axis=2),
    )
    m16_other = shift(m16, "yh", 1)
    m16_other, key_rows, value_rows, queries, step_rates = lax.optimization_barrier(
        (m16_other, key_rows, value_rows, queries, step_rates)
    )
    both = jnp.stack([m16, m16_other], axis=1)
    pieces = gather_direct(both.astype(bf16))

    def split_in(a):
        keep = lax.dynamic_slice_in_dim(a, core * 1024, 1024, 2)
        give = lax.dynamic_slice_in_dim(a, (1 - core) * 1024, 1024, 2)
        return keep, shift(give, "core", 1)

    k_own, k_rec = split_in(key_rows)
    v_own, v_rec = split_in(value_rows)
    q_rec = split_in(queries)[1]
    rates = step_rates[:, 0, :]
    r_own = lax.dynamic_slice_in_dim(rates, core * 2, 2, 0)
    r_rec = shift(lax.dynamic_slice_in_dim(rates, (1 - core) * 2, 2, 0), "core", 1)
    rates = jnp.stack([r_own, r_rec], axis=1)[..., None]

    chips = ("yh", "z", "x")
    row = [(i, (i + 1) % 32) for i in range(32)]
    pair = [
        jnp.where(
            core == 0,
            jnp.stack([k_own[c], k_rec[c], v_own[c], v_rec[c]]),
            jnp.stack([k_rec[c], k_own[c], v_rec[c], v_own[c]]),
        )
        for c in range(2)
    ]
    pair[0], pair[1], *pieces = lax.optimization_barrier((pair[0], pair[1], *pieces))
    halo0 = lax.ppermute(pair[0], chips, row)
    halo1 = lax.ppermute(pair[1], chips, [p for p in row if p[0] % 16 != 15])

    slabs = compute_grads(scal, pieces, key_rows, value_rows, k_rec, v_rec, rates)
    fast0, pow0 = fast_apply(0, scal, pieces, queries, q_rec)
    half_sums = scatter_rings(slabs)
    pow0 = sum(with_parts(pow0, (CORES,)))
    half_sums, pow0 = lax.optimization_barrier((half_sums, pow0))
    other_sums = shift(half_sums, "yh", 1)
    powers0 = with_parts(pow0, (HALVES,))
    grad_both = half_sums.astype(f32) + other_sums[:, ::-1].astype(f32)
    grad_both, pair1, *powers0 = lax.optimization_barrier((grad_both, pair[1], *powers0))
    new_both = both - grad_both
    new16 = new_both[:, 0]
    pieces2 = gather_rings(new_both.astype(bf16))
    turned1 = lax.ppermute(pair1, chips, [(15, 16)])
    own_rows = lax.dynamic_slice_in_dim(new16, core * 8, 8, 2)
    their_rows = shift(lax.dynamic_slice_in_dim(new16, (1 - core) * 8, 8, 2), "core", 1)
    new_all = jnp.where(
        core == 0,
        jnp.concatenate([own_rows, their_rows], axis=0),
        jnp.concatenate([their_rows, own_rows], axis=0),
    )

    gain = lax.dynamic_slice_in_dim(out_gain, core * 1024, 1024, 0)[None]

    def attend(c, before, mine):
        return attention(c, scal, queries, q_rec, before, mine)

    def complete(c, fast, powers, attended, layer):
        out_rec = finish(c, 1, scal, fast, powers, gain, attended)
        arrived = shift(out_rec, "core", 1)
        layer = finish(c, 0, scal, fast, powers, gain, attended, layer)
        return place(c, scal, arrived, layer)

    layer_out = complete(0, fast0, powers0, attend(0, halo0, pair[0]), None)
    before1 = jnp.where(chip == 0, halo0, jnp.where((z == 0) & (x == 0), turned1, halo1))
    att1 = attend(1, before1, pair[1])
    fast1, pow1 = fast_apply(1, scal, pieces2, queries, q_rec)
    powers1 = with_parts(pow1, (CORES, HALVES, ACROSS))
    layer_out = complete(1, fast1, powers1, att1, layer_out)
    return layer_out, new_all[:, 0], new_all[:, 1], new_all[:, 2]


def solution(mesh):
    fine = Mesh(mesh.devices.reshape(2, 2, 4, 4, 2), ("heads",) + SEQ)
    rows = P(None, SEQ, "heads")
    weight = P("heads", SEQ, None)
    return jax.shard_map(
        on_device,
        mesh=fine,
        in_specs=(rows, rows, rows, P("heads", None, SEQ), weight, weight, weight, P("heads")),
        out_specs=(rows, weight, weight, weight),
        check_vma=False,
    )
```

```python
import functools

import jax
import jax.numpy as jnp
from jax import lax
from jax.experimental import pallas as pl
from jax.experimental.pallas import tpu as pltpu
from jax.sharding import Mesh, PartitionSpec as P

NORM_EPS = 1e-05
MASKED = -1e30
SIZES = {"heads": 2, "yh": 2, "z": 4, "x": 4, "core": 2}
SEQ = ("yh", "z", "x", "core")
TOK = 384
DH = 512
SCALE = DH ** -0.5

f32 = jnp.float32
bf16 = jnp.bfloat16


def shift(value, axis, steps):
    count = SIZES[axis]
    return lax.ppermute(value, axis, [(i, (i + steps) % count) for i in range(count)])


def dot(a, b, dims):
    return lax.dot_general(a, b, (dims, ((), ())), preferred_element_type=f32)


NN = ((1,), (0,))
NT = ((1,), (1,))
TN = ((0,), (0,))


def cparams(**kw):
    return pltpu.CompilerParams(vmem_limit_bytes=56 * 1024 * 1024, **kw)


def piece_rows(kind, part, idx, item):
    yh, z, x = idx
    a, k = item % 2, item // 2
    y = lax.rem(yh + a, 2)
    if kind == 0:
        zz, xx = lax.rem(z + k, 4), lax.rem(x + part, 4)
    else:
        zz, xx = lax.rem(z + part, 4), lax.rem(x + k, 4)
    return pl.multiple_of(y * 256 + zz * 64 + xx * 16, 16)


def weight_copies(head, pieces, w_vmem, sem, idx):
    for part in range(4):
        for item in range(8):
            row = piece_rows(head, part, idx, item)
            yield pltpu.make_async_copy(
                pieces[head * 4 + part].at[item],
                w_vmem.at[head, :, pl.ds(row, 16), :],
                sem.at[head],
            )


def load_weights(pieces, w_vmem, sem, idx, head_now):
    @pl.when(head_now == 0)
    def _():
        for head in range(2):
            for copy in weight_copies(head, pieces, w_vmem, sem, idx):
                copy.start()

    for head in range(2):

        @pl.when(head_now == head)
        def _(head=head):
            pltpu.make_async_copy(w_vmem.at[head], w_vmem.at[head], sem.at[head]).wait()


def grads_kernel(s_ref, *refs):
    pieces = refs[:8]
    k_own, v_own, k_rec, v_rec, r_ref = refs[8:13]
    outs = refs[13:21]
    w_vmem, sums, sem = refs[21:]
    head = pl.program_id(0)
    idx = (s_ref[1], s_ref[2], s_ref[3])
    load_weights(pieces, w_vmem, sem, idx, head)
    gate, up, down = w_vmem[head, 0], w_vmem[head, 1], w_vmem[head, 2]
    halves = []
    for j, (k_ref, v_ref) in enumerate(((k_own, v_own), (k_rec, v_rec))):
        k = k_ref[0]
        rate = r_ref[0, j]
        target = (-(rate * v_ref[0].astype(f32))).astype(bf16)
        g = dot(k, gate, NN)
        u = dot(k, up, NN)
        back = dot(target, down, NT)
        s = jax.nn.sigmoid(g)
        silu = g * s
        active = (silu * u).astype(bf16)
        d_gate = (back * u * s * (1.0 + g * (1.0 - s))).astype(bf16)
        d_up = (back * silu).astype(bf16)
        halves.append((k, target, active, d_gate, d_up))
    k, target, active, d_gate, d_up = (jnp.concatenate(pair, axis=0) for pair in zip(*halves))
    sums[0] = dot(k, d_gate, TN)
    sums[1] = dot(k, d_up, TN)
    sums[2] = dot(active, target, TN)
    yh, z, x = idx
    for kind in range(2):

        @pl.when(head == kind)
        def _(kind=kind):
            for part in range(4):
                for item in range(8):
                    a, k = item % 2, item // 2
                    y = lax.rem(yh + a, 2)
                    zz = lax.rem(z + 4 - (k if kind == 0 else part), 4)
                    xx = lax.rem(x + 4 - (part if kind == 0 else k), 4)
                    row = pl.multiple_of(y * 256 + zz * 64 + xx * 16, 16)
                    for m in range(3):
                        outs[kind * 4 + part][item, m] = sums[m, pl.ds(row, 16), :].astype(bf16)


def own_spec(c):
    return pl.BlockSpec((1, TOK, DH), lambda h, s: (c, 0, s[0] * 2 + h))


def rec_spec(c):
    return pl.BlockSpec((1, TOK, DH), lambda h, s: (c, 0, h))


ANY = pl.BlockSpec(memory_space=pl.ANY)


def compute_grads(scal, pieces, k, v, k_rec, v_rec, rates):
    whole = pl.BlockSpec((8, 3, 16, DH), lambda h, s: (0, 0, 0, 0))
    return pl.pallas_call(
        grads_kernel,
        name="fast_grads",
        out_shape=[jax.ShapeDtypeStruct((8, 3, 16, DH), bf16)] * 8,
        grid_spec=pltpu.PrefetchScalarGridSpec(
            num_scalar_prefetch=1,
            grid=(2,),
            in_specs=[ANY] * 8
            + [own_spec(0), own_spec(0), rec_spec(0), rec_spec(0)]
            + [pl.BlockSpec((1, 2, TOK, 1), lambda h, s: (h, 0, 0, 0))],
            out_specs=[whole] * 8,
            scratch_shapes=[
                pltpu.VMEM((2, 3, DH, DH), bf16),
                pltpu.VMEM((3, DH, DH), f32),
                pltpu.SemaphoreType.DMA((2,)),
            ],
        ),
        compiler_params=cparams(),
    )(scal, *pieces, k, v, k_rec, v_rec, rates)


def apply_kernel(s_ref, *refs):
    pieces = refs[:8]
    q_own, q_rec = refs[8:10]
    out_ref, pow_ref = refs[10:12]
    w_vmem, sem = refs[12:]
    head = pl.program_id(0)
    idx = (s_ref[1], s_ref[2], s_ref[3])
    load_weights(pieces, w_vmem, sem, idx, head)
    gate, up, down = w_vmem[head, 0], w_vmem[head, 1], w_vmem[head, 2]
    core = s_ref[0]
    for j, q_ref in enumerate((q_own, q_rec)):
        block = core if j == 0 else 1 - core
        q = q_ref[0]
        g = dot(q, gate, NN)
        u = dot(q, up, NN)
        active = (g * jax.nn.sigmoid(g) * u).astype(bf16)
        out = dot(active, down, NN)
        out_ref[j] = out
        power = jnp.sum(out * out, axis=-1, keepdims=True)
        power = jnp.transpose(jnp.broadcast_to(power, (TOK, 128)))[:8]

        @pl.when(head == 0)
        def _(block=block, power=power):
            pow_ref[block] = power

        @pl.when(head == 1)
        def _(block=block, power=power):
            pow_ref[block] += power


def fast_apply(c, scal, pieces, q, q_rec):
    return pl.pallas_call(
        apply_kernel,
        name="fast_apply",
        out_shape=[
            jax.ShapeDtypeStruct((2, TOK, 2 * DH), f32),
            jax.ShapeDtypeStruct((2, 8, TOK), f32),
        ],
        grid_spec=pltpu.PrefetchScalarGridSpec(
            num_scalar_prefetch=1,
            grid=(2,),
            in_specs=[ANY] * 8 + [own_spec(c), rec_spec(c)],
            out_specs=[
                pl.BlockSpec((2, TOK, DH), lambda h, s: (0, 0, h)),
                pl.BlockSpec((2, 8, TOK), lambda h, s: (0, 0, 0)),
            ],
            scratch_shapes=[
                pltpu.VMEM((2, 3, DH, DH), bf16),
                pltpu.SemaphoreType.DMA((2,)),
            ],
        ),
        compiler_params=cparams(),
    )(scal, *pieces, q, q_rec)


LOG2E = 1.4426950408889634


def finish_kernel(c, j, sources, count, s_ref, *refs):
    core, chip = s_ref[0], s_ref[5]
    block = core if j == 0 else 1 - core
    q_ref, refs = refs[0], refs[1:]
    before, refs = refs[: 4 * sources], refs[4 * sources :]
    kb, k2, vb, v2, fast_ref, gain_ref = refs[:6]
    powers, out_ref = refs[6 : 6 + count], refs[-1]
    k0, ka, v0, va = (before[i][0] for i in range(4))
    for more in range(1, sources):
        here = chosen(s_ref) == more
        k0, ka, v0, va = (
            jnp.where(here, before[4 * more + i][0], old) for i, old in enumerate((k0, ka, v0, va))
        )
    first = block == 0
    keys = (k0, jnp.where(first, ka, kb[0]), k2[0])
    values = (v0, jnp.where(first, va, vb[0]), v2[0])
    row = lax.broadcasted_iota(jnp.int32, (TOK, TOK), 0)
    col = lax.broadcasted_iota(jnp.int32, (TOK, TOK), 1)
    scores = [dot(q_ref[0], k, NT) for k in keys]
    low = row
    if c == 0:
        low = jnp.where(chip == 0, TOK, row)
        scores[1] = jnp.where(col >= jnp.where((chip == 0) & first, TOK, 0), scores[1], MASKED)
    scores[0] = jnp.where(col > low, scores[0], MASKED)
    scores[2] = jnp.where(col <= row, scores[2], MASKED)
    peak = jnp.max(jnp.maximum(jnp.maximum(scores[0], scores[1]), scores[2]), axis=-1, keepdims=True)
    weights = [jnp.exp2((s - peak) * (SCALE * LOG2E)) for s in scores]
    inv = 1.0 / jnp.sum(weights[0] + weights[1] + weights[2], axis=-1, keepdims=True)
    attended = sum(dot((w * inv).astype(bf16), v, NN) for w, v in zip(weights, values))

    total = sum(p[0] for p in powers[1:]) + powers[0][0]
    rs = lax.rsqrt(total * (1.0 / 4096.0) + NORM_EPS)
    col = jnp.transpose(rs)[:, :1]
    out = (fast_ref[0] * gain_ref[...] * col + attended).astype(bf16)
    out_ref[...] = out.reshape(out_ref.shape)


def chosen(s):
    return jnp.where(s[5] == 0, 2, jnp.where(s[4] == 1, 1, 0))


def finish(c, j, scal, q, q_rec, mine, before, fast, powers, gain, layer=None):
    def block(s):
        return s[0] if j == 0 else 1 - s[0]

    def spec(at, holds=lambda s: True):
        return pl.BlockSpec(
            (1, TOK, DH),
            lambda h, s: (jnp.where(holds(s), at(s), 0), 0, jnp.where(holds(s), h, 0)),
        )

    def always(at):
        return pl.BlockSpec((1, TOK, DH), lambda h, s: (at(s), 0, h))

    sources = len(before)
    q_spec = own_spec(c) if j == 0 else rec_spec(c)
    specs = [q_spec]
    operands = [q if j == 0 else q_rec]
    for i, array in enumerate(before):
        holds = (lambda s, i=i: chosen(s) == i) if sources > 1 else (lambda s: True)
        specs += [
            spec(block, holds), spec(lambda s: 1, holds),
            spec(lambda s: 2 + block(s), holds), spec(lambda s: 3, holds),
        ]
        operands += [array] * 4
    specs += [
        always(lambda s: 0), always(block), always(lambda s: 2), always(lambda s: 2 + block(s)),
        pl.BlockSpec((1, TOK, DH), lambda h, s: (j, 0, h)),
        pl.BlockSpec((1, DH), lambda h, s: (0, h)),
    ]
    operands += [mine] * 4 + [fast, gain]
    specs += [pl.BlockSpec((1, 8, TOK), lambda h, s: (block(s), 0, 0))] * len(powers)
    operands += powers
    aliases = {}
    if layer is not None:
        aliases = {len(operands) + 1: 0}
        specs.append(ANY)
        operands.append(layer)
    if j == 0:
        shape = (2, TOK, 4 * DH)
        out_spec = pl.BlockSpec((1, TOK, DH), lambda h, s: (c, 0, s[0] * 2 + h))
    else:
        shape = (TOK, 2 * DH)
        out_spec = pl.BlockSpec((TOK, DH), lambda h, s: (0, h))
    return pl.pallas_call(
        functools.partial(finish_kernel, c, j, sources, len(powers)),
        name="attend_finish",
        out_shape=jax.ShapeDtypeStruct(shape, bf16),
        grid_spec=pltpu.PrefetchScalarGridSpec(
            num_scalar_prefetch=1, grid=(2,), in_specs=specs, out_specs=out_spec
        ),
        input_output_aliases=aliases,
        compiler_params=cparams(),
    )(scal, *operands)


def gather_direct(both):
    out = []
    for head, (first, last) in enumerate((("z", "x"), ("x", "z"))):
        v = both[head]
        v = jnp.concatenate([v] + [shift(v, first, -k) for k in range(1, 4)], axis=0)
        out.append([v] + [shift(v, last, -k) for k in range(1, 4)])
    return out[0] + out[1]


def gather_rings(both):
    axes = (("z", "x"), ("x", "z"))
    now = [both[h] for h in range(2)]
    held = [[n] for n in now]
    for _ in range(3):
        for h in range(2):
            now[h] = shift(now[h], axes[h][0], -1)
            held[h].append(now[h])
    now = [jnp.concatenate(held[h], axis=0) for h in range(2)]
    out = [[n] for n in now]
    for _ in range(3):
        for h in range(2):
            now[h] = shift(now[h], axes[h][1], -1)
            out[h].append(now[h])
    return out[0] + out[1]


def scatter_rings(slabs):
    axes = (("x", "z"), ("z", "x"))
    now = [slabs[3], slabs[7]]
    for k in (2, 1, 0):
        for h in range(2):
            got = shift(now[h], axes[h][0], -1)
            total = got.astype(f32) + slabs[h * 4 + k].astype(f32)
            now[h] = total.astype(bf16) if k else total
    parts = now
    now = [p[6:8].astype(bf16) for p in parts]
    for k in (2, 1, 0):
        for h in range(2):
            got = shift(now[h], axes[h][1], -1)
            now[h] = (got.astype(f32) + parts[h][2 * k : 2 * k + 2]).astype(bf16)
    return jnp.stack(now)


CORES = [(0, 1), (1, 0), (2, 3), (3, 2)]
HALVES = [(0, 2), (2, 0), (1, 3), (3, 1)]
ACROSS = [(0, 3), (3, 0), (1, 2), (2, 1)]


def with_parts(power, pairs):
    return [power] + [lax.ppermute(power, ("heads", "core"), p) for p in pairs]


def on_device(queries, key_rows, value_rows, step_rates, w_gate, w_up, w_down, out_gain):
    core = lax.axis_index("core")
    yh, z, x = lax.axis_index("yh"), lax.axis_index("z"), lax.axis_index("x")
    chip = (yh * 4 + z) * 4 + x
    turn = ((z == 0) & (x == 0)).astype(jnp.int32)
    scal = jnp.stack([core, yh, z, x, turn, chip]).astype(jnp.int32)

    masters = jnp.stack([w_gate, w_up, w_down], axis=1)
    mine = lax.dynamic_slice_in_dim(masters, core * 2, 2, 0)
    theirs = lax.dynamic_slice_in_dim(masters, (1 - core) * 2, 2, 0)
    got = shift(theirs, "core", 1)
    m16 = jnp.where(
        core == 0,
        jnp.concatenate([mine, got], axis=2),
        jnp.concatenate([got, mine], axis=2),
    )
    m16_other = shift(m16, "yh", 1)
    m16_other, key_rows, value_rows, queries, step_rates = lax.optimization_barrier(
        (m16_other, key_rows, value_rows, queries, step_rates)
    )
    both = jnp.stack([m16, m16_other], axis=1)
    pieces = gather_direct(both.astype(bf16))

    def split_in(a):
        keep = lax.dynamic_slice_in_dim(a, core * 1024, 1024, 2)
        give = lax.dynamic_slice_in_dim(a, (1 - core) * 1024, 1024, 2)
        return keep, shift(give, "core", 1)

    k_own, k_rec = split_in(key_rows)
    v_own, v_rec = split_in(value_rows)
    q_rec = split_in(queries)[1]
    rates = step_rates[:, 0, :]
    r_own = lax.dynamic_slice_in_dim(rates, core * 2, 2, 0)
    r_rec = shift(lax.dynamic_slice_in_dim(rates, (1 - core) * 2, 2, 0), "core", 1)
    rates = jnp.stack([r_own, r_rec], axis=1)[..., None]

    chips = ("yh", "z", "x")
    row = [(i, (i + 1) % 32) for i in range(32)]
    pair = [
        jnp.where(
            core == 0,
            jnp.stack([k_own[c], k_rec[c], v_own[c], v_rec[c]]),
            jnp.stack([k_rec[c], k_own[c], v_rec[c], v_own[c]]),
        )
        for c in range(2)
    ]
    pair[0], pair[1], *pieces = lax.optimization_barrier((pair[0], pair[1], *pieces))
    halo0 = lax.ppermute(pair[0], chips, row)
    halo1 = lax.ppermute(pair[1], chips, [p for p in row if p[0] % 16 != 15])

    slabs = compute_grads(scal, pieces, key_rows, value_rows, k_rec, v_rec, rates)
    fast0, pow0 = fast_apply(0, scal, pieces, queries, q_rec)
    half_sums = scatter_rings(slabs)
    pow0 = sum(with_parts(pow0, (CORES,)))
    half_sums, pow0 = lax.optimization_barrier((half_sums, pow0))
    other_sums = shift(half_sums, "yh", 1)
    powers0 = with_parts(pow0, (HALVES,))
    grad_both = half_sums.astype(f32) + other_sums[:, ::-1].astype(f32)
    grad_both, pair1, *powers0 = lax.optimization_barrier((grad_both, pair[1], *powers0))
    new_both = both - grad_both
    new16 = new_both[:, 0]
    pieces2 = gather_rings(new_both.astype(bf16))
    turned1 = lax.ppermute(pair1, chips, [(15, 16)])
    own_rows = lax.dynamic_slice_in_dim(new16, core * 8, 8, 2)
    their_rows = shift(lax.dynamic_slice_in_dim(new16, (1 - core) * 8, 8, 2), "core", 1)
    new_all = jnp.where(
        core == 0,
        jnp.concatenate([own_rows, their_rows], axis=0),
        jnp.concatenate([their_rows, own_rows], axis=0),
    )

    gain = lax.dynamic_slice_in_dim(out_gain, core * 1024, 1024, 0)[None]

    def complete(c, before, fast, powers, layer):
        args = (scal, queries, q_rec, pair[c], before, fast, powers, gain)
        out_rec = finish(c, 1, *args)
        arrived = shift(out_rec, "core", 1)
        layer = finish(c, 0, *args, layer)
        return lax.dynamic_update_slice(layer, arrived[None], (c, 0, (1 - core) * 1024))

    layer_out = complete(0, [halo0], fast0, powers0, None)
    fast1, pow1 = fast_apply(1, scal, pieces2, queries, q_rec)
    powers1 = with_parts(pow1, (CORES, HALVES, ACROSS))
    layer_out = complete(1, [halo1, turned1, halo0], fast1, powers1, layer_out)
    return layer_out, new_all[:, 0], new_all[:, 1], new_all[:, 2]


def solution(mesh):
    fine = Mesh(mesh.devices.reshape(2, 2, 4, 4, 2), ("heads",) + SEQ)
    rows = P(None, SEQ, "heads")
    weight = P("heads", SEQ, None)
    return jax.shard_map(
        on_device,
        mesh=fine,
        in_specs=(rows, rows, rows, P("heads", None, SEQ), weight, weight, weight, P("heads")),
        out_specs=(rows, weight, weight, weight),
        check_vma=False,
    )
```

```python
import functools

import jax
import jax.numpy as jnp
from jax import lax
from jax.experimental import pallas as pl
from jax.experimental.pallas import tpu as pltpu
from jax.sharding import Mesh, PartitionSpec as P

NORM_EPS = 1e-05
MASKED = -1e30
SIZES = {"heads": 2, "yh": 2, "z": 4, "x": 4, "core": 2}
SEQ = ("yh", "z", "x", "core")
TOK = 384
DH = 512
SCALE = DH ** -0.5

f32 = jnp.float32
bf16 = jnp.bfloat16


def shift(value, axis, steps):
    count = SIZES[axis]
    return lax.ppermute(value, axis, [(i, (i + steps) % count) for i in range(count)])


def dot(a, b, dims):
    return lax.dot_general(a, b, (dims, ((), ())), preferred_element_type=f32)


NN = ((1,), (0,))
NT = ((1,), (1,))
TN = ((0,), (0,))


def cparams(**kw):
    return pltpu.CompilerParams(vmem_limit_bytes=56 * 1024 * 1024, **kw)


def piece_rows(kind, part, idx, item, sign):
    yh, z, x = idx
    a, k = lax.rem(item, 2), lax.div(item, 2)
    y = lax.rem(yh + a, 2)
    zz = lax.rem(z + 4 + sign * (k if kind == 0 else part), 4)
    xx = lax.rem(x + 4 + sign * (part if kind == 0 else k), 4)
    return pl.multiple_of(y * 256 + zz * 64 + xx * 16, 16)


def load_weights(pieces, w_vmem, sem, idx, head_now, half):
    @pl.when((head_now == 0) & (half == 0))
    def _():
        for head in range(2):

            def start(item, carry, head=head):
                for part in range(4):
                    row = piece_rows(head, part, idx, item, 1)
                    pltpu.make_async_copy(
                        pieces[head * 4 + part].at[item],
                        w_vmem.at[head, :, pl.ds(row, 16), :],
                        sem.at[head],
                    ).start()
                return carry

            lax.fori_loop(0, 8, start, 0)

    for head in range(2):

        @pl.when((head_now == head) & (half == 0))
        def _(head=head):
            pltpu.make_async_copy(w_vmem.at[head], w_vmem.at[head], sem.at[head]).wait()


def grads_kernel(s_ref, *refs):
    pieces = refs[:8]
    k_own, v_own, k_rec, v_rec, r_ref = refs[8:13]
    outs = refs[13:21]
    w_vmem, held, sums, sem = refs[21:]
    head, half = pl.program_id(0), pl.program_id(1)
    idx = (s_ref[1], s_ref[2], s_ref[3])
    load_weights(pieces, w_vmem, sem, idx, head, half)
    gate, up, down = w_vmem[head, 0], w_vmem[head, 1], w_vmem[head, 2]
    k = jnp.where(half == 0, k_own[0], k_rec[0])
    v = jnp.where(half == 0, v_own[0], v_rec[0])
    target = (-(r_ref[0, half] * v.astype(f32))).astype(bf16)
    g = dot(k, gate, NN)
    u = dot(k, up, NN)
    back = dot(target, down, NT)
    s = jax.nn.sigmoid(g)
    silu = g * s
    rows = pl.ds(pl.multiple_of(half * TOK, TOK), TOK)
    held[0, rows] = k
    held[1, rows] = target
    held[2, rows] = (silu * u).astype(bf16)
    held[3, rows] = (back * u * s * (1.0 + g * (1.0 - s))).astype(bf16)
    held[4, rows] = (back * silu).astype(bf16)

    @pl.when(half == 1)
    def _():
        sums[0] = dot(held[0], held[3], TN)
        sums[1] = dot(held[0], held[4], TN)
        sums[2] = dot(held[2], held[1], TN)

    for kind in range(2):

        @pl.when((head == kind) & (half == 1))
        def _(kind=kind):
            def store(item, carry):
                for part in range(4):
                    row = piece_rows(kind, part, idx, item, -1)
                    for m in range(3):
                        outs[kind * 4 + part][item, m] = sums[m, pl.ds(row, 16), :].astype(bf16)
                return carry

            lax.fori_loop(0, 8, store, 0)


def own_spec(c):
    return pl.BlockSpec((1, TOK, DH), lambda *at: (c, 0, at[-1][0] * 2 + at[0]))


def rec_spec(c):
    return pl.BlockSpec((1, TOK, DH), lambda *at: (c, 0, at[0]))


ANY = pl.BlockSpec(memory_space=pl.ANY)


def compute_grads(scal, pieces, k, v, k_rec, v_rec, rates):
    whole = pl.BlockSpec((8, 3, 16, DH), lambda h, j, s: (0, 0, 0, 0))
    return pl.pallas_call(
        grads_kernel,
        name="fast_grads",
        out_shape=[jax.ShapeDtypeStruct((8, 3, 16, DH), bf16)] * 8,
        grid_spec=pltpu.PrefetchScalarGridSpec(
            num_scalar_prefetch=1,
            grid=(2, 2),
            in_specs=[ANY] * 8
            + [own_spec(0), own_spec(0), rec_spec(0), rec_spec(0)]
            + [pl.BlockSpec((1, 2, TOK, 1), lambda h, j, s: (h, 0, 0, 0))],
            out_specs=[whole] * 8,
            scratch_shapes=[
                pltpu.VMEM((2, 3, DH, DH), bf16),
                pltpu.VMEM((5, 2 * TOK, DH), bf16),
                pltpu.VMEM((3, DH, DH), f32),
                pltpu.SemaphoreType.DMA((2,)),
            ],
        ),
        compiler_params=cparams(),
    )(scal, *pieces, k, v, k_rec, v_rec, rates)


def apply_kernel(s_ref, *refs):
    pieces = refs[:8]
    q_own, q_rec = refs[8:10]
    out_ref, pow_ref = refs[10:12]
    w_vmem, sem = refs[12:]
    head, half = pl.program_id(0), pl.program_id(1)
    idx = (s_ref[1], s_ref[2], s_ref[3])
    load_weights(pieces, w_vmem, sem, idx, head, half)
    gate, up, down = w_vmem[head, 0], w_vmem[head, 1], w_vmem[head, 2]
    block = jnp.where(half == 0, s_ref[0], 1 - s_ref[0])
    q = jnp.where(half == 0, q_own[0], q_rec[0])
    g = dot(q, gate, NN)
    u = dot(q, up, NN)
    active = (g * jax.nn.sigmoid(g) * u).astype(bf16)
    out = dot(active, down, NN)
    out_ref[0] = out
    power = jnp.sum(out * out, axis=-1, keepdims=True)
    power = jnp.transpose(jnp.broadcast_to(power, (TOK, 128)))[:8]

    @pl.when(head == 0)
    def _():
        pow_ref[block] = power

    @pl.when(head == 1)
    def _():
        pow_ref[block] += power


def fast_apply(c, scal, pieces, q, q_rec):
    return pl.pallas_call(
        apply_kernel,
        name="fast_apply",
        out_shape=[
            jax.ShapeDtypeStruct((2, TOK, 2 * DH), f32),
            jax.ShapeDtypeStruct((2, 8, TOK), f32),
        ],
        grid_spec=pltpu.PrefetchScalarGridSpec(
            num_scalar_prefetch=1,
            grid=(2, 2),
            in_specs=[ANY] * 8 + [own_spec(c), rec_spec(c)],
            out_specs=[
                pl.BlockSpec((1, TOK, DH), lambda h, j, s: (j, 0, h)),
                pl.BlockSpec((2, 8, TOK), lambda h, j, s: (0, 0, 0)),
            ],
            scratch_shapes=[
                pltpu.VMEM((2, 3, DH, DH), bf16),
                pltpu.SemaphoreType.DMA((2,)),
            ],
        ),
        compiler_params=cparams(),
    )(scal, *pieces, q, q_rec)


LOG2E = 1.4426950408889634


def partial_attention(q, blocks):
    scores = []
    for k, _, mask in blocks:
        s = dot(q, k, NT)
        scores.append(s if mask is None else jnp.where(mask, s, MASKED))
    peak = jnp.max(functools.reduce(jnp.maximum, scores), axis=-1, keepdims=True)
    weights = [jnp.exp2((s - peak) * (SCALE * LOG2E)) for s in scores]
    total = jnp.sum(sum(weights[1:], weights[0]), axis=-1, keepdims=True)
    acc = sum(dot(w.astype(bf16), v, NN) for w, (_, v, _) in zip(weights, blocks))
    return acc, peak, total


def local_kernel(s_ref, qo, qr, kb, k2, vb, v2, acc_ref, stat_ref):
    block = pl.program_id(1)
    q = jnp.where(s_ref[0] == block, qo[0], qr[0])
    row = lax.broadcasted_iota(jnp.int32, (TOK, TOK), 0)
    col = lax.broadcasted_iota(jnp.int32, (TOK, TOK), 1)
    lane = lax.broadcasted_iota(jnp.int32, (TOK, 128), 1)
    for b in range(2):

        @pl.when(block == b)
        def _(b=b):
            blocks = [(k2[0], v2[0], col <= row)]
            if b == 1:
                blocks.append((kb[0], vb[0], None))
            acc, peak, total = partial_attention(q, blocks)
            acc_ref[0] = acc
            stat_ref[0, 0] = jnp.where(lane < 64, peak, total)


def attend_local(c, scal, q, q_rec, mine):
    def block(at):
        return pl.BlockSpec((1, TOK, DH), lambda h, b, s: (at(b), 0, h))

    return pl.pallas_call(
        local_kernel,
        name="attend_local",
        out_shape=[
            jax.ShapeDtypeStruct((2, TOK, 2 * DH), f32),
            jax.ShapeDtypeStruct((2, 2, TOK, 128), f32),
        ],
        grid_spec=pltpu.PrefetchScalarGridSpec(
            num_scalar_prefetch=1,
            grid=(2, 2),
            in_specs=[
                pl.BlockSpec((1, TOK, DH), lambda h, b, s: (c, 0, s[0] * 2 + h)),
                pl.BlockSpec((1, TOK, DH), lambda h, b, s: (c, 0, h)),
                block(lambda b: 0), block(lambda b: b), block(lambda b: 2), block(lambda b: 2 + b),
            ],
            out_specs=[
                pl.BlockSpec((1, TOK, DH), lambda h, b, s: (b, 0, h)),
                pl.BlockSpec((1, 1, TOK, 128), lambda h, b, s: (b, h, 0, 0)),
            ],
        ),
        compiler_params=cparams(),
    )(scal, q, q_rec, mine, mine, mine, mine)


def finish_kernel(c, j, sources, count, s_ref, *refs):
    core, chip = s_ref[0], s_ref[5]
    block = core if j == 0 else 1 - core
    q_ref, refs = refs[0], refs[1:]
    before, refs = refs[: 4 * sources], refs[4 * sources :]
    own, refs = (refs[:4], refs[4:]) if c == 0 else (refs[:2], refs[2:])
    fast_ref, gain_ref = refs[:2]
    powers = refs[2 : 2 + count]
    out_ref = refs[-1]
    row = lax.broadcasted_iota(jnp.int32, (TOK, TOK), 0)
    col = lax.broadcasted_iota(jnp.int32, (TOK, TOK), 1)
    total = sum(p[0] for p in powers[1:]) + powers[0][0]
    rs = lax.rsqrt(total * (1.0 / 4096.0) + NORM_EPS)
    fast = fast_ref[0] * gain_ref[...] * jnp.transpose(rs)[:, :1]

    def put(attended):
        out_ref[...] = (fast + attended).astype(bf16).reshape(out_ref.shape)

    if c == 1:
        acc_ref, stat_ref = own

        def here(i):
            found = before[i][0]
            for more in range(1, sources):
                found = jnp.where(chosen(s_ref) == more, before[4 * more + i][0], found)
            return found

        for b in range(2):

            @pl.when(block == b)
            def _(b=b):
                blocks = [(here(0), here(2), col > row)]
                if b == 0:
                    blocks.append((here(1), here(3), None))
                acc, peak, total = partial_attention(q_ref[0], blocks)
                peak_own, total_own = stat_ref[0, 0, :, :1], stat_ref[0, 0, :, 64:65]
                top = jnp.maximum(peak, peak_own)
                scale = jnp.exp2((peak - top) * (SCALE * LOG2E))
                scale_own = jnp.exp2((peak_own - top) * (SCALE * LOG2E))
                inv = 1.0 / (total * scale + total_own * scale_own)
                put(acc * (scale * inv) + acc_ref[0] * (scale_own * inv))

        return

    kb, k2, vb, v2 = own
    k0, ka, v0, va = before
    first = block == 0
    keys = (k0[0], jnp.where(first, ka[0], kb[0]), k2[0])
    values = (v0[0], jnp.where(first, va[0], vb[0]), v2[0])
    scores = [dot(q_ref[0], k, NT) for k in keys]
    low = jnp.where(chip == 0, TOK, row)
    scores[1] = jnp.where(col >= jnp.where((chip == 0) & first, TOK, 0), scores[1], MASKED)
    scores[0] = jnp.where(col > low, scores[0], MASKED)
    scores[2] = jnp.where(col <= row, scores[2], MASKED)
    peak = jnp.max(jnp.maximum(jnp.maximum(scores[0], scores[1]), scores[2]), axis=-1, keepdims=True)
    weights = [jnp.exp2((s - peak) * (SCALE * LOG2E)) for s in scores]
    inv = 1.0 / jnp.sum(weights[0] + weights[1] + weights[2], axis=-1, keepdims=True)
    put(sum(dot((w * inv).astype(bf16), v, NN) for w, v in zip(weights, values)))


def chosen(s):
    return jnp.where(s[5] == 0, 2, jnp.where(s[4] == 1, 1, 0))


def finish(c, j, scal, q, q_rec, own, before, fast, powers, gain, layer=None):
    def block(s):
        return s[0] if j == 0 else 1 - s[0]

    def spec(at, holds=lambda s: True):
        return pl.BlockSpec(
            (1, TOK, DH),
            lambda h, s: (jnp.where(holds(s), at(s), 0), 0, jnp.where(holds(s), h, 0)),
        )

    def always(at):
        return pl.BlockSpec((1, TOK, DH), lambda h, s: (at(s), 0, h))

    sources = len(before)
    q_spec = own_spec(c) if j == 0 else rec_spec(c)
    specs = [q_spec]
    operands = [q if j == 0 else q_rec]
    for i, array in enumerate(before):
        holds = (lambda s, i=i: chosen(s) == i) if sources > 1 else (lambda s: True)
        specs += [
            spec(block, holds), spec(lambda s: 1, holds),
            spec(lambda s: 2 + block(s), holds), spec(lambda s: 3, holds),
        ]
        operands += [array] * 4
    if c == 0:
        specs += [
            always(lambda s: 0), always(block), always(lambda s: 2), always(lambda s: 2 + block(s))
        ]
        operands += [own] * 4
    else:
        specs += [
            always(block), pl.BlockSpec((1, 1, TOK, 128), lambda h, s: (block(s), h, 0, 0))
        ]
        operands += list(own)
    specs += [
        pl.BlockSpec((1, TOK, DH), lambda h, s: (j, 0, h)),
        pl.BlockSpec((1, DH), lambda h, s: (0, h)),
    ]
    operands += [fast, gain]
    specs += [pl.BlockSpec((1, 8, TOK), lambda h, s: (block(s), 0, 0))] * len(powers)
    operands += powers
    aliases = {}
    if layer is not None:
        aliases = {len(operands) + 1: 0}
        specs.append(ANY)
        operands.append(layer)
    if j == 0:
        shape = (2, TOK, 4 * DH)
        out_spec = pl.BlockSpec((1, TOK, DH), lambda h, s: (c, 0, s[0] * 2 + h))
    else:
        shape = (TOK, 2 * DH)
        out_spec = pl.BlockSpec((TOK, DH), lambda h, s: (0, h))
    return pl.pallas_call(
        functools.partial(finish_kernel, c, j, sources, len(powers)),
        name="attend_finish",
        out_shape=jax.ShapeDtypeStruct(shape, bf16),
        grid_spec=pltpu.PrefetchScalarGridSpec(
            num_scalar_prefetch=1, grid=(2,), in_specs=specs, out_specs=out_spec
        ),
        input_output_aliases=aliases,
        compiler_params=cparams(),
    )(scal, *operands)


def gather_direct(both):
    out = []
    for head, (first, last) in enumerate((("z", "x"), ("x", "z"))):
        v = both[head]
        v = jnp.concatenate([v] + [shift(v, first, -k) for k in range(1, 4)], axis=0)
        out.append([v] + [shift(v, last, -k) for k in range(1, 4)])
    return out[0] + out[1]


def gather_rings(both):
    axes = (("z", "x"), ("x", "z"))
    now = [both[h] for h in range(2)]
    held = [[n] for n in now]
    for _ in range(3):
        for h in range(2):
            now[h] = shift(now[h], axes[h][0], -1)
            held[h].append(now[h])
    now = [jnp.concatenate(held[h], axis=0) for h in range(2)]
    out = [[n] for n in now]
    for _ in range(3):
        for h in range(2):
            now[h] = shift(now[h], axes[h][1], -1)
            out[h].append(now[h])
    return out[0] + out[1]


def scatter_rings(slabs):
    axes = (("x", "z"), ("z", "x"))
    now = [slabs[3], slabs[7]]
    for k in (2, 1, 0):
        for h in range(2):
            got = shift(now[h], axes[h][0], -1)
            total = got.astype(f32) + slabs[h * 4 + k].astype(f32)
            now[h] = total.astype(bf16) if k else total
    parts = now
    now = [p[6:8].astype(bf16) for p in parts]
    for k in (2, 1, 0):
        for h in range(2):
            got = shift(now[h], axes[h][1], -1)
            now[h] = (got.astype(f32) + parts[h][2 * k : 2 * k + 2]).astype(bf16)
    return jnp.stack(now)


CORES = [(0, 1), (1, 0), (2, 3), (3, 2)]
HALVES = [(0, 2), (2, 0), (1, 3), (3, 1)]
ACROSS = [(0, 3), (3, 0), (1, 2), (2, 1)]


def with_parts(power, pairs):
    return [power] + [lax.ppermute(power, ("heads", "core"), p) for p in pairs]


def on_device(queries, key_rows, value_rows, step_rates, w_gate, w_up, w_down, out_gain):
    core = lax.axis_index("core")
    yh, z, x = lax.axis_index("yh"), lax.axis_index("z"), lax.axis_index("x")
    chip = (yh * 4 + z) * 4 + x
    turn = ((z == 0) & (x == 0)).astype(jnp.int32)
    scal = jnp.stack([core, yh, z, x, turn, chip]).astype(jnp.int32)

    masters = jnp.stack([w_gate, w_up, w_down], axis=1)
    mine = lax.dynamic_slice_in_dim(masters, core * 2, 2, 0)
    theirs = lax.dynamic_slice_in_dim(masters, (1 - core) * 2, 2, 0)
    got = shift(theirs, "core", 1)
    m16 = jnp.where(
        core == 0,
        jnp.concatenate([mine, got], axis=2),
        jnp.concatenate([got, mine], axis=2),
    )
    m16_other = shift(m16, "yh", 1)
    m16_other, key_rows, value_rows, queries, step_rates = lax.optimization_barrier(
        (m16_other, key_rows, value_rows, queries, step_rates)
    )
    both = jnp.stack([m16, m16_other], axis=1)
    pieces = gather_direct(both.astype(bf16))

    def split_in(a):
        keep = lax.dynamic_slice_in_dim(a, core * 1024, 1024, 2)
        give = lax.dynamic_slice_in_dim(a, (1 - core) * 1024, 1024, 2)
        return keep, shift(give, "core", 1)

    k_own, k_rec = split_in(key_rows)
    v_own, v_rec = split_in(value_rows)
    q_rec = split_in(queries)[1]
    rates = step_rates[:, 0, :]
    r_own = lax.dynamic_slice_in_dim(rates, core * 2, 2, 0)
    r_rec = shift(lax.dynamic_slice_in_dim(rates, (1 - core) * 2, 2, 0), "core", 1)
    rates = jnp.stack([r_own, r_rec], axis=1)[..., None]

    chips = ("yh", "z", "x")
    row = [(i, (i + 1) % 32) for i in range(32)]
    pair = [
        jnp.where(
            core == 0,
            jnp.stack([k_own[c], k_rec[c], v_own[c], v_rec[c]]),
            jnp.stack([k_rec[c], k_own[c], v_rec[c], v_own[c]]),
        )
        for c in range(2)
    ]
    pair[0], pair[1], *pieces = lax.optimization_barrier((pair[0], pair[1], *pieces))
    halo0 = lax.ppermute(pair[0], chips, row)
    halo1 = lax.ppermute(pair[1], chips, [p for p in row if p[0] % 16 != 15])

    slabs = compute_grads(scal, pieces, key_rows, value_rows, k_rec, v_rec, rates)
    fast0, pow0 = fast_apply(0, scal, pieces, queries, q_rec)
    half_sums = scatter_rings(slabs)
    pow0 = sum(with_parts(pow0, (CORES,)))
    half_sums, pow0 = lax.optimization_barrier((half_sums, pow0))
    other_sums = shift(half_sums, "yh", 1)
    powers0 = with_parts(pow0, (HALVES,))
    grad_both = half_sums.astype(f32) + other_sums[:, ::-1].astype(f32)
    grad_both, pair1, *powers0 = lax.optimization_barrier((grad_both, pair[1], *powers0))
    new_both = both - grad_both
    new16 = new_both[:, 0]
    pieces2 = gather_rings(new_both.astype(bf16))
    turned1 = lax.ppermute(pair1, chips, [(15, 16)])
    own_rows = lax.dynamic_slice_in_dim(new16, core * 8, 8, 2)
    their_rows = shift(lax.dynamic_slice_in_dim(new16, (1 - core) * 8, 8, 2), "core", 1)
    new_all = jnp.where(
        core == 0,
        jnp.concatenate([own_rows, their_rows], axis=0),
        jnp.concatenate([their_rows, own_rows], axis=0),
    )

    gain = lax.dynamic_slice_in_dim(out_gain, core * 1024, 1024, 0)[None]

    def complete(c, own, before, fast, powers, layer):
        args = (scal, queries, q_rec, own, before, fast, powers, gain)
        out_rec = finish(c, 1, *args)
        arrived = shift(out_rec, "core", 1)
        layer = finish(c, 0, *args, layer)
        return lax.dynamic_update_slice(layer, arrived[None], (c, 0, (1 - core) * 1024))

    local1 = attend_local(1, scal, queries, q_rec, pair[1])
    layer_out = complete(0, pair[0], [halo0], fast0, powers0, None)
    fast1, pow1 = fast_apply(1, scal, pieces2, queries, q_rec)
    powers1 = with_parts(pow1, (CORES, HALVES, ACROSS))
    layer_out = complete(1, local1, [halo1, turned1, halo0], fast1, powers1, layer_out)
    return layer_out, new_all[:, 0], new_all[:, 1], new_all[:, 2]


def solution(mesh):
    fine = Mesh(mesh.devices.reshape(2, 2, 4, 4, 2), ("heads",) + SEQ)
    rows = P(None, SEQ, "heads")
    weight = P("heads", SEQ, None)
    return jax.shard_map(
        on_device,
        mesh=fine,
        in_specs=(rows, rows, rows, P("heads", None, SEQ), weight, weight, weight, P("heads")),
        out_specs=(rows, weight, weight, weight),
        check_vma=False,
    )
```

```python
import functools

import jax
import jax.numpy as jnp
from jax import lax
from jax.experimental import pallas as pl
from jax.experimental.pallas import tpu as pltpu
from jax.sharding import Mesh, PartitionSpec as P

NORM_EPS = 1e-05
MASKED = -1e30
SIZES = {"heads": 2, "yh": 2, "z": 4, "x": 4, "core": 2}
SEQ = ("yh", "z", "x", "core")
TOK = 384
DH = 512
SCALE = DH ** -0.5

f32 = jnp.float32
bf16 = jnp.bfloat16


def shift(value, axis, steps):
    count = SIZES[axis]
    return lax.ppermute(value, axis, [(i, (i + steps) % count) for i in range(count)])


def dot(a, b, dims):
    return lax.dot_general(a, b, (dims, ((), ())), preferred_element_type=f32)


NN = ((1,), (0,))
NT = ((1,), (1,))
TN = ((0,), (0,))


def cparams(**kw):
    return pltpu.CompilerParams(vmem_limit_bytes=56 * 1024 * 1024, **kw)


def piece_rows(kind, part, idx, item, sign):
    yh, z, x = idx
    a, k = lax.rem(item, 2), lax.div(item, 2)
    y = lax.rem(yh + a, 2)
    zz = lax.rem(z + 4 + sign * (k if kind == 0 else part), 4)
    xx = lax.rem(x + 4 + sign * (part if kind == 0 else k), 4)
    return pl.multiple_of(y * 256 + zz * 64 + xx * 16, 16)


def load_weights(pieces, w_vmem, sem, idx, head_now, half):
    @pl.when((head_now == 0) & (half == 0))
    def _():
        for head in range(2):

            def start(item, carry, head=head):
                for part in range(4):
                    row = piece_rows(head, part, idx, item, 1)
                    pltpu.make_async_copy(
                        pieces[head * 4 + part].at[item],
                        w_vmem.at[head, :, pl.ds(row, 16), :],
                        sem.at[head],
                    ).start()
                return carry

            lax.fori_loop(0, 8, start, 0)

    for head in range(2):

        @pl.when((head_now == head) & (half == 0))
        def _(head=head):
            pltpu.make_async_copy(w_vmem.at[head], w_vmem.at[head], sem.at[head]).wait()


def grads_kernel(s_ref, *refs):
    pieces = refs[:8]
    k_own, v_own, k_rec, v_rec, r_ref = refs[8:13]
    outs = refs[13:21]
    w_vmem, held, sums, sem = refs[21:]
    head, half = pl.program_id(0), pl.program_id(1)
    idx = (s_ref[1], s_ref[2], s_ref[3])
    load_weights(pieces, w_vmem, sem, idx, head, half)
    gate, up, down = w_vmem[head, 0], w_vmem[head, 1], w_vmem[head, 2]
    k = jnp.where(half == 0, k_own[0], k_rec[0])
    v = jnp.where(half == 0, v_own[0], v_rec[0])
    target = (-(r_ref[0, half] * v.astype(f32))).astype(bf16)
    g = dot(k, gate, NN)
    u = dot(k, up, NN)
    back = dot(target, down, NT)
    s = jax.nn.sigmoid(g)
    silu = g * s
    rows = pl.ds(pl.multiple_of(half * TOK, TOK), TOK)
    held[0, rows] = k
    held[1, rows] = target
    held[2, rows] = (silu * u).astype(bf16)
    held[3, rows] = (back * u * s * (1.0 + g * (1.0 - s))).astype(bf16)
    held[4, rows] = (back * silu).astype(bf16)

    @pl.when(half == 1)
    def _():
        sums[0] = dot(held[0], held[3], TN)
        sums[1] = dot(held[0], held[4], TN)
        sums[2] = dot(held[2], held[1], TN)

    for kind in range(2):

        @pl.when((head == kind) & (half == 1))
        def _(kind=kind):
            def store(item, carry):
                for part in range(4):
                    row = piece_rows(kind, part, idx, item, -1)
                    for m in range(3):
                        outs[kind * 4 + part][item, m] = sums[m, pl.ds(row, 16), :].astype(bf16)
                return carry

            lax.fori_loop(0, 8, store, 0)


def own_spec(c):
    return pl.BlockSpec((1, TOK, DH), lambda *at: (c, 0, at[-1][0] * 2 + at[0]))


def rec_spec(c):
    return pl.BlockSpec((1, TOK, DH), lambda *at: (c, 0, at[0]))


ANY = pl.BlockSpec(memory_space=pl.ANY)


def compute_grads(scal, pieces, k, v, k_rec, v_rec, rates):
    whole = pl.BlockSpec((8, 3, 16, DH), lambda h, j, s: (0, 0, 0, 0))
    return pl.pallas_call(
        grads_kernel,
        name="fast_grads",
        out_shape=[jax.ShapeDtypeStruct((8, 3, 16, DH), bf16)] * 8,
        grid_spec=pltpu.PrefetchScalarGridSpec(
            num_scalar_prefetch=1,
            grid=(2, 2),
            in_specs=[ANY] * 8
            + [own_spec(0), own_spec(0), rec_spec(0), rec_spec(0)]
            + [pl.BlockSpec((1, 2, TOK, 1), lambda h, j, s: (h, 0, 0, 0))],
            out_specs=[whole] * 8,
            scratch_shapes=[
                pltpu.VMEM((2, 3, DH, DH), bf16),
                pltpu.VMEM((5, 2 * TOK, DH), bf16),
                pltpu.VMEM((3, DH, DH), f32),
                pltpu.SemaphoreType.DMA((2,)),
            ],
        ),
        compiler_params=cparams(),
    )(scal, *pieces, k, v, k_rec, v_rec, rates)


def apply_kernel(s_ref, *refs):
    pieces = refs[:8]
    q_own, q_rec = refs[8:10]
    out_ref, pow_ref = refs[10:12]
    w_vmem, sem = refs[12:]
    head, half = pl.program_id(0), pl.program_id(1)
    idx = (s_ref[1], s_ref[2], s_ref[3])
    load_weights(pieces, w_vmem, sem, idx, head, half)
    gate, up, down = w_vmem[head, 0], w_vmem[head, 1], w_vmem[head, 2]
    block = jnp.where(half == 0, s_ref[0], 1 - s_ref[0])
    q = jnp.where(half == 0, q_own[0], q_rec[0])
    g = dot(q, gate, NN)
    u = dot(q, up, NN)
    active = (g * jax.nn.sigmoid(g) * u).astype(bf16)
    out = dot(active, down, NN)
    out_ref[0] = out
    power = jnp.sum(out * out, axis=-1, keepdims=True)
    power = jnp.transpose(jnp.broadcast_to(power, (TOK, 128)))[:8]

    @pl.when(head == 0)
    def _():
        pow_ref[block] = power

    @pl.when(head == 1)
    def _():
        pow_ref[block] += power


def fast_apply(c, scal, pieces, q, q_rec):
    return pl.pallas_call(
        apply_kernel,
        name="fast_apply",
        out_shape=[
            jax.ShapeDtypeStruct((2, TOK, 2 * DH), f32),
            jax.ShapeDtypeStruct((2, 8, TOK), f32),
        ],
        grid_spec=pltpu.PrefetchScalarGridSpec(
            num_scalar_prefetch=1,
            grid=(2, 2),
            in_specs=[ANY] * 8 + [own_spec(c), rec_spec(c)],
            out_specs=[
                pl.BlockSpec((1, TOK, DH), lambda h, j, s: (j, 0, h)),
                pl.BlockSpec((2, 8, TOK), lambda h, j, s: (0, 0, 0)),
            ],
            scratch_shapes=[
                pltpu.VMEM((2, 3, DH, DH), bf16),
                pltpu.SemaphoreType.DMA((2,)),
            ],
        ),
        compiler_params=cparams(),
    )(scal, *pieces, q, q_rec)


LOG2E = 1.4426950408889634


def partial_attention(q, blocks):
    scores = []
    for k, _, mask in blocks:
        s = dot(q, k, NT)
        scores.append(s if mask is None else jnp.where(mask, s, MASKED))
    peak = jnp.max(functools.reduce(jnp.maximum, scores), axis=-1, keepdims=True)
    weights = [jnp.exp2((s - peak) * (SCALE * LOG2E)) for s in scores]
    total = jnp.sum(sum(weights[1:], weights[0]), axis=-1, keepdims=True)
    acc = sum(dot(w.astype(bf16), v, NN) for w, (_, v, _) in zip(weights, blocks))
    return acc, peak, total


def local_kernel(s_ref, qo, qr, kb, k2, vb, v2, acc_ref, stat_ref):
    block = pl.program_id(1)
    q = jnp.where(s_ref[0] == block, qo[0], qr[0])
    row = lax.broadcasted_iota(jnp.int32, (TOK, TOK), 0)
    col = lax.broadcasted_iota(jnp.int32, (TOK, TOK), 1)
    lane = lax.broadcasted_iota(jnp.int32, (TOK, 128), 1)
    for b in range(2):

        @pl.when(block == b)
        def _(b=b):
            blocks = [(k2[0], v2[0], col <= row)]
            if b == 1:
                blocks.append((kb[0], vb[0], None))
            acc, peak, total = partial_attention(q, blocks)
            acc_ref[0] = acc
            stat_ref[0, 0] = jnp.where(lane < 64, peak, total)


def attend_local(c, scal, q, q_rec, mine):
    def block(at):
        return pl.BlockSpec((1, TOK, DH), lambda h, b, s: (at(b), 0, h))

    return pl.pallas_call(
        local_kernel,
        name="attend_local",
        out_shape=[
            jax.ShapeDtypeStruct((2, TOK, 2 * DH), f32),
            jax.ShapeDtypeStruct((2, 2, TOK, 128), f32),
        ],
        grid_spec=pltpu.PrefetchScalarGridSpec(
            num_scalar_prefetch=1,
            grid=(2, 2),
            in_specs=[
                pl.BlockSpec((1, TOK, DH), lambda h, b, s: (c, 0, s[0] * 2 + h)),
                pl.BlockSpec((1, TOK, DH), lambda h, b, s: (c, 0, h)),
                block(lambda b: 0), block(lambda b: b), block(lambda b: 2), block(lambda b: 2 + b),
            ],
            out_specs=[
                pl.BlockSpec((1, TOK, DH), lambda h, b, s: (b, 0, h)),
                pl.BlockSpec((1, 1, TOK, 128), lambda h, b, s: (b, h, 0, 0)),
            ],
        ),
        compiler_params=cparams(),
    )(scal, q, q_rec, mine, mine, mine, mine)


def load_before(s_ref, before, block, kv, sem):
    head_now = pl.program_id(0)

    @pl.when(head_now == 0)
    def _():
        for i, array in enumerate(before):
            @pl.when(chosen(s_ref) == i)
            def _(array=array):
                for head in range(2):

                    def start(at, slot, head=head):
                        pltpu.make_async_copy(
                            array.at[at, :, pl.ds(head * DH, DH)], kv.at[head, slot], sem.at[head]
                        ).start()

                    start(block, 0)
                    start(2 + block, 1)

                    @pl.when(block == 0)
                    def _(start=start):
                        start(1, 2)
                        start(3, 3)

    for head in range(2):
        for b in range(2):

            @pl.when((head_now == head) & (block == b))
            def _(head=head, b=b):
                slots = kv.at[head, pl.ds(0, 4 - 2 * b)]
                pltpu.make_async_copy(slots, slots, sem.at[head]).wait()


def finish_kernel(c, j, sources, count, s_ref, *refs):
    core, chip = s_ref[0], s_ref[5]
    block = core if j == 0 else 1 - core
    q_ref, refs = refs[0], refs[1:]
    if c == 1:
        before, refs = refs[:sources], refs[sources:]
        kv, sem, refs = refs[-2], refs[-1], refs[:-2]
        load_before(s_ref, before, block, kv, sem)
    else:
        before, refs = refs[:4], refs[4:]
    own, refs = (refs[:4], refs[4:]) if c == 0 else (refs[:2], refs[2:])
    fast_ref, gain_ref = refs[:2]
    powers = refs[2 : 2 + count]
    out_ref = refs[-1]
    row = lax.broadcasted_iota(jnp.int32, (TOK, TOK), 0)
    col = lax.broadcasted_iota(jnp.int32, (TOK, TOK), 1)
    total = sum(p[0] for p in powers[1:]) + powers[0][0]
    rs = lax.rsqrt(total * (1.0 / 4096.0) + NORM_EPS)
    fast = fast_ref[0] * gain_ref[...] * jnp.transpose(rs)[:, :1]

    def put(attended):
        out_ref[...] = (fast + attended).astype(bf16).reshape(out_ref.shape)

    if c == 1:
        acc_ref, stat_ref = own

        head = pl.program_id(0)

        for b in range(2):

            @pl.when(block == b)
            def _(b=b):
                blocks = [(kv[head, 0], kv[head, 1], col > row)]
                if b == 0:
                    blocks.append((kv[head, 2], kv[head, 3], None))
                acc, peak, total = partial_attention(q_ref[0], blocks)
                peak_own, total_own = stat_ref[0, 0, :, :1], stat_ref[0, 0, :, 64:65]
                top = jnp.maximum(peak, peak_own)
                scale = jnp.exp2((peak - top) * (SCALE * LOG2E))
                scale_own = jnp.exp2((peak_own - top) * (SCALE * LOG2E))
                inv = 1.0 / (total * scale + total_own * scale_own)
                put(acc * (scale * inv) + acc_ref[0] * (scale_own * inv))

        return

    kb, k2, vb, v2 = own
    k0, ka, v0, va = before
    first = block == 0
    keys = (k0[0], jnp.where(first, ka[0], kb[0]), k2[0])
    values = (v0[0], jnp.where(first, va[0], vb[0]), v2[0])
    scores = [dot(q_ref[0], k, NT) for k in keys]
    low = jnp.where(chip == 0, TOK, row)
    scores[1] = jnp.where(col >= jnp.where((chip == 0) & first, TOK, 0), scores[1], MASKED)
    scores[0] = jnp.where(col > low, scores[0], MASKED)
    scores[2] = jnp.where(col <= row, scores[2], MASKED)
    peak = jnp.max(jnp.maximum(jnp.maximum(scores[0], scores[1]), scores[2]), axis=-1, keepdims=True)
    weights = [jnp.exp2((s - peak) * (SCALE * LOG2E)) for s in scores]
    inv = 1.0 / jnp.sum(weights[0] + weights[1] + weights[2], axis=-1, keepdims=True)
    put(sum(dot((w * inv).astype(bf16), v, NN) for w, v in zip(weights, values)))


def chosen(s):
    return jnp.where(s[5] == 0, 2, jnp.where(s[4] == 1, 1, 0))


def finish(c, j, scal, q, q_rec, own, before, fast, powers, gain, layer=None):
    def block(s):
        return s[0] if j == 0 else 1 - s[0]

    def always(at):
        return pl.BlockSpec((1, TOK, DH), lambda h, s: (at(s), 0, h))

    sources = len(before)
    q_spec = own_spec(c) if j == 0 else rec_spec(c)
    specs = [q_spec]
    operands = [q if j == 0 else q_rec]
    scratch = []
    if c == 0:
        specs += [always(block), always(lambda s: 1), always(lambda s: 2 + block(s)), always(lambda s: 3)]
        operands += before * 4
    else:
        specs += [ANY] * sources
        operands += before
        scratch = [pltpu.VMEM((2, 4, TOK, DH), bf16), pltpu.SemaphoreType.DMA((2,))]
    if c == 0:
        specs += [
            always(lambda s: 0), always(block), always(lambda s: 2), always(lambda s: 2 + block(s))
        ]
        operands += [own] * 4
    else:
        specs += [
            always(block), pl.BlockSpec((1, 1, TOK, 128), lambda h, s: (block(s), h, 0, 0))
        ]
        operands += list(own)
    specs += [
        pl.BlockSpec((1, TOK, DH), lambda h, s: (j, 0, h)),
        pl.BlockSpec((1, DH), lambda h, s: (0, h)),
    ]
    operands += [fast, gain]
    specs += [pl.BlockSpec((1, 8, TOK), lambda h, s: (block(s), 0, 0))] * len(powers)
    operands += powers
    aliases = {}
    if layer is not None:
        aliases = {len(operands) + 1: 0}
        specs.append(ANY)
        operands.append(layer)
    if j == 0:
        shape = (2, TOK, 4 * DH)
        out_spec = pl.BlockSpec((1, TOK, DH), lambda h, s: (c, 0, s[0] * 2 + h))
    else:
        shape = (TOK, 2 * DH)
        out_spec = pl.BlockSpec((TOK, DH), lambda h, s: (0, h))
    return pl.pallas_call(
        functools.partial(finish_kernel, c, j, sources, len(powers)),
        name="attend_finish",
        out_shape=jax.ShapeDtypeStruct(shape, bf16),
        grid_spec=pltpu.PrefetchScalarGridSpec(
            num_scalar_prefetch=1,
            grid=(2,),
            in_specs=specs,
            out_specs=out_spec,
            scratch_shapes=scratch,
        ),
        input_output_aliases=aliases,
        compiler_params=cparams(),
    )(scal, *operands)


def gather_direct(both):
    out = []
    for head, (first, last) in enumerate((("z", "x"), ("x", "z"))):
        v = both[head]
        v = jnp.concatenate([v] + [shift(v, first, -k) for k in range(1, 4)], axis=0)
        out.append([v] + [shift(v, last, -k) for k in range(1, 4)])
    return out[0] + out[1]


def gather_rings(both):
    axes = (("z", "x"), ("x", "z"))
    now = [both[h] for h in range(2)]
    held = [[n] for n in now]
    for _ in range(3):
        for h in range(2):
            now[h] = shift(now[h], axes[h][0], -1)
            held[h].append(now[h])
    now = [jnp.concatenate(held[h], axis=0) for h in range(2)]
    out = [[n] for n in now]
    for _ in range(3):
        for h in range(2):
            now[h] = shift(now[h], axes[h][1], -1)
            out[h].append(now[h])
    return out[0] + out[1]


def scatter_rings(slabs):
    axes = (("x", "z"), ("z", "x"))
    now = [slabs[3], slabs[7]]
    for k in (2, 1, 0):
        for h in range(2):
            got = shift(now[h], axes[h][0], -1)
            total = got.astype(f32) + slabs[h * 4 + k].astype(f32)
            now[h] = total.astype(bf16) if k else total
    parts = now
    now = [p[6:8].astype(bf16) for p in parts]
    for k in (2, 1, 0):
        for h in range(2):
            got = shift(now[h], axes[h][1], -1)
            now[h] = (got.astype(f32) + parts[h][2 * k : 2 * k + 2]).astype(bf16)
    return jnp.stack(now)


CORES = [(0, 1), (1, 0), (2, 3), (3, 2)]
HALVES = [(0, 2), (2, 0), (1, 3), (3, 1)]
ACROSS = [(0, 3), (3, 0), (1, 2), (2, 1)]


def with_parts(power, pairs):
    return [power] + [lax.ppermute(power, ("heads", "core"), p) for p in pairs]


def on_device(queries, key_rows, value_rows, step_rates, w_gate, w_up, w_down, out_gain):
    core = lax.axis_index("core")
    yh, z, x = lax.axis_index("yh"), lax.axis_index("z"), lax.axis_index("x")
    chip = (yh * 4 + z) * 4 + x
    turn = ((z == 0) & (x == 0)).astype(jnp.int32)
    scal = jnp.stack([core, yh, z, x, turn, chip]).astype(jnp.int32)

    masters = jnp.stack([w_gate, w_up, w_down], axis=1)
    mine = lax.dynamic_slice_in_dim(masters, core * 2, 2, 0)
    theirs = lax.dynamic_slice_in_dim(masters, (1 - core) * 2, 2, 0)
    got = shift(theirs, "core", 1)
    m16 = jnp.where(
        core == 0,
        jnp.concatenate([mine, got], axis=2),
        jnp.concatenate([got, mine], axis=2),
    )
    m16_other = shift(m16, "yh", 1)
    m16_other, key_rows, value_rows, queries, step_rates = lax.optimization_barrier(
        (m16_other, key_rows, value_rows, queries, step_rates)
    )
    both = jnp.stack([m16, m16_other], axis=1)
    pieces = gather_direct(both.astype(bf16))

    def split_in(a):
        keep = lax.dynamic_slice_in_dim(a, core * 1024, 1024, 2)
        give = lax.dynamic_slice_in_dim(a, (1 - core) * 1024, 1024, 2)
        return keep, shift(give, "core", 1)

    k_own, k_rec = split_in(key_rows)
    v_own, v_rec = split_in(value_rows)
    q_rec = split_in(queries)[1]
    rates = step_rates[:, 0, :]
    r_own = lax.dynamic_slice_in_dim(rates, core * 2, 2, 0)
    r_rec = shift(lax.dynamic_slice_in_dim(rates, (1 - core) * 2, 2, 0), "core", 1)
    rates = jnp.stack([r_own, r_rec], axis=1)[..., None]

    chips = ("yh", "z", "x")
    row = [(i, (i + 1) % 32) for i in range(32)]
    pair = [
        jnp.where(
            core == 0,
            jnp.stack([k_own[c], k_rec[c], v_own[c], v_rec[c]]),
            jnp.stack([k_rec[c], k_own[c], v_rec[c], v_own[c]]),
        )
        for c in range(2)
    ]
    pair[0], pair[1], *pieces = lax.optimization_barrier((pair[0], pair[1], *pieces))
    halo0 = lax.ppermute(pair[0], chips, row)
    halo1 = lax.ppermute(pair[1], chips, [p for p in row if p[0] % 16 != 15])

    slabs = compute_grads(scal, pieces, key_rows, value_rows, k_rec, v_rec, rates)
    fast0, pow0 = fast_apply(0, scal, pieces, queries, q_rec)
    half_sums = scatter_rings(slabs)
    pow0 = sum(with_parts(pow0, (CORES,)))
    half_sums, pow0 = lax.optimization_barrier((half_sums, pow0))
    other_sums = shift(half_sums, "yh", 1)
    powers0 = with_parts(pow0, (HALVES,))
    grad_both = half_sums.astype(f32) + other_sums[:, ::-1].astype(f32)
    grad_both, pair1, *powers0 = lax.optimization_barrier((grad_both, pair[1], *powers0))
    new_both = both - grad_both
    new16 = new_both[:, 0]
    pieces2 = gather_rings(new_both.astype(bf16))
    turned1 = lax.ppermute(pair1, chips, [(15, 16)])
    own_rows = lax.dynamic_slice_in_dim(new16, core * 8, 8, 2)
    their_rows = shift(lax.dynamic_slice_in_dim(new16, (1 - core) * 8, 8, 2), "core", 1)
    new_all = jnp.where(
        core == 0,
        jnp.concatenate([own_rows, their_rows], axis=0),
        jnp.concatenate([their_rows, own_rows], axis=0),
    )

    gain = lax.dynamic_slice_in_dim(out_gain, core * 1024, 1024, 0)[None]

    def complete(c, own, before, fast, powers, layer):
        args = (scal, queries, q_rec, own, before, fast, powers, gain)
        out_rec = finish(c, 1, *args)
        arrived = shift(out_rec, "core", 1)
        layer = finish(c, 0, *args, layer)
        return lax.dynamic_update_slice(layer, arrived[None], (c, 0, (1 - core) * 1024))

    local1 = attend_local(1, scal, queries, q_rec, pair[1])
    layer_out = complete(0, pair[0], [halo0], fast0, powers0, None)
    fast1, pow1 = fast_apply(1, scal, pieces2, queries, q_rec)
    powers1 = with_parts(pow1, (CORES, HALVES, ACROSS))
    layer_out = complete(1, local1, [halo1, turned1, halo0], fast1, powers1, layer_out)
    return layer_out, new_all[:, 0], new_all[:, 1], new_all[:, 2]


def solution(mesh):
    fine = Mesh(mesh.devices.reshape(2, 2, 4, 4, 2), ("heads",) + SEQ)
    rows = P(None, SEQ, "heads")
    weight = P("heads", SEQ, None)
    return jax.shard_map(
        on_device,
        mesh=fine,
        in_specs=(rows, rows, rows, P("heads", None, SEQ), weight, weight, weight, P("heads")),
        out_specs=(rows, weight, weight, weight),
        check_vma=False,
    )
```

```python
import functools

import jax
import jax.numpy as jnp
from jax import lax
from jax.experimental import pallas as pl
from jax.experimental.pallas import tpu as pltpu
from jax.sharding import Mesh, PartitionSpec as P

NORM_EPS = 1e-05
MASKED = -1e30
SIZES = {"heads": 2, "yh": 2, "z": 4, "x": 4, "core": 2}
SEQ = ("yh", "z", "x", "core")
TOK = 384
DH = 512
SCALE = DH ** -0.5

f32 = jnp.float32
bf16 = jnp.bfloat16


def shift(value, axis, steps):
    count = SIZES[axis]
    return lax.ppermute(value, axis, [(i, (i + steps) % count) for i in range(count)])


def dot(a, b, dims):
    return lax.dot_general(a, b, (dims, ((), ())), preferred_element_type=f32)


NN = ((1,), (0,))
NT = ((1,), (1,))
TN = ((0,), (0,))


def cparams(mib):
    return pltpu.CompilerParams(vmem_limit_bytes=mib * 1024 * 1024)


def piece_rows(kind, part, idx, item, sign):
    yh, z, x = idx
    a, k = lax.rem(item, 2), lax.div(item, 2)
    y = lax.rem(yh + a, 2)
    zz = lax.rem(z + 4 + sign * (k if kind == 0 else part), 4)
    xx = lax.rem(x + 4 + sign * (part if kind == 0 else k), 4)
    return pl.multiple_of(y * 256 + zz * 64 + xx * 16, 16)


def load_weights(pieces, w_vmem, sem, idx, head_now, half):
    @pl.when((head_now == 0) & (half == 0))
    def _():
        for head in range(2):

            def start(item, carry, head=head):
                for part in range(4):
                    row = piece_rows(head, part, idx, item, 1)
                    pltpu.make_async_copy(
                        pieces[head * 4 + part].at[item],
                        w_vmem.at[head, :, pl.ds(row, 16), :],
                        sem.at[head],
                    ).start()
                return carry

            lax.fori_loop(0, 8, start, 0)

    for head in range(2):

        @pl.when((head_now == head) & (half == 0))
        def _(head=head):
            pltpu.make_async_copy(w_vmem.at[head], w_vmem.at[head], sem.at[head]).wait()


def grads_kernel(s_ref, *refs):
    pieces = refs[:8]
    k_own, v_own, k_rec, v_rec, r_ref = refs[8:13]
    outs = refs[13:21]
    w_vmem, held, sums, sem = refs[21:]
    head, half = pl.program_id(0), pl.program_id(1)
    idx = (s_ref[1], s_ref[2], s_ref[3])
    load_weights(pieces, w_vmem, sem, idx, head, half)
    gate, up, down = w_vmem[head, 0], w_vmem[head, 1], w_vmem[head, 2]
    k = jnp.where(half == 0, k_own[0], k_rec[0])
    v = jnp.where(half == 0, v_own[0], v_rec[0])
    target = (-(r_ref[0, half] * v.astype(f32))).astype(bf16)
    g = dot(k, gate, NN)
    u = dot(k, up, NN)
    back = dot(target, down, NT)
    s = jax.nn.sigmoid(g)
    silu = g * s
    rows = pl.ds(pl.multiple_of(half * TOK, TOK), TOK)
    held[0, rows] = k
    held[1, rows] = target
    held[2, rows] = (silu * u).astype(bf16)
    held[3, rows] = (back * u * s * (1.0 + g * (1.0 - s))).astype(bf16)
    held[4, rows] = (back * silu).astype(bf16)

    @pl.when(half == 1)
    def _():
        sums[0] = dot(held[0], held[3], TN)
        sums[1] = dot(held[0], held[4], TN)
        sums[2] = dot(held[2], held[1], TN)

    for kind in range(2):

        @pl.when((head == kind) & (half == 1))
        def _(kind=kind):
            def store(item, carry):
                for part in range(4):
                    row = piece_rows(kind, part, idx, item, -1)
                    for m in range(3):
                        outs[kind * 4 + part][item, m] = sums[m, pl.ds(row, 16), :].astype(bf16)
                return carry

            lax.fori_loop(0, 8, store, 0)


def own_spec(c):
    return pl.BlockSpec((1, TOK, DH), lambda *at: (c, 0, at[-1][0] * 2 + at[0]))


def rec_spec(c):
    return pl.BlockSpec((1, TOK, DH), lambda *at: (c, 0, at[0]))


ANY = pl.BlockSpec(memory_space=pl.ANY)


def compute_grads(scal, pieces, k, v, k_rec, v_rec, rates):
    whole = pl.BlockSpec((8, 3, 16, DH), lambda h, j, s: (0, 0, 0, 0))
    return pl.pallas_call(
        grads_kernel,
        name="fast_grads",
        out_shape=[jax.ShapeDtypeStruct((8, 3, 16, DH), bf16)] * 8,
        grid_spec=pltpu.PrefetchScalarGridSpec(
            num_scalar_prefetch=1,
            grid=(2, 2),
            in_specs=[ANY] * 8
            + [own_spec(0), own_spec(0), rec_spec(0), rec_spec(0)]
            + [pl.BlockSpec((1, 2, TOK, 1), lambda h, j, s: (h, 0, 0, 0))],
            out_specs=[whole] * 8,
            scratch_shapes=[
                pltpu.VMEM((2, 3, DH, DH), bf16),
                pltpu.VMEM((5, 2 * TOK, DH), bf16),
                pltpu.VMEM((3, DH, DH), f32),
                pltpu.SemaphoreType.DMA((2,)),
            ],
        ),
        compiler_params=cparams(36),
    )(scal, *pieces, k, v, k_rec, v_rec, rates)


def apply_kernel(s_ref, *refs):
    pieces = refs[:8]
    q_own, q_rec = refs[8:10]
    out_ref, pow_ref = refs[10:12]
    w_vmem, sem = refs[12:]
    head, half = pl.program_id(0), pl.program_id(1)
    idx = (s_ref[1], s_ref[2], s_ref[3])
    load_weights(pieces, w_vmem, sem, idx, head, half)
    gate, up, down = w_vmem[head, 0], w_vmem[head, 1], w_vmem[head, 2]
    block = jnp.where(half == 0, s_ref[0], 1 - s_ref[0])
    q = jnp.where(half == 0, q_own[0], q_rec[0])
    g = dot(q, gate, NN)
    u = dot(q, up, NN)
    active = (g * jax.nn.sigmoid(g) * u).astype(bf16)
    out = dot(active, down, NN)
    out_ref[0] = out
    power = jnp.sum(out * out, axis=-1, keepdims=True)
    power = jnp.transpose(jnp.broadcast_to(power, (TOK, 128)))[:8]

    @pl.when(head == 0)
    def _():
        pow_ref[block] = power

    @pl.when(head == 1)
    def _():
        pow_ref[block] += power


def fast_apply(c, scal, pieces, q, q_rec):
    return pl.pallas_call(
        apply_kernel,
        name="fast_apply",
        out_shape=[
            jax.ShapeDtypeStruct((2, TOK, 2 * DH), f32),
            jax.ShapeDtypeStruct((2, 8, TOK), f32),
        ],
        grid_spec=pltpu.PrefetchScalarGridSpec(
            num_scalar_prefetch=1,
            grid=(2, 2),
            in_specs=[ANY] * 8 + [own_spec(c), rec_spec(c)],
            out_specs=[
                pl.BlockSpec((1, TOK, DH), lambda h, j, s: (j, 0, h)),
                pl.BlockSpec((2, 8, TOK), lambda h, j, s: (0, 0, 0)),
            ],
            scratch_shapes=[
                pltpu.VMEM((2, 3, DH, DH), bf16),
                pltpu.SemaphoreType.DMA((2,)),
            ],
        ),
        compiler_params=cparams(20),
    )(scal, *pieces, q, q_rec)


LOG2E = 1.4426950408889634


def partial_attention(q, blocks):
    scores = []
    for k, _, mask in blocks:
        s = dot(q, k, NT)
        scores.append(s if mask is None else jnp.where(mask, s, MASKED))
    peak = jnp.max(functools.reduce(jnp.maximum, scores), axis=-1, keepdims=True)
    weights = [jnp.exp2((s - peak) * (SCALE * LOG2E)) for s in scores]
    total = jnp.sum(sum(weights[1:], weights[0]), axis=-1, keepdims=True)
    acc = sum(dot(w.astype(bf16), v, NN) for w, (_, v, _) in zip(weights, blocks))
    return acc, peak, total


def local_kernel(s_ref, qo, qr, kb, k2, vb, v2, acc_ref, stat_ref):
    block = pl.program_id(1)
    q = jnp.where(s_ref[0] == block, qo[0], qr[0])
    row = lax.broadcasted_iota(jnp.int32, (TOK, TOK), 0)
    col = lax.broadcasted_iota(jnp.int32, (TOK, TOK), 1)
    lane = lax.broadcasted_iota(jnp.int32, (TOK, 128), 1)
    for b in range(2):

        @pl.when(block == b)
        def _(b=b):
            blocks = [(k2[0], v2[0], col <= row)]
            if b == 1:
                blocks.append((kb[0], vb[0], None))
            acc, peak, total = partial_attention(q, blocks)
            acc_ref[0] = acc
            stat_ref[0, 0] = jnp.where(lane < 64, peak, total)


def attend_local(c, scal, q, q_rec, mine):
    def block(at):
        return pl.BlockSpec((1, TOK, DH), lambda h, b, s: (at(b), 0, h))

    return pl.pallas_call(
        local_kernel,
        name="attend_local",
        out_shape=[
            jax.ShapeDtypeStruct((2, TOK, 2 * DH), f32),
            jax.ShapeDtypeStruct((2, 2, TOK, 128), f32),
        ],
        grid_spec=pltpu.PrefetchScalarGridSpec(
            num_scalar_prefetch=1,
            grid=(2, 2),
            in_specs=[
                pl.BlockSpec((1, TOK, DH), lambda h, b, s: (c, 0, s[0] * 2 + h)),
                pl.BlockSpec((1, TOK, DH), lambda h, b, s: (c, 0, h)),
                block(lambda b: 0), block(lambda b: b), block(lambda b: 2), block(lambda b: 2 + b),
            ],
            out_specs=[
                pl.BlockSpec((1, TOK, DH), lambda h, b, s: (b, 0, h)),
                pl.BlockSpec((1, 1, TOK, 128), lambda h, b, s: (b, h, 0, 0)),
            ],
        ),
        compiler_params=cparams(24),
    )(scal, q, q_rec, mine, mine, mine, mine)


def tail_kernel(s_ref, *refs):
    before, (qo, qr, acc_ref, stat_ref, out_ref, kv, sem) = refs[:3], refs[3:]
    head, block = pl.program_id(0), pl.program_id(1)

    @pl.when((head == 0) & (block == 0))
    def _():
        for i, array in enumerate(before):
            @pl.when(chosen(s_ref) == i)
            def _(array=array):
                for h in range(2):
                    pltpu.make_async_copy(
                        array.at[:, :, pl.ds(h * DH, DH)], kv.at[h], sem.at[h]
                    ).start()

    for h in range(2):

        @pl.when((head == h) & (block == 0))
        def _(h=h):
            pltpu.make_async_copy(kv.at[h], kv.at[h], sem.at[h]).wait()

    q = jnp.where(s_ref[0] == block, qo[0], qr[0])
    row = lax.broadcasted_iota(jnp.int32, (TOK, TOK), 0)
    col = lax.broadcasted_iota(jnp.int32, (TOK, TOK), 1)
    for b in range(2):

        @pl.when(block == b)
        def _(b=b):
            blocks = [(kv[head, b], kv[head, 2 + b], col > row)]
            if b == 0:
                blocks.append((kv[head, 1], kv[head, 3], None))
            acc, peak, total = partial_attention(q, blocks)
            peak_own, total_own = stat_ref[0, 0, :, :1], stat_ref[0, 0, :, 64:65]
            top = jnp.maximum(peak, peak_own)
            scale = jnp.exp2((peak - top) * (SCALE * LOG2E))
            scale_own = jnp.exp2((peak_own - top) * (SCALE * LOG2E))
            inv = 1.0 / (total * scale + total_own * scale_own)
            out_ref[0] = acc * (scale * inv) + acc_ref[0] * (scale_own * inv)


def attend_tail(c, scal, q, q_rec, local, before):
    return pl.pallas_call(
        tail_kernel,
        name="attend_tail",
        out_shape=jax.ShapeDtypeStruct((2, TOK, 2 * DH), f32),
        grid_spec=pltpu.PrefetchScalarGridSpec(
            num_scalar_prefetch=1,
            grid=(2, 2),
            in_specs=[ANY] * 3
            + [
                pl.BlockSpec((1, TOK, DH), lambda h, b, s: (c, 0, s[0] * 2 + h)),
                pl.BlockSpec((1, TOK, DH), lambda h, b, s: (c, 0, h)),
                pl.BlockSpec((1, TOK, DH), lambda h, b, s: (b, 0, h)),
                pl.BlockSpec((1, 1, TOK, 128), lambda h, b, s: (b, h, 0, 0)),
            ],
            out_specs=pl.BlockSpec((1, TOK, DH), lambda h, b, s: (b, 0, h)),
            scratch_shapes=[pltpu.VMEM((2, 4, TOK, DH), bf16), pltpu.SemaphoreType.DMA((2,))],
        ),
        compiler_params=cparams(24),
    )(scal, *before, q, q_rec, *local)


def norm_kernel(j, count, s_ref, fast_ref, att_ref, gain_ref, *refs):
    powers, out_ref = refs[:count], refs[-1]
    block = s_ref[0] if j == 0 else 1 - s_ref[0]
    total = sum((p[block] for p in powers[1:]), powers[0][block])
    rs = lax.rsqrt(total * (1.0 / 4096.0) + NORM_EPS)
    col = jnp.transpose(rs)[:, :1]
    out_ref[...] = (fast_ref[j] * gain_ref[...] * col + att_ref[block]).astype(bf16)


def norm_add(j, scal, fast, att, gain, powers):
    whole = pl.BlockSpec(memory_space=pltpu.VMEM)
    return pl.pallas_call(
        functools.partial(norm_kernel, j, len(powers)),
        name="norm_add",
        out_shape=jax.ShapeDtypeStruct((TOK, 2 * DH), bf16),
        in_specs=[pl.BlockSpec(memory_space=pltpu.SMEM)] + [whole] * (3 + len(powers)),
        out_specs=whole,
        compiler_params=cparams(20),
    )(scal, fast, att, gain, *powers)


def finish_kernel(j, count, s_ref, *refs):
    core, chip = s_ref[0], s_ref[5]
    block = core if j == 0 else 1 - core
    q_ref, before, own, refs = refs[0], refs[1:5], refs[5:9], refs[9:]
    fast_ref, gain_ref = refs[:2]
    powers = refs[2 : 2 + count]
    out_ref = refs[-1]
    row = lax.broadcasted_iota(jnp.int32, (TOK, TOK), 0)
    col = lax.broadcasted_iota(jnp.int32, (TOK, TOK), 1)
    total = sum(p[0] for p in powers[1:]) + powers[0][0]
    rs = lax.rsqrt(total * (1.0 / 4096.0) + NORM_EPS)
    fast = fast_ref[0] * gain_ref[...] * jnp.transpose(rs)[:, :1]

    def put(attended):
        out_ref[...] = (fast + attended).astype(bf16).reshape(out_ref.shape)

    kb, k2, vb, v2 = own
    k0, ka, v0, va = before
    first = block == 0
    keys = (k0[0], jnp.where(first, ka[0], kb[0]), k2[0])
    values = (v0[0], jnp.where(first, va[0], vb[0]), v2[0])
    scores = [dot(q_ref[0], k, NT) for k in keys]
    low = jnp.where(chip == 0, TOK, row)
    scores[1] = jnp.where(col >= jnp.where((chip == 0) & first, TOK, 0), scores[1], MASKED)
    scores[0] = jnp.where(col > low, scores[0], MASKED)
    scores[2] = jnp.where(col <= row, scores[2], MASKED)
    peak = jnp.max(jnp.maximum(jnp.maximum(scores[0], scores[1]), scores[2]), axis=-1, keepdims=True)
    weights = [jnp.exp2((s - peak) * (SCALE * LOG2E)) for s in scores]
    inv = 1.0 / jnp.sum(weights[0] + weights[1] + weights[2], axis=-1, keepdims=True)
    put(sum(dot((w * inv).astype(bf16), v, NN) for w, v in zip(weights, values)))


def chosen(s):
    return jnp.where(s[5] == 0, 2, jnp.where(s[4] == 1, 1, 0))


def finish(c, j, scal, q, q_rec, own, before, fast, powers, gain, layer=None):
    def block(s):
        return s[0] if j == 0 else 1 - s[0]

    def spec(at, holds=lambda s: True):
        return pl.BlockSpec(
            (1, TOK, DH),
            lambda h, s: (jnp.where(holds(s), at(s), 0), 0, jnp.where(holds(s), h, 0)),
        )

    def always(at):
        return pl.BlockSpec((1, TOK, DH), lambda h, s: (at(s), 0, h))

    sources = len(before)
    q_spec = own_spec(c) if j == 0 else rec_spec(c)
    specs = [q_spec]
    operands = [q if j == 0 else q_rec]
    for i, array in enumerate(before):
        holds = (lambda s, i=i: chosen(s) == i) if sources > 1 else (lambda s: True)
        specs += [
            spec(block, holds), spec(lambda s: 1, holds),
            spec(lambda s: 2 + block(s), holds), spec(lambda s: 3, holds),
        ]
        operands += [array] * 4
    if c == 0:
        specs += [
            always(lambda s: 0), always(block), always(lambda s: 2), always(lambda s: 2 + block(s))
        ]
        operands += [own] * 4
    else:
        specs += [
            always(block), pl.BlockSpec((1, 1, TOK, 128), lambda h, s: (block(s), h, 0, 0))
        ]
        operands += list(own)
    specs += [
        pl.BlockSpec((1, TOK, DH), lambda h, s: (j, 0, h)),
        pl.BlockSpec((1, DH), lambda h, s: (0, h)),
    ]
    operands += [fast, gain]
    specs += [pl.BlockSpec((1, 8, TOK), lambda h, s: (block(s), 0, 0))] * len(powers)
    operands += powers
    aliases = {}
    if layer is not None:
        aliases = {len(operands) + 1: 0}
        specs.append(ANY)
        operands.append(layer)
    if j == 0:
        shape = (2, TOK, 4 * DH)
        out_spec = pl.BlockSpec((1, TOK, DH), lambda h, s: (c, 0, s[0] * 2 + h))
    else:
        shape = (TOK, 2 * DH)
        out_spec = pl.BlockSpec((TOK, DH), lambda h, s: (0, h))
    return pl.pallas_call(
        functools.partial(finish_kernel, j, len(powers)),
        name="attend_finish",
        out_shape=jax.ShapeDtypeStruct(shape, bf16),
        grid_spec=pltpu.PrefetchScalarGridSpec(
            num_scalar_prefetch=1, grid=(2,), in_specs=specs, out_specs=out_spec
        ),
        input_output_aliases=aliases,
        compiler_params=cparams(24),
    )(scal, *operands)


def gather_direct(both):
    out = []
    for head, (first, last) in enumerate((("z", "x"), ("x", "z"))):
        v = both[head]
        v = jnp.concatenate([v] + [shift(v, first, -k) for k in range(1, 4)], axis=0)
        out.append([v] + [shift(v, last, -k) for k in range(1, 4)])
    return out[0] + out[1]


def gather_rings(both):
    axes = (("z", "x"), ("x", "z"))
    now = [both[h] for h in range(2)]
    held = [[n] for n in now]
    for _ in range(3):
        for h in range(2):
            now[h] = shift(now[h], axes[h][0], -1)
            held[h].append(now[h])
    now = [jnp.concatenate(held[h], axis=0) for h in range(2)]
    out = [[n] for n in now]
    for _ in range(3):
        for h in range(2):
            now[h] = shift(now[h], axes[h][1], -1)
            out[h].append(now[h])
    return out[0] + out[1]


def scatter_rings(slabs):
    axes = (("x", "z"), ("z", "x"))
    now = [slabs[3], slabs[7]]
    for k in (2, 1, 0):
        for h in range(2):
            got = shift(now[h], axes[h][0], -1)
            total = got.astype(f32) + slabs[h * 4 + k].astype(f32)
            now[h] = total.astype(bf16) if k else total
    parts = now
    now = [p[6:8].astype(bf16) for p in parts]
    for k in (2, 1, 0):
        for h in range(2):
            got = shift(now[h], axes[h][1], -1)
            now[h] = (got.astype(f32) + parts[h][2 * k : 2 * k + 2]).astype(bf16)
    return jnp.stack(now)


CORES = [(0, 1), (1, 0), (2, 3), (3, 2)]
HALVES = [(0, 2), (2, 0), (1, 3), (3, 1)]
ACROSS = [(0, 3), (3, 0), (1, 2), (2, 1)]


def with_parts(power, pairs):
    return [power] + [lax.ppermute(power, ("heads", "core"), p) for p in pairs]


def on_device(queries, key_rows, value_rows, step_rates, w_gate, w_up, w_down, out_gain):
    core = lax.axis_index("core")
    yh, z, x = lax.axis_index("yh"), lax.axis_index("z"), lax.axis_index("x")
    chip = (yh * 4 + z) * 4 + x
    turn = ((z == 0) & (x == 0)).astype(jnp.int32)
    scal = jnp.stack([core, yh, z, x, turn, chip]).astype(jnp.int32)

    masters = jnp.stack([w_gate, w_up, w_down], axis=1)
    mine = lax.dynamic_slice_in_dim(masters, core * 2, 2, 0)
    theirs = lax.dynamic_slice_in_dim(masters, (1 - core) * 2, 2, 0)
    got = shift(theirs, "core", 1)
    m16 = jnp.where(
        core == 0,
        jnp.concatenate([mine, got], axis=2),
        jnp.concatenate([got, mine], axis=2),
    )
    m16_other = shift(m16, "yh", 1)
    m16_other, key_rows, value_rows, queries, step_rates = lax.optimization_barrier(
        (m16_other, key_rows, value_rows, queries, step_rates)
    )
    both = jnp.stack([m16, m16_other], axis=1)
    pieces = gather_direct(both.astype(bf16))

    def split_in(a):
        keep = lax.dynamic_slice_in_dim(a, core * 1024, 1024, 2)
        give = lax.dynamic_slice_in_dim(a, (1 - core) * 1024, 1024, 2)
        return keep, shift(give, "core", 1)

    k_own, k_rec = split_in(key_rows)
    v_own, v_rec = split_in(value_rows)
    q_rec = split_in(queries)[1]
    rates = step_rates[:, 0, :]
    r_own = lax.dynamic_slice_in_dim(rates, core * 2, 2, 0)
    r_rec = shift(lax.dynamic_slice_in_dim(rates, (1 - core) * 2, 2, 0), "core", 1)
    rates = jnp.stack([r_own, r_rec], axis=1)[..., None]

    chips = ("yh", "z", "x")
    row = [(i, (i + 1) % 32) for i in range(32)]
    pair = [
        jnp.where(
            core == 0,
            jnp.stack([k_own[c], k_rec[c], v_own[c], v_rec[c]]),
            jnp.stack([k_rec[c], k_own[c], v_rec[c], v_own[c]]),
        )
        for c in range(2)
    ]
    pair[0], pair[1], *pieces = lax.optimization_barrier((pair[0], pair[1], *pieces))
    halo0 = lax.ppermute(pair[0], chips, row)
    halo1 = lax.ppermute(pair[1], chips, [p for p in row if p[0] % 16 != 15])

    slabs = compute_grads(scal, pieces, key_rows, value_rows, k_rec, v_rec, rates)
    fast0, pow0 = fast_apply(0, scal, pieces, queries, q_rec)
    half_sums = scatter_rings(slabs)
    pow0 = sum(with_parts(pow0, (CORES,)))
    half_sums, pow0 = lax.optimization_barrier((half_sums, pow0))
    other_sums = shift(half_sums, "yh", 1)
    powers0 = with_parts(pow0, (HALVES,))
    grad_both = half_sums.astype(f32) + other_sums[:, ::-1].astype(f32)
    grad_both, pair1, *powers0 = lax.optimization_barrier((grad_both, pair[1], *powers0))
    new_both = both - grad_both
    new16 = new_both[:, 0]
    pieces2 = gather_rings(new_both.astype(bf16))
    turned1 = lax.ppermute(pair1, chips, [(15, 16)])
    own_rows = lax.dynamic_slice_in_dim(new16, core * 8, 8, 2)
    their_rows = shift(lax.dynamic_slice_in_dim(new16, (1 - core) * 8, 8, 2), "core", 1)
    new_all = jnp.where(
        core == 0,
        jnp.concatenate([own_rows, their_rows], axis=0),
        jnp.concatenate([their_rows, own_rows], axis=0),
    )

    gain = lax.dynamic_slice_in_dim(out_gain, core * 1024, 1024, 0)[None]

    def complete(c, own, before, fast, powers, layer):
        args = (scal, queries, q_rec, own, before, fast, powers, gain)
        out_rec = finish(c, 1, *args)
        arrived = shift(out_rec, "core", 1)
        layer = finish(c, 0, *args, layer)
        return lax.dynamic_update_slice(layer, arrived[None], (c, 0, (1 - core) * 1024))

    local1 = attend_local(1, scal, queries, q_rec, pair[1])
    layer_out = complete(0, pair[0], [halo0], fast0, powers0, None)
    fast1, pow1 = fast_apply(1, scal, pieces2, queries, q_rec)
    powers1 = with_parts(pow1, (CORES, HALVES, ACROSS))
    att1 = attend_tail(1, scal, queries, q_rec, local1, [halo1, turned1, halo0])
    out_rec = norm_add(1, scal, fast1, att1, gain, powers1)
    arrived = shift(out_rec, "core", 1)
    out_own = norm_add(0, scal, fast1, att1, gain, powers1)
    layer_out = lax.dynamic_update_slice(layer_out, out_own[None], (1, 0, core * 1024))
    layer_out = lax.dynamic_update_slice(layer_out, arrived[None], (1, 0, (1 - core) * 1024))
    return layer_out, new_all[:, 0], new_all[:, 1], new_all[:, 2]


def solution(mesh):
    fine = Mesh(mesh.devices.reshape(2, 2, 4, 4, 2), ("heads",) + SEQ)
    rows = P(None, SEQ, "heads")
    weight = P("heads", SEQ, None)
    return jax.shard_map(
        on_device,
        mesh=fine,
        in_specs=(rows, rows, rows, P("heads", None, SEQ), weight, weight, weight, P("heads")),
        out_specs=(rows, weight, weight, weight),
        check_vma=False,
    )
```

```python
import functools

import jax
import jax.numpy as jnp
from jax import lax
from jax.experimental import pallas as pl
from jax.experimental.pallas import tpu as pltpu
from jax.sharding import Mesh, PartitionSpec as P

NORM_EPS = 1e-05
MASKED = -1e30
SIZES = {"heads": 2, "yh": 2, "z": 4, "x": 4, "core": 2}
SEQ = ("yh", "z", "x", "core")
TOK = 384
DH = 512
SCALE = DH ** -0.5

f32 = jnp.float32
bf16 = jnp.bfloat16


def shift(value, axis, steps):
    count = SIZES[axis]
    return lax.ppermute(value, axis, [(i, (i + steps) % count) for i in range(count)])


def dot(a, b, dims):
    return lax.dot_general(a, b, (dims, ((), ())), preferred_element_type=f32)


NN = ((1,), (0,))
NT = ((1,), (1,))
TN = ((0,), (0,))


def cparams(mib):
    return pltpu.CompilerParams(vmem_limit_bytes=mib * 1024 * 1024)


def piece_rows(kind, part, idx, item, sign):
    yh, z, x = idx
    a, k = lax.rem(item, 2), lax.div(item, 2)
    y = lax.rem(yh + a, 2)
    zz = lax.rem(z + 4 + sign * (k if kind == 0 else part), 4)
    xx = lax.rem(x + 4 + sign * (part if kind == 0 else k), 4)
    return pl.multiple_of(y * 256 + zz * 64 + xx * 16, 16)


def load_weights(pieces, w_vmem, sem, idx, head_now, half):
    @pl.when((head_now == 0) & (half == 0))
    def _():
        for head in range(2):

            def start(item, carry, head=head):
                for part in range(4):
                    row = piece_rows(head, part, idx, item, 1)
                    pltpu.make_async_copy(
                        pieces[head * 4 + part].at[item],
                        w_vmem.at[head, :, pl.ds(row, 16), :],
                        sem.at[head],
                    ).start()
                return carry

            lax.fori_loop(0, 8, start, 0)

    for head in range(2):

        @pl.when((head_now == head) & (half == 0))
        def _(head=head):
            pltpu.make_async_copy(w_vmem.at[head], w_vmem.at[head], sem.at[head]).wait()


def grads_kernel(s_ref, *refs):
    pieces = refs[:8]
    k_own, v_own, k_rec, v_rec, r_ref = refs[8:13]
    outs = refs[13:21]
    w_vmem, held, sums, sem = refs[21:]
    head, half = pl.program_id(0), pl.program_id(1)
    idx = (s_ref[1], s_ref[2], s_ref[3])
    load_weights(pieces, w_vmem, sem, idx, head, half)
    gate, up, down = w_vmem[head, 0], w_vmem[head, 1], w_vmem[head, 2]
    k = jnp.where(half == 0, k_own[0], k_rec[0])
    v = jnp.where(half == 0, v_own[0], v_rec[0])
    target = (-(r_ref[0, half] * v.astype(f32))).astype(bf16)
    g = dot(k, gate, NN)
    u = dot(k, up, NN)
    back = dot(target, down, NT)
    s = jax.nn.sigmoid(g)
    silu = g * s
    rows = pl.ds(pl.multiple_of(half * TOK, TOK), TOK)
    held[0, rows] = k
    held[1, rows] = target
    held[2, rows] = (silu * u).astype(bf16)
    held[3, rows] = (back * u * s * (1.0 + g * (1.0 - s))).astype(bf16)
    held[4, rows] = (back * silu).astype(bf16)

    @pl.when(half == 1)
    def _():
        sums[0] = dot(held[0], held[3], TN)
        sums[1] = dot(held[0], held[4], TN)
        sums[2] = dot(held[2], held[1], TN)

    for kind in range(2):

        @pl.when((head == kind) & (half == 1))
        def _(kind=kind):
            def store(item, carry):
                for part in range(4):
                    row = piece_rows(kind, part, idx, item, -1)
                    for m in range(3):
                        outs[kind * 4 + part][item, m] = sums[m, pl.ds(row, 16), :].astype(bf16)
                return carry

            lax.fori_loop(0, 8, store, 0)


def own_spec(c):
    return pl.BlockSpec((1, TOK, DH), lambda *at: (c, 0, at[-1][0] * 2 + at[0]))


def rec_spec(c):
    return pl.BlockSpec((1, TOK, DH), lambda *at: (c, 0, at[0]))


ANY = pl.BlockSpec(memory_space=pl.ANY)


def compute_grads(scal, pieces, k, v, k_rec, v_rec, rates):
    whole = pl.BlockSpec((8, 3, 16, DH), lambda h, j, s: (0, 0, 0, 0))
    return pl.pallas_call(
        grads_kernel,
        name="fast_grads",
        out_shape=[jax.ShapeDtypeStruct((8, 3, 16, DH), bf16)] * 8,
        grid_spec=pltpu.PrefetchScalarGridSpec(
            num_scalar_prefetch=1,
            grid=(2, 2),
            in_specs=[ANY] * 8
            + [own_spec(0), own_spec(0), rec_spec(0), rec_spec(0)]
            + [pl.BlockSpec((1, 2, TOK, 1), lambda h, j, s: (h, 0, 0, 0))],
            out_specs=[whole] * 8,
            scratch_shapes=[
                pltpu.VMEM((2, 3, DH, DH), bf16),
                pltpu.VMEM((5, 2 * TOK, DH), bf16),
                pltpu.VMEM((3, DH, DH), f32),
                pltpu.SemaphoreType.DMA((2,)),
            ],
        ),
        compiler_params=cparams(36),
    )(scal, *pieces, k, v, k_rec, v_rec, rates)


def apply_kernel(s_ref, *refs):
    pieces = refs[:8]
    q_own, q_rec = refs[8:10]
    out_ref, pow_ref = refs[10:12]
    w_vmem, sem = refs[12:]
    head, half = pl.program_id(0), pl.program_id(1)
    idx = (s_ref[1], s_ref[2], s_ref[3])
    load_weights(pieces, w_vmem, sem, idx, head, half)
    gate, up, down = w_vmem[head, 0], w_vmem[head, 1], w_vmem[head, 2]
    block = jnp.where(half == 0, s_ref[0], 1 - s_ref[0])
    q = jnp.where(half == 0, q_own[0], q_rec[0])
    g = dot(q, gate, NN)
    u = dot(q, up, NN)
    active = (g * jax.nn.sigmoid(g) * u).astype(bf16)
    out = dot(active, down, NN)
    out_ref[0] = out
    power = jnp.sum(out * out, axis=-1, keepdims=True)
    power = jnp.transpose(jnp.broadcast_to(power, (TOK, 128)))[:8]

    @pl.when(head == 0)
    def _():
        pow_ref[block] = power

    @pl.when(head == 1)
    def _():
        pow_ref[block] += power


def fast_apply(c, scal, pieces, q, q_rec):
    return pl.pallas_call(
        apply_kernel,
        name="fast_apply",
        out_shape=[
            jax.ShapeDtypeStruct((2, TOK, 2 * DH), f32),
            jax.ShapeDtypeStruct((2, 8, TOK), f32),
        ],
        grid_spec=pltpu.PrefetchScalarGridSpec(
            num_scalar_prefetch=1,
            grid=(2, 2),
            in_specs=[ANY] * 8 + [own_spec(c), rec_spec(c)],
            out_specs=[
                pl.BlockSpec((1, TOK, DH), lambda h, j, s: (j, 0, h)),
                pl.BlockSpec((2, 8, TOK), lambda h, j, s: (0, 0, 0)),
            ],
            scratch_shapes=[
                pltpu.VMEM((2, 3, DH, DH), bf16),
                pltpu.SemaphoreType.DMA((2,)),
            ],
        ),
        compiler_params=cparams(20),
    )(scal, *pieces, q, q_rec)


LOG2E = 1.4426950408889634


def partial_attention(q, blocks):
    scores = []
    for k, _, mask in blocks:
        s = dot(q, k, NT)
        scores.append(s if mask is None else jnp.where(mask, s, MASKED))
    peak = jnp.max(functools.reduce(jnp.maximum, scores), axis=-1, keepdims=True)
    weights = [jnp.exp2((s - peak) * (SCALE * LOG2E)) for s in scores]
    total = jnp.sum(sum(weights[1:], weights[0]), axis=-1, keepdims=True)
    acc = sum(dot(w.astype(bf16), v, NN) for w, (_, v, _) in zip(weights, blocks))
    return acc, peak, total


def local_kernel(s_ref, qo, qr, kb, k2, vb, v2, acc_ref, stat_ref):
    block = pl.program_id(1)
    q = jnp.where(s_ref[0] == block, qo[0], qr[0])
    row = lax.broadcasted_iota(jnp.int32, (TOK, TOK), 0)
    col = lax.broadcasted_iota(jnp.int32, (TOK, TOK), 1)
    lane = lax.broadcasted_iota(jnp.int32, (TOK, 128), 1)
    for b in range(2):

        @pl.when(block == b)
        def _(b=b):
            blocks = [(k2[0], v2[0], col <= row)]
            if b == 1:
                blocks.append((kb[0], vb[0], None))
            acc, peak, total = partial_attention(q, blocks)
            acc_ref[0] = acc
            stat_ref[0, 0] = jnp.where(lane < 64, peak, total)


def attend_local(c, scal, q, q_rec, mine):
    def block(at):
        return pl.BlockSpec((1, TOK, DH), lambda h, b, s: (at(b), 0, h))

    return pl.pallas_call(
        local_kernel,
        name="attend_local",
        out_shape=[
            jax.ShapeDtypeStruct((2, TOK, 2 * DH), f32),
            jax.ShapeDtypeStruct((2, 2, TOK, 128), f32),
        ],
        grid_spec=pltpu.PrefetchScalarGridSpec(
            num_scalar_prefetch=1,
            grid=(2, 2),
            in_specs=[
                pl.BlockSpec((1, TOK, DH), lambda h, b, s: (c, 0, s[0] * 2 + h)),
                pl.BlockSpec((1, TOK, DH), lambda h, b, s: (c, 0, h)),
                block(lambda b: 0), block(lambda b: b), block(lambda b: 2), block(lambda b: 2 + b),
            ],
            out_specs=[
                pl.BlockSpec((1, TOK, DH), lambda h, b, s: (b, 0, h)),
                pl.BlockSpec((1, 1, TOK, 128), lambda h, b, s: (b, h, 0, 0)),
            ],
        ),
        compiler_params=cparams(24),
    )(scal, q, q_rec, mine, mine, mine, mine)


def tail_kernel(s_ref, *refs):
    before, (qo, qr, acc_ref, stat_ref, out_ref, kv, sem) = refs[:3], refs[3:]
    head, block = pl.program_id(0), pl.program_id(1)

    @pl.when((head == 0) & (block == 0))
    def _():
        for i, array in enumerate(before):
            @pl.when(chosen(s_ref) == i)
            def _(array=array):
                for h in range(2):
                    pltpu.make_async_copy(
                        array.at[:, :, pl.ds(h * DH, DH)], kv.at[h], sem.at[h]
                    ).start()

    for h in range(2):

        @pl.when((head == h) & (block == 0))
        def _(h=h):
            pltpu.make_async_copy(kv.at[h], kv.at[h], sem.at[h]).wait()

    q = jnp.where(s_ref[0] == block, qo[0], qr[0])
    row = lax.broadcasted_iota(jnp.int32, (TOK, TOK), 0)
    col = lax.broadcasted_iota(jnp.int32, (TOK, TOK), 1)
    for b in range(2):

        @pl.when(block == b)
        def _(b=b):
            blocks = [(kv[head, b], kv[head, 2 + b], col > row)]
            if b == 0:
                blocks.append((kv[head, 1], kv[head, 3], None))
            acc, peak, total = partial_attention(q, blocks)
            peak_own, total_own = stat_ref[0, 0, :, :1], stat_ref[0, 0, :, 64:65]
            top = jnp.maximum(peak, peak_own)
            scale = jnp.exp2((peak - top) * (SCALE * LOG2E))
            scale_own = jnp.exp2((peak_own - top) * (SCALE * LOG2E))
            inv = 1.0 / (total * scale + total_own * scale_own)
            out_ref[0] = acc * (scale * inv) + acc_ref[0] * (scale_own * inv)


def attend_tail(c, scal, q, q_rec, local, before):
    return pl.pallas_call(
        tail_kernel,
        name="attend_tail",
        out_shape=jax.ShapeDtypeStruct((2, TOK, 2 * DH), f32),
        grid_spec=pltpu.PrefetchScalarGridSpec(
            num_scalar_prefetch=1,
            grid=(2, 2),
            in_specs=[ANY] * 3
            + [
                pl.BlockSpec((1, TOK, DH), lambda h, b, s: (c, 0, s[0] * 2 + h)),
                pl.BlockSpec((1, TOK, DH), lambda h, b, s: (c, 0, h)),
                pl.BlockSpec((1, TOK, DH), lambda h, b, s: (b, 0, h)),
                pl.BlockSpec((1, 1, TOK, 128), lambda h, b, s: (b, h, 0, 0)),
            ],
            out_specs=pl.BlockSpec((1, TOK, DH), lambda h, b, s: (b, 0, h)),
            scratch_shapes=[pltpu.VMEM((2, 4, TOK, DH), bf16), pltpu.SemaphoreType.DMA((2,))],
        ),
        compiler_params=cparams(24),
    )(scal, *before, q, q_rec, *local)


def norm_kernel(j, count, s_ref, fast_ref, att_ref, gain_ref, *refs):
    powers, out_ref = refs[:count], refs[-1]
    block = s_ref[0] if j == 0 else 1 - s_ref[0]
    total = sum((p[block] for p in powers[1:]), powers[0][block])
    rs = lax.rsqrt(total * (1.0 / 4096.0) + NORM_EPS)
    col = jnp.transpose(rs)[:, :1]
    out_ref[...] = (fast_ref[j] * gain_ref[...] * col + att_ref[block]).astype(bf16)


def norm_add(j, scal, fast, att, gain, powers):
    whole = pl.BlockSpec(memory_space=pltpu.VMEM)
    return pl.pallas_call(
        functools.partial(norm_kernel, j, len(powers)),
        name="norm_add",
        out_shape=jax.ShapeDtypeStruct((TOK, 2 * DH), bf16),
        in_specs=[pl.BlockSpec(memory_space=pltpu.SMEM)] + [whole] * (3 + len(powers)),
        out_specs=whole,
        compiler_params=cparams(20),
    )(scal, fast, att, gain, *powers)


def finish_kernel(j, count, s_ref, *refs):
    core, chip = s_ref[0], s_ref[5]
    block = core if j == 0 else 1 - core
    q_ref, before, own, refs = refs[0], refs[1:5], refs[5:9], refs[9:]
    fast_ref, gain_ref = refs[:2]
    powers = refs[2 : 2 + count]
    out_ref = refs[-1]
    row = lax.broadcasted_iota(jnp.int32, (TOK, TOK), 0)
    col = lax.broadcasted_iota(jnp.int32, (TOK, TOK), 1)
    total = sum(p[0] for p in powers[1:]) + powers[0][0]
    rs = lax.rsqrt(total * (1.0 / 4096.0) + NORM_EPS)
    fast = fast_ref[0] * gain_ref[...] * jnp.transpose(rs)[:, :1]

    def put(attended):
        out_ref[...] = (fast + attended).astype(bf16).reshape(out_ref.shape)

    kb, k2, vb, v2 = own
    k0, ka, v0, va = before
    first = block == 0
    keys = (k0[0], jnp.where(first, ka[0], kb[0]), k2[0])
    values = (v0[0], jnp.where(first, va[0], vb[0]), v2[0])
    scores = [dot(q_ref[0], k, NT) for k in keys]
    low = jnp.where(chip == 0, TOK, row)
    scores[1] = jnp.where(col >= jnp.where((chip == 0) & first, TOK, 0), scores[1], MASKED)
    scores[0] = jnp.where(col > low, scores[0], MASKED)
    scores[2] = jnp.where(col <= row, scores[2], MASKED)
    peak = jnp.max(jnp.maximum(jnp.maximum(scores[0], scores[1]), scores[2]), axis=-1, keepdims=True)
    weights = [jnp.exp2((s - peak) * (SCALE * LOG2E)) for s in scores]
    inv = 1.0 / jnp.sum(weights[0] + weights[1] + weights[2], axis=-1, keepdims=True)
    put(sum(dot((w * inv).astype(bf16), v, NN) for w, v in zip(weights, values)))


def chosen(s):
    return jnp.where(s[5] == 0, 2, jnp.where(s[4] == 1, 1, 0))


def finish(c, j, scal, q, q_rec, own, before, fast, powers, gain, layer=None):
    def block(s):
        return s[0] if j == 0 else 1 - s[0]

    def spec(at, holds=lambda s: True):
        return pl.BlockSpec(
            (1, TOK, DH),
            lambda h, s: (jnp.where(holds(s), at(s), 0), 0, jnp.where(holds(s), h, 0)),
        )

    def always(at):
        return pl.BlockSpec((1, TOK, DH), lambda h, s: (at(s), 0, h))

    sources = len(before)
    q_spec = own_spec(c) if j == 0 else rec_spec(c)
    specs = [q_spec]
    operands = [q if j == 0 else q_rec]
    for i, array in enumerate(before):
        holds = (lambda s, i=i: chosen(s) == i) if sources > 1 else (lambda s: True)
        specs += [
            spec(block, holds), spec(lambda s: 1, holds),
            spec(lambda s: 2 + block(s), holds), spec(lambda s: 3, holds),
        ]
        operands += [array] * 4
    if c == 0:
        specs += [
            always(lambda s: 0), always(block), always(lambda s: 2), always(lambda s: 2 + block(s))
        ]
        operands += [own] * 4
    else:
        specs += [
            always(block), pl.BlockSpec((1, 1, TOK, 128), lambda h, s: (block(s), h, 0, 0))
        ]
        operands += list(own)
    specs += [
        pl.BlockSpec((1, TOK, DH), lambda h, s: (j, 0, h)),
        pl.BlockSpec((1, DH), lambda h, s: (0, h)),
    ]
    operands += [fast, gain]
    specs += [pl.BlockSpec((1, 8, TOK), lambda h, s: (block(s), 0, 0))] * len(powers)
    operands += powers
    aliases = {}
    if layer is not None:
        aliases = {len(operands) + 1: 0}
        specs.append(ANY)
        operands.append(layer)
    if j == 0:
        shape = (2, TOK, 4 * DH)
        out_spec = pl.BlockSpec((1, TOK, DH), lambda h, s: (c, 0, s[0] * 2 + h))
    else:
        shape = (TOK, 2 * DH)
        out_spec = pl.BlockSpec((TOK, DH), lambda h, s: (0, h))
    return pl.pallas_call(
        functools.partial(finish_kernel, j, len(powers)),
        name="attend_finish",
        out_shape=jax.ShapeDtypeStruct(shape, bf16),
        grid_spec=pltpu.PrefetchScalarGridSpec(
            num_scalar_prefetch=1, grid=(2,), in_specs=specs, out_specs=out_spec
        ),
        input_output_aliases=aliases,
        compiler_params=cparams(24),
    )(scal, *operands)


def gather_direct(both):
    out = []
    for head, (first, last) in enumerate((("z", "x"), ("x", "z"))):
        v = both[head]
        v = jnp.concatenate([v] + [shift(v, first, -k) for k in range(1, 4)], axis=0)
        out.append([v] + [shift(v, last, -k) for k in range(1, 4)])
    return out[0] + out[1]


def gather_rings(both):
    axes = (("z", "x"), ("x", "z"))
    now = [both[h] for h in range(2)]
    held = [[n] for n in now]
    for _ in range(3):
        for h in range(2):
            now[h] = shift(now[h], axes[h][0], -1)
            held[h].append(now[h])
    now = [jnp.concatenate(held[h], axis=0) for h in range(2)]
    out = [[n] for n in now]
    for _ in range(3):
        for h in range(2):
            now[h] = shift(now[h], axes[h][1], -1)
            out[h].append(now[h])
    return out[0] + out[1]


def scatter_rings(slabs):
    axes = (("x", "z"), ("z", "x"))
    now = [slabs[3], slabs[7]]
    for k in (2, 1, 0):
        for h in range(2):
            got = shift(now[h], axes[h][0], -1)
            total = got.astype(f32) + slabs[h * 4 + k].astype(f32)
            now[h] = total.astype(bf16) if k else total
    parts = now
    now = [p[6:8].astype(bf16) for p in parts]
    for k in (2, 1, 0):
        for h in range(2):
            got = shift(now[h], axes[h][1], -1)
            now[h] = (got.astype(f32) + parts[h][2 * k : 2 * k + 2]).astype(bf16)
    return jnp.stack(now)


CORES = [(0, 1), (1, 0), (2, 3), (3, 2)]
HALVES = [(0, 2), (2, 0), (1, 3), (3, 1)]
ACROSS = [(0, 3), (3, 0), (1, 2), (2, 1)]


def with_parts(power, pairs):
    return [power] + [lax.ppermute(power, ("heads", "core"), p) for p in pairs]


def on_device(queries, key_rows, value_rows, step_rates, w_gate, w_up, w_down, out_gain):
    core = lax.axis_index("core")
    yh, z, x = lax.axis_index("yh"), lax.axis_index("z"), lax.axis_index("x")
    chip = (yh * 4 + z) * 4 + x
    turn = ((z == 0) & (x == 0)).astype(jnp.int32)
    scal = jnp.stack([core, yh, z, x, turn, chip]).astype(jnp.int32)

    masters = jnp.stack([w_gate, w_up, w_down], axis=1)
    mine = lax.dynamic_slice_in_dim(masters, core * 2, 2, 0)
    theirs = lax.dynamic_slice_in_dim(masters, (1 - core) * 2, 2, 0)
    got = shift(theirs, "core", 1)
    m16 = jnp.where(
        core == 0,
        jnp.concatenate([mine, got], axis=2),
        jnp.concatenate([got, mine], axis=2),
    )
    m16_other = shift(m16, "yh", 1)
    m16_other, key_rows, value_rows, queries, step_rates = lax.optimization_barrier(
        (m16_other, key_rows, value_rows, queries, step_rates)
    )
    both = jnp.stack([m16, m16_other], axis=1)
    pieces = gather_direct(both.astype(bf16))

    def split_in(a):
        keep = lax.dynamic_slice_in_dim(a, core * 1024, 1024, 2)
        give = lax.dynamic_slice_in_dim(a, (1 - core) * 1024, 1024, 2)
        return keep, shift(give, "core", 1)

    k_own, k_rec = split_in(key_rows)
    v_own, v_rec = split_in(value_rows)
    q_rec = split_in(queries)[1]
    rates = step_rates[:, 0, :]
    r_own = lax.dynamic_slice_in_dim(rates, core * 2, 2, 0)
    r_rec = shift(lax.dynamic_slice_in_dim(rates, (1 - core) * 2, 2, 0), "core", 1)
    rates = jnp.stack([r_own, r_rec], axis=1)[..., None]

    chips = ("yh", "z", "x")
    row = [(i, (i + 1) % 32) for i in range(32)]
    pair = [
        jnp.where(
            core == 0,
            jnp.stack([k_own[c], k_rec[c], v_own[c], v_rec[c]]),
            jnp.stack([k_rec[c], k_own[c], v_rec[c], v_own[c]]),
        )
        for c in range(2)
    ]
    pair[0], pair[1], *pieces = lax.optimization_barrier((pair[0], pair[1], *pieces))
    halo0 = lax.ppermute(pair[0], chips, row)
    halo1 = lax.ppermute(pair[1], chips, [p for p in row if p[0] % 16 != 15])

    slabs = compute_grads(scal, pieces, key_rows, value_rows, k_rec, v_rec, rates)
    fast0, pow0 = fast_apply(0, scal, pieces, queries, q_rec)
    half_sums = scatter_rings(slabs)
    pow0 = sum(with_parts(pow0, (CORES,)))
    half_sums, pow0 = lax.optimization_barrier((half_sums, pow0))
    other_sums = shift(half_sums, "yh", 1)
    powers0 = with_parts(pow0, (HALVES,))
    grad_both = half_sums.astype(f32) + other_sums[:, ::-1].astype(f32)
    grad_both, pair1, *powers0 = lax.optimization_barrier((grad_both, pair[1], *powers0))
    new_both = both - grad_both
    pieces2 = gather_rings(new_both.astype(bf16))
    turned1 = lax.ppermute(pair1, chips, [(15, 16)])
    own_rows = lax.dynamic_slice(new_both, (0, 0, 0, core * 8, 0), (2, 1, 3, 8, 512))[:, 0]
    their_rows = lax.dynamic_slice(new_both, (0, 0, 0, (1 - core) * 8, 0), (2, 1, 3, 8, 512))
    their_rows = shift(their_rows[:, 0], "core", 1)
    new_all = jnp.where(
        core == 0,
        jnp.concatenate([own_rows, their_rows], axis=0),
        jnp.concatenate([their_rows, own_rows], axis=0),
    )

    gain = lax.dynamic_slice_in_dim(out_gain, core * 1024, 1024, 0)[None]

    def complete(c, own, before, fast, powers, layer):
        args = (scal, queries, q_rec, own, before, fast, powers, gain)
        out_rec = finish(c, 1, *args)
        arrived = shift(out_rec, "core", 1)
        layer = finish(c, 0, *args, layer)
        return lax.dynamic_update_slice(layer, arrived[None], (c, 0, (1 - core) * 1024))

    local1 = attend_local(1, scal, queries, q_rec, pair[1])
    layer_out = complete(0, pair[0], [halo0], fast0, powers0, None)
    fast1, pow1 = fast_apply(1, scal, pieces2, queries, q_rec)
    powers1 = with_parts(pow1, (CORES, HALVES, ACROSS))
    att1 = attend_tail(1, scal, queries, q_rec, local1, [halo1, turned1, halo0])
    out_rec = norm_add(1, scal, fast1, att1, gain, powers1)
    arrived = shift(out_rec, "core", 1)
    out_own = norm_add(0, scal, fast1, att1, gain, powers1)
    layer_out = lax.dynamic_update_slice(layer_out, out_own[None], (1, 0, core * 1024))
    layer_out = lax.dynamic_update_slice(layer_out, arrived[None], (1, 0, (1 - core) * 1024))
    return layer_out, new_all[:, 0], new_all[:, 1], new_all[:, 2]


def solution(mesh):
    fine = Mesh(mesh.devices.reshape(2, 2, 4, 4, 2), ("heads",) + SEQ)
    rows = P(None, SEQ, "heads")
    weight = P("heads", SEQ, None)
    return jax.shard_map(
        on_device,
        mesh=fine,
        in_specs=(rows, rows, rows, P("heads", None, SEQ), weight, weight, weight, P("heads")),
        out_specs=(rows, weight, weight, weight),
        check_vma=False,
    )
```
